128 devices in a mesh: blk: 16 (over y, z), rep: 8 (over x, core).
Axes of the slice: x: 4, y: 4, z: 4, core: 2. Of those that a mesh axis runs over, the one named last changes fastest.
Arguments:
- dense: bfloat16 [131072, 1024], P(('blk', 'rep')), may hold values from -6 to 6
- labels: int32 [131072], P(('blk', 'rep')), may hold values 0 or 1
- tile_values: bfloat16 [16384, 64, 128], P(('blk', 'rep')), may hold values from -1.1953125 to 1.1953125
- tile_block: int32 [16384, 64], P(('blk', 'rep')), may hold values from 0 to 1023
- tile_example: int32 [16384, 64], P(('blk', 'rep')), may hold values from 0 to 1023
- tile_count: int32 [16384], P(('blk', 'rep')), may hold values from 16 to 64, as said below
- z_state: float32 [131072, 128], P(('blk', 'rep')), may hold values from -6 to 6
- n_state: float32 [131072, 128], P(('blk', 'rep')), may hold values from 0.01 to 4
- w_one: bfloat16 [1024, 512], replicated, may hold values from -0.1875 to 0.1875
- b_one: float32 [512], replicated, may hold values from -3 to 3
- w_two: bfloat16 [512, 256], replicated, may hold values from -0.25 to 0.25
- b_two: float32 [256], replicated, may hold values from -3 to 3
- head: bfloat16 [256], replicated, may hold values from -0.375 to 0.375
Outputs:
- probability: float32 [131072], P(('blk', 'rep'))
- z_new: float32 [131072, 128], P(('blk', 'rep'))
- n_new: float32 [131072, 128], P(('blk', 'rep'))
- grad_w_one: float32 [1024, 512], replicated
- grad_b_one: float32 [512], replicated
- grad_w_two: float32 [512, 256], replicated
- grad_b_two: float32 [256], replicated
- grad_head: float32 [256], replicated
The draws below stay inside these ranges and needn't reach their ends.
Inputs may be any that keep to these rules, and one draw needn't show every extreme that they name: `tile_count`: slots at or beyond a list's count are padding; in every draw some owners receive 64 live slots from every device.
All inputs are finite; a program needn't handle non-finite values. No bound on the sum of `labels` on one device may be relied on, other than what follows from the above.
Results may differ from the reference program's by a relative error of at most 0.013.
Values may be sent and summed in bfloat16 or wider, within the bound.
A program may use at most 64 MiB of HBM per device.

```python
import math
import jax
import jax.numpy as jnp
from jax import lax

W = 128
DIN = 1024
H1 = 512
H2 = 256
B_DEV = 1024
BLK_DEV = 1024
CAP = 64
OWNERS = 128
EXAMPLES = 131072
BLOCKS = 131072


def draw_tile_count(key, part):
    hot_key, base_key = jax.random.split(jax.random.fold_in(key, 11))
    order = jax.random.permutation(hot_key, OWNERS)
    hot = order < max(OWNERS // 16, 1)
    base = jax.random.randint(base_key, (OWNERS, OWNERS), CAP // 4, CAP // 2 + 1)
    counts = jnp.where(hot[None, :], CAP, base)
    return counts.reshape(OWNERS * OWNERS).astype(jnp.int32)


def draw_tile_block(key, part):
    first_key, second_key, table_key = jax.random.split(jax.random.fold_in(key, 23), 3)
    first = jax.random.randint(first_key, (OWNERS * OWNERS, CAP), 0, BLK_DEV)
    second = jax.random.randint(second_key, (OWNERS * OWNERS, CAP), 0, BLK_DEV)
    skewed = jnp.minimum(first * (second + 1) // BLK_DEV, BLK_DEV - 1)
    table = jax.random.permutation(table_key, BLK_DEV)
    return jnp.take(table, skewed).astype(jnp.int32)


def draw_tile_example(key, part):
    example_key = jax.random.fold_in(key, 37)
    return jax.random.randint(example_key, (OWNERS * OWNERS, CAP), 0, B_DEV).astype(jnp.int32)


def touch_ends(result, key, smallest, largest):
    longest = result.shape.index(max(result.shape))
    spots = []
    for shift in (0, 1):
        where = [jax.random.randint(jax.random.fold_in(key, axis), (), 0, length) for axis, length in enumerate(result.shape)]
        where[longest] = (where[longest] + shift) % result.shape[longest]
        spots.append(tuple(where))
    return result.at[spots[0]].set(smallest).at[spots[1]].set(largest)


def steps_of(key, shape, cuts, least, largest):
    gain, own = 1.0, jax.random.fold_in(key, 6)
    for axis_at, shards_of in cuts:
        heights = jnp.exp(jax.random.uniform(jax.random.fold_in(own, axis_at), (shards_of,), jnp.float32, least / len(cuts), largest / len(cuts)))
        gain = gain * jnp.repeat(heights, shape[axis_at] // shards_of).reshape([-1 if axis == axis_at else 1 for axis in range(len(shape))])
    return gain


def gaussian(rng, dims, deviation, limit, pieces=(), kind=jnp.bfloat16):
    level = steps_of(rng, dims, pieces, -0.22, 0.18) if pieces else 1.0
    entries = jax.random.normal(rng, dims, jnp.float32) * deviation * level
    return jnp.minimum(jnp.maximum(entries, -limit), limit).astype(kind)


def setup_inputs(seed: int = 0) -> dict:
    splits = jax.random.split(jax.random.key(seed), 14)
    dense = gaussian(splits[0], (EXAMPLES, DIN), 1.0, 6.0, ((0, 128),))
    labels = touch_ends((jax.random.randint(splits[1], (EXAMPLES,), 0, 4) < 1).astype(jnp.int32), jax.random.fold_in(splits[1], 1), 0, 1)
    tile_values = gaussian(splits[2], (OWNERS * OWNERS, CAP, W), 0.2, 1.1953125, ((0, 128),))
    tile_block = draw_tile_block(jax.random.fold_in(splits[13], 71), 0)
    tile_example = draw_tile_example(jax.random.fold_in(splits[13], 71), 0)
    tile_count = draw_tile_count(jax.random.fold_in(splits[13], 71), 0)
    z_state = gaussian(splits[6], (BLOCKS, W), 1.0, 6.0, ((0, 128),), jnp.float32)
    n_state = jnp.clip(jnp.exp(math.log(4.0) - 5.9914646 * jax.random.uniform(splits[7], (BLOCKS, W), jnp.float32) ** steps_of(splits[7], (BLOCKS, W), ((0, 128),), -0.2, 0.2)), 0.01, 4.0)
    w_one = gaussian(splits[8], (DIN, H1), DIN ** -0.5, 0.1875)
    b_one = gaussian(splits[9], (H1,), 0.5, 3.0, (), jnp.float32)
    w_two = gaussian(splits[10], (H1, H2), H1 ** -0.5, 0.25)
    b_two = gaussian(splits[11], (H2,), 0.5, 3.0, (), jnp.float32)
    head = gaussian(splits[12], (H2,), H2 ** -0.5, 0.375)
    return {"dense": dense, "labels": labels, "tile_values": tile_values, "tile_block": tile_block, "tile_example": tile_example, "tile_count": tile_count, "z_state": z_state, "n_state": n_state, "w_one": w_one, "b_one": b_one, "w_two": w_two, "b_two": b_two, "head": head}


alpha_rate = 0.5
beta_shift = 1.0
lasso_term = 0.5
ridge_term = 0.1

def wide_weight(z_state, n_state):
    shrunk = z_state - jnp.sign(z_state) * lasso_term
    denominator = (beta_shift + jnp.sqrt(n_state)) / alpha_rate + ridge_term
    return jnp.where(jnp.abs(z_state) > lasso_term, -shrunk / denominator, jnp.zeros_like(z_state))

def silu_slope(pre):
    gate = jax.nn.sigmoid(pre)
    return gate * (1.0 + pre * (1.0 - gate))

def live_values(values, counts):
    slots = jnp.arange(values.shape[1], dtype=jnp.int32)
    live = slots[None, :] < counts[:, None]
    return jnp.where(live[:, :, None], values, jnp.zeros_like(values))

def reference(dense, labels, tile_values, tile_block, tile_example, tile_count, z_state, n_state, w_one, b_one, w_two, b_two, head):
    weight = wide_weight(z_state, n_state)
    owner_base = (jnp.arange(OWNERS, dtype=jnp.int32) * BLK_DEV)[:, None]
    sources = jnp.arange(OWNERS, dtype=jnp.int32)

    def source_rows(src):
        start = (src * OWNERS).astype(jnp.int32)
        values = live_values(lax.dynamic_slice_in_dim(tile_values, start, OWNERS, 0), lax.dynamic_slice_in_dim(tile_count, start, OWNERS, 0))
        blocks = (lax.dynamic_slice_in_dim(tile_block, start, OWNERS, 0) + owner_base).astype(jnp.int32)
        examples = lax.dynamic_slice_in_dim(tile_example, start, OWNERS, 0).astype(jnp.int32)
        return (values, blocks, examples)

    def source_logits(src):
        values, blocks, examples = source_rows(src)
        picked = jnp.take(weight, blocks.reshape(-1), axis=0)
        tile_logit = lax.optimization_barrier(jnp.sum(values.reshape(-1, W).astype(jnp.float32) * picked, axis=1))
        return jax.ops.segment_sum(tile_logit, examples.reshape(-1), num_segments=B_DEV)
    wide = lax.map(source_logits, sources).reshape(EXAMPLES)
    pre_one = jnp.dot(dense, w_one, preferred_element_type=jnp.float32) + b_one
    hid_one = jax.nn.silu(pre_one).astype(jnp.bfloat16)
    pre_two = jnp.dot(hid_one, w_two, preferred_element_type=jnp.float32) + b_two
    hid_two = jax.nn.silu(pre_two).astype(jnp.bfloat16)
    deep = jnp.dot(hid_two, head, preferred_element_type=jnp.float32)
    probability = jax.nn.sigmoid(wide + deep)
    residual = probability - labels.astype(jnp.float32)

    def add_source(total, src):
        values, blocks, examples = source_rows(src)
        own = lax.dynamic_slice_in_dim(residual, (src * B_DEV).astype(jnp.int32), B_DEV, 0)
        tile_residual = jnp.take(own, examples.reshape(-1))
        contrib = values.reshape(-1, W).astype(jnp.float32) * tile_residual[:, None]
        return (total.at[blocks.reshape(-1)].add(contrib), None)
    grad_block, _ = lax.scan(add_source, jnp.zeros((BLOCKS, W), jnp.float32), sources)
    n_new = n_state + grad_block * grad_block
    sigma = (jnp.sqrt(n_new) - jnp.sqrt(n_state)) / alpha_rate
    z_new = z_state + grad_block - sigma * weight
    dlogit = residual.astype(jnp.bfloat16)
    grad_head = jnp.dot(dlogit, hid_two, preferred_element_type=jnp.float32)
    d_two = (dlogit.astype(jnp.float32)[:, None] * head.astype(jnp.float32)[None, :] * silu_slope(pre_two)).astype(jnp.bfloat16)
    grad_w_two = lax.dot_general(hid_one, d_two, (((0,), (0,)), ((), ())), preferred_element_type=jnp.float32)
    grad_b_two = lax.optimization_barrier(jnp.sum(d_two.astype(jnp.float32), axis=0))
    back_one = lax.dot_general(d_two, w_two, (((1,), (1,)), ((), ())), preferred_element_type=jnp.float32)
    d_one = (back_one * silu_slope(pre_one)).astype(jnp.bfloat16)
    grad_w_one = lax.dot_general(dense, d_one, (((0,), (0,)), ((), ())), preferred_element_type=jnp.float32)
    grad_b_one = lax.optimization_barrier(jnp.sum(d_one.astype(jnp.float32), axis=0))
    return (probability, z_new, n_new, grad_w_one, grad_b_one, grad_w_two, grad_b_two, grad_head)
```

```python
import functools

import jax
import jax.numpy as jnp
from jax import lax
from jax.experimental import pallas as pl
from jax.experimental.pallas import tpu as pltpu
from jax.sharding import PartitionSpec as P

MESH = pl.DeviceIdType.MESH
F32 = jnp.float32
BF16 = jnp.bfloat16
NT = (((1,), (1,)), ((), ()))


def mm(a, b):
    return jnp.dot(a, b, preferred_element_type=F32)


def mm_nt(a, b):
    return lax.dot_general(a, b, NT, preferred_element_type=F32)


def step_kernel(
    B, R,
    dense_h, labels_h, values_h, index_h, example_h, z_h, n_h,
    w_one_h, b_one_h, w_two_h, b_two_h, head_h,
    prob_o, z_o, n_o, g_one_o, g_two_o, small_o,
    dense_v, labels_v, example_v, z_v, n_v, w_one_v, b_one_v, w_two_v, b_two_v, head_v,
    got_values, got_index, weight_v, weight_pair,
    hid_two_v, dense_t, hid_one_t, scale_one, scale_two, deep_v, low_hot,
    logit_send, logit_got, spread, picked, res_send, res_got,
    block_hot, total, z_out_v, n_out_v,
    d_one_v, d_two_v,
    part_one, part_two, own_one, pair_one, pair_two,
    sum_one, sum_two, got_one, got_two, fin_one, fin_two, full_one, full_two,
    small_v, small_rep, small_sum, small_blk,
    load_sem, own_sem, index_sem, value_sem, logit_sem, res_sem,
    pair_sem, rs_sem, ag_sem, fw_sem, small_sem,
    send_sem, out_sem,
):
    ND = B * R
    NC = ND // 2
    X = R // 2
    E, DIN = dense_v.shape
    H1 = w_one_v.shape[1]
    H2 = w_two_v.shape[1]
    CAP, W = got_values.shape[1], got_values.shape[2]
    BD = z_v.shape[0]
    NH = E // 128
    NP = ND // 2
    c1 = DIN * H1 // (128 * ND)
    c2 = H1 * H2 // (128 * ND)
    j1 = H1 // 128
    j2 = H2 // 128
    blk = lax.axis_index("blk")
    rep = lax.axis_index("rep")
    core = rep % 2
    other = 1 - core
    me = blk * R + rep
    chip = blk * X + rep // 2

    loads = [
        (z_h, z_v), (n_h, n_v), (dense_h, dense_v), (w_one_h, w_one_v), (b_one_h, b_one_v),
        (w_two_h, w_two_v), (b_two_h, b_two_v), (head_h, head_v), (example_h, example_v), (labels_h, labels_v),
    ]
    copies = [pltpu.make_async_copy(s, d, load_sem.at[i]) for i, (s, d) in enumerate(loads)]
    for copy in copies:
        copy.start()
    own_value = pltpu.make_async_copy(values_h.at[me], got_values.at[me], own_sem.at[0])
    own_value.start()
    own_index = pltpu.make_async_copy(index_h.at[me], got_index.at[me], own_sem.at[1])
    own_index.start()

    def send(src, dst, sem_at, recv, where):
        pltpu.make_async_remote_copy(
            src_ref=src, dst_ref=dst, send_sem=send_sem.at[sem_at], recv_sem=recv,
            device_id=where, device_id_type=MESH,
        ).start()

    def wait_for(ref, sem):
        pltpu.make_async_copy(ref, ref, sem).wait()

    barrier = pltpu.get_barrier_semaphore()

    @pl.loop(1, ND)
    def _(k):
        there = lax.rem(me + k, ND)
        pl.semaphore_signal(barrier, inc=1, device_id=(there // R, lax.rem(there, R)), device_id_type=MESH)

    copies[0].wait()
    copies[1].wait()
    z = z_v[...]
    shrunk = z - jnp.where(z > 0, 0.5, -0.5)
    weight = jnp.where(jnp.abs(z) > 0.5, -shrunk / ((1.0 + jnp.sqrt(n_v[...])) / 0.5 + 0.1), 0.0)
    weight_v[...] = weight
    high = weight.astype(BF16)
    weight_pair[:, :W] = high
    weight_pair[:, W:] = (weight - high.astype(F32)).astype(BF16)

    pl.semaphore_wait(barrier, ND - 1)

    @pl.loop(1, ND)
    def _(k):
        blk_to = lax.rem(blk + k // R, B)
        rep_to = lax.rem(rep + lax.rem(k, R), R)
        to = blk_to * R + rep_to
        send(index_h.at[to], got_index.at[me], 0, index_sem, (blk_to, rep_to))

    @pl.loop(1, ND)
    def _(k):
        blk_to = lax.rem(blk + k // R, B)
        rep_to = lax.rem(rep + lax.rem(k, R), R)
        to = blk_to * R + rep_to
        send(values_h.at[to], got_values.at[me], 1, value_sem.at[k // R], (blk_to, rep_to))

    for copy in copies[2:]:
        copy.wait()
    rows = 256
    head_rows = jnp.broadcast_to(head_v[...], (8, H2))

    @pl.loop(0, E // rows)
    def _(i):
        at = pl.multiple_of(i * rows, rows)
        dense = dense_v[pl.ds(at, rows), :]
        pre_one = mm(dense, w_one_v[...]) + b_one_v[...]
        gate_one = jax.nn.sigmoid(pre_one)
        hid_one = (pre_one * gate_one).astype(BF16)
        pre_two = mm(hid_one, w_two_v[...]) + b_two_v[...]
        gate_two = jax.nn.sigmoid(pre_two)
        hid_two = (pre_two * gate_two).astype(BF16)
        hid_two_v[pl.ds(at, rows), :] = hid_two
        two = head_v[...].astype(F32) * (gate_two * (1.0 + pre_two * (1.0 - gate_two)))
        scale_two[pl.ds(at, rows), :] = two
        back = mm_nt(two.astype(BF16), w_two_v[...])
        scale_one[pl.ds(at, rows), :] = back * (gate_one * (1.0 + pre_one * (1.0 - gate_one)))
        deep = mm_nt(head_rows, hid_two)
        for q in range(rows // 128):
            deep_v[pl.ds(i * (rows // 128) + q, 1), :] = deep[0:1, q * 128:(q + 1) * 128]
        dense_t[:, pl.ds(at, rows)] = dense.T
        hid_one_t[:, pl.ds(at, rows)] = hid_one.T

    @pl.loop(0, NP)
    def _(p):
        at = pl.multiple_of(p * 128, 128)
        low = lax.bitwise_and(example_v[p], 127)
        low_hot[:, pl.ds(at, 128)] = (lax.broadcasted_iota(jnp.int32, (128, 128), 0) == low).astype(F32).astype(BF16)

    own_value.wait()
    own_index.wait()
    wait_for(got_index.at[pl.ds(0, ND - 1)], index_sem)
    first_half = lax.broadcasted_iota(jnp.int32, (1, 128), 1) < CAP

    def merged(ref, p):
        return jnp.where(first_half, ref[2 * p], ref[2 * p + 1])

    def flipped(row):
        return pltpu.roll(jnp.broadcast_to(row, (8, 128)), CAP, axis=1)[0:1]

    def logits_of(j):
        blk_from = lax.rem(blk + B - j, B)
        base = blk_from * R
        for h in range(R // 4):
            four = got_values[pl.ds(base + 4 * h, 4)].reshape(4 * CAP, W)
            score = mm_nt(weight_pair[...], jnp.concatenate([four, four], axis=1))
            p = blk_from * X + 2 * h
            for q in range(2):
                name = merged(got_index, p + q)
                hit = lax.broadcasted_iota(jnp.int32, (BD, 128), 0) == name
                row = jnp.sum(jnp.where(hit, score[:, q * 128:(q + 1) * 128], 0.0), axis=0, keepdims=True)
                logit_send[0, p + q] = row
                logit_send[1, p + q] = flipped(row)

        def back(r, _):
            rep_to = lax.rem(rep + r, R)
            to = base + rep_to
            send(logit_send.at[lax.rem(rep_to + core, 2), to // 2], logit_got.at[me], 2, logit_sem, (blk_from, rep_to))
            return 0

        return back

    wait_for(got_values.at[pl.ds(0, R - 1)], value_sem.at[0])
    lax.fori_loop(1, R, logits_of(0), 0)
    logit_got[me] = logit_send[0, me // 2]

    @pl.loop(1, B)
    def _(j):
        wait_for(got_values.at[pl.ds(0, R)], value_sem.at[j])
        lax.fori_loop(0, R, logits_of(j), 0)

    wait_for(logit_got.at[pl.ds(0, ND - 1)], logit_sem)
    eight = lax.broadcasted_iota(jnp.int32, (NH, 128), 0)

    @pl.loop(0, NP)
    def _(p):
        at = pl.multiple_of(p * 128, 128)
        mine = eight == lax.shift_right_logical(example_v[p], 7)
        term = jnp.where(mine, merged(logit_got, p), 0.0)
        top = term.astype(BF16).astype(F32)
        spread[:, pl.ds(at, 128)] = jnp.concatenate([top, term - top], axis=0).astype(BF16)

    wide = mm_nt(spread[...], low_hot[...])
    prob = jax.nn.sigmoid(wide[:NH] + wide[NH:] + deep_v[...])
    prob_o[...] = prob
    residual = prob - labels_v[...].astype(F32)
    dlogit = residual.astype(BF16).astype(F32)

    table = jnp.concatenate([dlogit, jnp.zeros_like(dlogit)], axis=0).astype(BF16)
    picked[...] = mm(table, low_hot[...])

    @pl.loop(0, NP)
    def _(p):
        at = pl.multiple_of(p * 128, 128)
        mine = eight == lax.shift_right_logical(example_v[p], 7)
        row = jnp.sum(jnp.where(mine, picked[0:NH, pl.ds(at, 128)], 0.0), axis=0, keepdims=True)
        res_send[0, p] = row
        res_send[1, p] = flipped(row)

    @pl.loop(1, ND)
    def _(k):
        blk_to = lax.rem(blk + k // R, B)
        rep_to = lax.rem(rep + lax.rem(k, R), R)
        to = blk_to * R + rep_to
        send(res_send.at[lax.rem(rep_to + core, 2), to // 2], res_got.at[me], 3, res_sem, (blk_to, rep_to))

    res_got[me] = res_send[0, me // 2]

    upright = jnp.concatenate([dlogit, jnp.zeros((128 - NH, 128), F32)], axis=0).T
    grad_head = jnp.zeros((8, H2), F32)
    for q in range(NH):
        span = slice(q * 128, (q + 1) * 128)
        column = upright[:, q:q + 1]
        d_two_v[span, :] = (scale_two[span, :] * column).astype(BF16)
        d_one_v[span, :] = (scale_one[span, :] * column).astype(BF16)
        grad_head += mm(jnp.broadcast_to(dlogit[q:q + 1, :], (8, 128)).astype(BF16), hid_two_v[span, :])
    ones = jnp.ones((8, E), BF16)
    bias_one = mm(ones, d_one_v[...])
    bias_two = mm(ones, d_two_v[...])
    small_v[...] = jnp.zeros_like(small_v)
    for q in range(j1):
        small_v[q:q + 1, :] = bias_one[0:1, q * 128:(q + 1) * 128]
    for q in range(j2):
        small_v[j1 + q:j1 + q + 1, :] = bias_two[0:1, q * 128:(q + 1) * 128]
        small_v[j1 + j2 + q:j1 + j2 + q + 1, :] = grad_head[0:1, q * 128:(q + 1) * 128]

    half_one, half_two = DIN // 2, H1 // 2
    theirs_one = pl.multiple_of(other * half_one, half_one)
    theirs_two = pl.multiple_of(other * half_two, half_two)
    mine_one = pl.multiple_of(core * half_one, half_one)
    mine_two = pl.multiple_of(core * half_two, half_two)
    rep_other = rep + 1 - 2 * core
    part_one[...] = mm(dense_t[pl.ds(theirs_one, half_one), :], d_one_v[...]).astype(BF16)
    send(part_one, pair_one, 4, pair_sem.at[0], (blk, rep_other))
    part_two[...] = mm(hid_one_t[pl.ds(theirs_two, half_two), :], d_two_v[...])
    send(part_two, pair_two, 5, pair_sem.at[1], (blk, rep_other))

    @pl.loop(1, R)
    def _(r):
        send(small_v, small_rep.at[rep], 6, small_sem.at[0], (blk, lax.rem(rep + r, R)))

    small_rep[rep] = small_v[...]

    own_one[...] = mm(dense_t[pl.ds(mine_one, half_one), :], d_one_v[...])
    own_two = mm(hid_one_t[pl.ds(mine_two, half_two), :], d_two_v[...])
    wait_for(pair_one, pair_sem.at[0])
    sum_one[...] = (own_one[...] + pair_one[...].astype(F32)).astype(BF16)
    wait_for(pair_two, pair_sem.at[1])
    sum_two[...] = own_two + pair_two[...]

    def piece_one(ref, q, base):
        row = pl.multiple_of(base + (q // j1) * c1, c1)
        return ref.at[pl.ds(row, c1), pl.ds(pl.multiple_of(lax.rem(q, j1) * 128, 128), 128)]

    def piece_two(ref, q, base):
        row = pl.multiple_of(base + (q // j2) * c2, c2)
        return ref.at[pl.ds(row, c2), pl.ds(pl.multiple_of(lax.rem(q, j2) * 128, 128), 128)]

    @pl.loop(1, NC)
    def _(k):
        blk_to = lax.rem(blk + k // X, B)
        x_to = lax.rem(rep // 2 + lax.rem(k, X), X)
        q = blk_to * X + x_to
        where = (blk_to, x_to * 2 + core)
        send(piece_one(sum_one, q, 0), got_one.at[chip], 7, rs_sem.at[0], where)
        send(piece_two(sum_two, q, 0), got_two.at[chip], 8, rs_sem.at[1], where)

    own_a = pltpu.make_async_copy(piece_one(sum_one, chip, 0), got_one.at[chip], own_sem.at[2])
    own_a.start()
    own_b = pltpu.make_async_copy(piece_two(sum_two, chip, 0), got_two.at[chip], own_sem.at[3])
    own_b.start()

    wait_for(res_got.at[pl.ds(0, ND - 1)], res_sem)
    total[...] = jnp.zeros_like(total)

    @pl.loop(0, B)
    def _(g):
        for h in range(X):
            p = g * X + h
            hit = lax.broadcasted_iota(jnp.int32, (BD, 128), 0) == merged(got_index, p)
            block_hot[:, h * 128:(h + 1) * 128] = jnp.where(hit, merged(res_got, p), 0.0).astype(BF16)
        values = got_values[pl.ds(g * R, R)].reshape(R * CAP, W)
        total[...] += mm(block_hot[...], values)

    wait_for(small_rep.at[pl.ds(0, R - 1)], small_sem.at[0])
    acc = small_rep[0]
    for r in range(1, R):
        acc = acc + small_rep[r]
    small_sum[...] = acc

    @pl.loop(1, B)
    def _(k):
        send(small_sum, small_blk.at[blk], 9, small_sem.at[1], (lax.rem(blk + k, B), rep))

    small_blk[blk] = acc
    own_a.wait()
    own_b.wait()
    wait_for(got_one.at[pl.ds(0, NC - 1)], rs_sem.at[0])
    wait_for(got_two.at[pl.ds(0, NC - 1)], rs_sem.at[1])
    fin_one[...] = lax.fori_loop(
        1, NC, lambda q, a: a + got_one[q].astype(F32), got_one[0].astype(F32)
    ).astype(BF16)
    fin_two[...] = lax.fori_loop(1, NC, lambda q, a: a + got_two[q], got_two[0])

    @pl.loop(1, NC)
    def _(k):
        blk_to = lax.rem(blk + k // X, B)
        where = (blk_to, lax.rem(rep // 2 + lax.rem(k, X), X) * 2 + core)
        send(fin_one, piece_one(full_one, chip, mine_one), 10, ag_sem.at[0, k // X], where)
        send(fin_two, piece_two(full_two, chip, mine_two), 11, ag_sem.at[1, k // X], where)

    own_c = pltpu.make_async_copy(fin_one, piece_one(full_one, chip, mine_one), own_sem.at[4])
    own_c.start()
    own_d = pltpu.make_async_copy(fin_two, piece_two(full_two, chip, mine_two), own_sem.at[5])
    own_d.start()

    grad = total[...]
    n_old = n_v[...]
    n_new = n_old + grad * grad
    n_out_v[...] = n_new
    z_out_v[...] = z_v[...] + grad - (jnp.sqrt(n_new) - jnp.sqrt(n_old)) / 0.5 * weight_v[...]
    out_z = pltpu.make_async_copy(z_out_v, z_o, out_sem.at[0])
    out_z.start()
    out_n = pltpu.make_async_copy(n_out_v, n_o, out_sem.at[1])
    out_n.start()

    own_c.wait()
    own_d.wait()
    rows_one, rows_two = X // j1 * c1, X // j2 * c2

    def stripe_one(j, base):
        at = pl.multiple_of(base + lax.rem(blk + B - j, B) * rows_one, rows_one)
        return full_one.at[pl.ds(at, rows_one), :]

    def stripe_two(j, base):
        at = pl.multiple_of(base + lax.rem(blk + B - j, B) * rows_two, rows_two)
        return full_two.at[pl.ds(at, rows_two), :]

    def forward(j):
        send(stripe_one(j, mine_one), stripe_one(j, mine_one), 12, fw_sem.at[0], (blk, rep_other))
        send(stripe_two(j, mine_two), stripe_two(j, mine_two), 13, fw_sem.at[1], (blk, rep_other))

    wait_for(got_one.at[pl.ds(0, X - 1)], ag_sem.at[0, 0])
    wait_for(got_two.at[pl.ds(0, X - 1)], ag_sem.at[1, 0])
    forward(0)

    @pl.loop(1, B)
    def _(j):
        wait_for(got_one.at[pl.ds(0, X)], ag_sem.at[0, j])
        wait_for(got_two.at[pl.ds(0, X)], ag_sem.at[1, j])
        forward(j)

    out_a = pltpu.make_async_copy(full_one.at[pl.ds(mine_one, half_one)], g_one_o.at[pl.ds(mine_one, half_one)], out_sem.at[2])
    out_a.start()
    out_b = pltpu.make_async_copy(full_two.at[pl.ds(mine_two, half_two)], g_two_o.at[pl.ds(mine_two, half_two)], out_sem.at[3])
    out_b.start()

    wait_for(small_blk.at[pl.ds(0, B - 1)], small_sem.at[1])
    acc = small_blk[0]
    for r in range(1, B):
        acc = acc + small_blk[r]
    small_o[...] = acc

    wait_for(full_one.at[pl.ds(0, half_one)], fw_sem.at[0])
    wait_for(full_two.at[pl.ds(0, half_two)], fw_sem.at[1])
    out_c = pltpu.make_async_copy(full_one.at[pl.ds(theirs_one, half_one)], g_one_o.at[pl.ds(theirs_one, half_one)], out_sem.at[4])
    out_c.start()
    out_d = pltpu.make_async_copy(full_two.at[pl.ds(theirs_two, half_two)], g_two_o.at[pl.ds(theirs_two, half_two)], out_sem.at[5])
    out_d.start()
    for copy in (out_z, out_n, out_a, out_b, out_c, out_d):
        copy.wait()

    wait_for(got_index.at[pl.ds(0, ND - 1)], send_sem.at[0])
    wait_for(got_values.at[pl.ds(0, ND - 1)], send_sem.at[1])
    wait_for(logit_got.at[pl.ds(0, ND - 1)], send_sem.at[2])
    wait_for(res_got.at[pl.ds(0, ND - 1)], send_sem.at[3])
    wait_for(part_one, send_sem.at[4])
    wait_for(part_two, send_sem.at[5])
    wait_for(small_rep.at[pl.ds(0, R - 1)], send_sem.at[6])
    wait_for(got_one.at[pl.ds(0, NC - 1)], send_sem.at[7])
    wait_for(got_two.at[pl.ds(0, NC - 1)], send_sem.at[8])
    wait_for(small_blk.at[pl.ds(0, B - 1)], send_sem.at[9])
    wait_for(got_one.at[pl.ds(0, NC - 1)], send_sem.at[10])
    wait_for(got_two.at[pl.ds(0, NC - 1)], send_sem.at[11])
    wait_for(full_one.at[pl.ds(0, half_one)], send_sem.at[12])
    wait_for(full_two.at[pl.ds(0, half_two)], send_sem.at[13])


def solution(mesh):
    B, R = mesh.shape["blk"], mesh.shape["rep"]
    ND = B * R
    NC = ND // 2

    def per_device(
        dense, labels, tile_values, tile_block, tile_example, tile_count, z_state, n_state,
        w_one, b_one, w_two, b_two, head,
    ):
        E, DIN = dense.shape
        _, CAP, W = tile_values.shape
        BD = z_state.shape[0]
        H1, H2 = w_two.shape
        NH = E // 128
        NP = ND // 2
        c1 = DIN * H1 // (128 * ND)
        c2 = H1 * H2 // (128 * ND)
        live = jnp.arange(CAP, dtype=jnp.int32)[None, :] < tile_count[:, None]
        named = jnp.where(live, tile_block, -1)
        index = jnp.concatenate([named, named], axis=1).reshape(ND, 1, 2 * CAP)
        example = tile_example.reshape(NP, 1, 128)
        hbm = pl.BlockSpec(memory_space=pl.ANY)
        vmem = pl.BlockSpec(memory_space=pltpu.VMEM)

        def V(shape, kind=F32):
            return pltpu.VMEM(shape, kind)

        dma = pltpu.SemaphoreType.DMA
        scratch = [
            V((E, DIN), BF16), V((NH, 128), jnp.int32), V((NP, 1, 128), jnp.int32), V((BD, W)), V((BD, W)),
            V((DIN, H1), BF16), V((1, H1)), V((H1, H2), BF16), V((1, H2)), V((1, H2), BF16),
            V((ND, CAP, W), BF16), V((ND, 1, 128), jnp.int32), V((BD, W)), V((BD, 2 * W), BF16),
            V((E, H2), BF16), V((DIN, E), BF16), V((H1, E), BF16), V((E, H1)), V((E, H2)),
            V((NH, 128)), V((128, ND * CAP), BF16),
            V((2, NP, 1, 128)), V((ND, 1, 128)), V((2 * NH, ND * CAP), BF16), V((2 * NH, ND * CAP)),
            V((2, NP, 1, 128)), V((ND, 1, 128)),
            V((BD, R * CAP), BF16), V((BD, W)), V((BD, W)), V((BD, W)),
            V((E, H1), BF16), V((E, H2), BF16),
            V((DIN // 2, H1), BF16), V((H1 // 2, H2)), V((DIN // 2, H1)), V((DIN // 2, H1), BF16), V((H1 // 2, H2)),
            V((DIN // 2, H1), BF16), V((H1 // 2, H2)), V((NC, c1, 128), BF16), V((NC, c2, 128)),
            V((c1, 128), BF16), V((c2, 128)), V((DIN, H1), BF16), V((H1, H2)),
            V((8, 128)), V((R, 8, 128)), V((8, 128)), V((B, 8, 128)),
            dma((10,)), dma((6,)), dma(()), dma((B,)), dma(()), dma(()),
            dma((2,)), dma((2,)), dma((2, B)), dma((2,)), dma((2,)),
            dma((14,)), dma((6,)),
        ]
        shape = jax.ShapeDtypeStruct
        prob, z_new, n_new, g_one, g_two, small = pl.pallas_call(
            functools.partial(step_kernel, B, R),
            out_shape=(
                shape((NH, 128), F32), shape((BD, W), F32), shape((BD, W), F32),
                shape((DIN, H1), BF16), shape((H1, H2), F32), shape((8, 128), F32),
            ),
            in_specs=[hbm] * 12,
            out_specs=(vmem, hbm, hbm, hbm, hbm, vmem),
            scratch_shapes=scratch,
            compiler_params=pltpu.CompilerParams(
                collective_id=0, has_side_effects=True, vmem_limit_bytes=60 * 1024 * 1024
            ),
        )(
            dense, labels.reshape(NH, 128), tile_values, index, example, z_state, n_state,
            w_one, b_one.reshape(1, H1), w_two, b_two.reshape(1, H2), head.reshape(1, H2),
        )
        flat = small.reshape(-1)
        return (
            prob.reshape(E), z_new, n_new, g_one.astype(F32), flat[:H1], g_two,
            flat[H1:H1 + H2], flat[H1 + H2:H1 + 2 * H2],
        )

    every = ("blk", "rep")
    return jax.shard_map(
        per_device,
        mesh=mesh,
        in_specs=(
            P(every, None), P(every), P(every, None, None), P(every, None), P(every, None), P(every),
            P(every, None), P(every, None), P(), P(), P(), P(), P(),
        ),
        out_specs=(P(every), P(every, None), P(every, None), P(), P(), P(), P(), P()),
        check_vma=False,
    )
```

```python
import functools

import jax
import jax.numpy as jnp
from jax import lax
from jax.experimental import pallas as pl
from jax.experimental.pallas import tpu as pltpu
from jax.sharding import PartitionSpec as P

MESH = pl.DeviceIdType.MESH
F32 = jnp.float32
BF16 = jnp.bfloat16
NT = (((1,), (1,)), ((), ()))
STRIDE = 27


def mm(a, b):
    return jnp.dot(a, b, preferred_element_type=F32)


def mm_nt(a, b):
    return lax.dot_general(a, b, NT, preferred_element_type=F32)


def step_kernel(
    B, R,
    dense_h, labels_h, values_h, block_h, example_h, count_h, z_h, n_h,
    w_one_h, b_one_h, w_two_h, b_two_h, head_h,
    prob_o, z_o, n_o, grads_o, small_o,
    dense_v, labels_v, block_v, example_t, count_v, z_v, n_v, w_one_v, b_one_v, w_two_v, b_two_v, head_v,
    table_v, index_send, example_v,
    got_values, got_index, weight_v, weight_pair,
    hid_two_v, dense_t, hid_one_t, scale_one, scale_two, deep_v, low_hot, slot_hot,
    logit_send, logit_got, spread, picked, res_send, res_got,
    block_hot, total, z_out_v, n_out_v,
    d_one_v, d_two_v, own_one, own_two,
    part, pair, summed, got, final, full,
    small_v, small_rep, small_sum, small_blk,
    load_sem, own_sem, ready_sem, index_sem, value_sem, logit_sem, res_sem,
    pair_sem, rs_sem, ag_sem, fw_sem, small_sem,
    send_sem, out_sem,
):
    ND = B * R
    NC = ND // 2
    X = R // 2
    Z = 4 if B % 4 == 0 else B
    Y = B // Z
    E, DIN = dense_v.shape
    H1 = w_one_v.shape[1]
    H2 = w_two_v.shape[1]
    CAP, W = got_values.shape[1], got_values.shape[2]
    BD = z_v.shape[0]
    NH = E // 128
    NP = ND // 2
    c1 = DIN * H1 // (128 * ND)
    c2 = H1 * H2 // (128 * ND)
    j1 = H1 // 128
    j2 = H2 // 128
    blk = lax.axis_index("blk")
    rep = lax.axis_index("rep")
    y, zz = lax.div(blk, Z), lax.rem(blk, Z)
    x, core = lax.div(rep, 2), lax.rem(rep, 2)
    other = 1 - core
    me = blk * R + rep
    chip = blk * X + x
    y_at = [lax.rem(y + i, Y) * Z for i in range(Y)]
    z_at = [lax.rem(zz + i, Z) for i in range(Z)]
    x_at = [lax.rem(x + i, X) for i in range(X)]

    def chip_at(m):
        spot = (m * STRIDE) % NC
        dy, dz, dx = spot // (Z * X), spot // X % Z, spot % X
        return y_at[dy] + z_at[dz], x_at[dx]

    def chip_from(m):
        spot = lax.rem(m * STRIDE, NC)
        dy, dz, dx = lax.div(spot, Z * X), lax.rem(lax.div(spot, X), Z), lax.rem(spot, X)
        return lax.rem(y + Y - dy, Y) * Z + lax.rem(zz + Z - dz, Z), lax.rem(x + X - dx, X)

    loads = [
        (block_h, block_v), (count_h, count_v), (example_h, example_t), (z_h, z_v), (n_h, n_v), (dense_h, dense_v),
        (w_one_h, w_one_v), (b_one_h, b_one_v), (w_two_h, w_two_v), (b_two_h, b_two_v), (head_h, head_v),
        (labels_h, labels_v),
    ]
    copies = [pltpu.make_async_copy(s, d, load_sem.at[i]) for i, (s, d) in enumerate(loads)]
    for copy in copies:
        copy.start()

    def send(src, dst, sem_at, recv, where):
        pltpu.make_async_remote_copy(
            src_ref=src, dst_ref=dst, send_sem=send_sem.at[sem_at], recv_sem=recv,
            device_id=where, device_id_type=MESH,
        ).start()

    def wait_for(ref, sem):
        pltpu.make_async_copy(ref, ref, sem).wait()

    barrier = pltpu.get_barrier_semaphore()
    for k in range(1, B):
        pl.semaphore_signal(barrier, inc=1, device_id=(lax.rem(blk + k, B), rep), device_id_type=MESH)
    for k in range(1, R):
        pl.semaphore_signal(barrier, inc=1, device_id=(blk, lax.rem(rep + k, R)), device_id_type=MESH)
    own_value = pltpu.make_async_copy(values_h.at[me], got_values.at[me], own_sem.at[0])
    own_value.start()

    first_half = lax.broadcasted_iota(jnp.int32, (1, 128), 1) < CAP
    copies[0].wait()
    copies[1].wait()
    live = lax.broadcasted_iota(jnp.int32, (CAP, ND), 0) < count_v[...]
    named = jnp.where(live, block_v[...], -1).astype(F32)
    table_v[...] = jnp.concatenate([named, named], axis=0).T.astype(jnp.int32)
    for o in range(ND):
        index_send[o] = table_v[o:o + 1, :]

    pl.semaphore_wait(barrier, B + R - 2)
    for k in range(1, R):
        pl.semaphore_signal(ready_sem, inc=1, device_id=(blk, lax.rem(rep + k, R)), device_id_type=MESH)
    copies[2].wait()
    named = example_t[...].astype(F32)
    table_v[...] = jnp.concatenate([named, named], axis=0).T.astype(jnp.int32)
    for p in range(NP):
        example_v[p] = jnp.where(first_half, table_v[2 * p:2 * p + 1, :], table_v[2 * p + 1:2 * p + 2, :])
    pl.semaphore_wait(ready_sem, R - 1)

    for m in range(NC):
        blk_to, x_to = chip_at(m)
        for c in ((1,) if m == 0 else (0, 1)):
            rep_to = x_to * 2 + (other if m == 0 else c)
            to = blk_to * R + rep_to
            send(index_send.at[to], got_index.at[me], 0, index_sem.at[m // 2], (blk_to, rep_to))
            send(values_h.at[to], got_values.at[me], 1, value_sem.at[m // 2], (blk_to, rep_to))
    got_index[me] = index_send[me]

    copies[3].wait()
    copies[4].wait()
    z = z_v[...]
    shrunk = z - jnp.where(z > 0, 0.5, -0.5)
    weight = jnp.where(jnp.abs(z) > 0.5, -shrunk / ((1.0 + jnp.sqrt(n_v[...])) / 0.5 + 0.1), 0.0)
    weight_v[...] = weight
    high = weight.astype(BF16)
    weight_pair[:, :W] = high
    weight_pair[:, W:] = (weight - high.astype(F32)).astype(BF16)

    for copy in copies[5:]:
        copy.wait()
    rows = 256
    head_row = jnp.concatenate([head_v[q:q + 1, :] for q in range(j2)], axis=1)
    head_rows = jnp.broadcast_to(head_row, (8, H2))

    @pl.loop(0, E // rows)
    def _(i):
        at = pl.multiple_of(i * rows, rows)
        dense = dense_v[pl.ds(at, rows), :]
        pre_one = mm(dense, w_one_v[...]) + b_one_v[...]
        gate_one = jax.nn.sigmoid(pre_one)
        hid_one = (pre_one * gate_one).astype(BF16)
        pre_two = mm(hid_one, w_two_v[...]) + b_two_v[...]
        gate_two = jax.nn.sigmoid(pre_two)
        hid_two = (pre_two * gate_two).astype(BF16)
        hid_two_v[pl.ds(at, rows), :] = hid_two
        two = head_row.astype(F32) * (gate_two * (1.0 + pre_two * (1.0 - gate_two)))
        scale_two[pl.ds(at, rows), :] = two
        back = mm_nt(two.astype(BF16), w_two_v[...])
        scale_one[pl.ds(at, rows), :] = back * (gate_one * (1.0 + pre_one * (1.0 - gate_one)))
        deep = mm_nt(head_rows, hid_two)
        for q in range(rows // 128):
            deep_v[pl.ds(i * (rows // 128) + q, 1), :] = deep[0:1, q * 128:(q + 1) * 128]
        dense_t[:, pl.ds(at, rows)] = dense.T
        hid_one_t[:, pl.ds(at, rows)] = hid_one.T

    @pl.loop(0, NP)
    def _(p):
        at = pl.multiple_of(p * 128, 128)
        low = lax.bitwise_and(example_v[p], 127)
        hot = (lax.broadcasted_iota(jnp.int32, (128, 128), 0) == low).astype(F32)
        low_hot[:, pl.ds(at, 128)] = hot.astype(BF16)
        slot_hot[pl.ds(at, 128), :] = hot.T.astype(BF16)

    def merged(ref, p):
        return jnp.where(first_half, ref[2 * p], ref[2 * p + 1])

    def flipped(row):
        return pltpu.roll(jnp.broadcast_to(row, (8, 128)), CAP, axis=1)[0:1]

    def logits_of(places):
        spots = [b * X + xs for b, xs in places]
        four = jnp.concatenate([got_values[pl.ds(2 * q, 2)].reshape(2 * CAP, W) for q in spots], axis=0)
        score = mm_nt(weight_pair[...], jnp.concatenate([four, four], axis=1))
        for i, q in enumerate(spots):
            hit = lax.broadcasted_iota(jnp.int32, (BD, 128), 0) == merged(got_index, q)
            row = jnp.sum(jnp.where(hit, score[:, i * 128:(i + 1) * 128], 0.0), axis=0, keepdims=True)
            logit_send[0, q] = row
            logit_send[1, q] = flipped(row)

    own_value.wait()
    wait_for(got_index.at[pl.ds(0, 3)], index_sem.at[0])
    wait_for(got_values.at[pl.ds(0, 3)], value_sem.at[0])
    b_next, x_next = chip_from(1)
    logits_of([(blk, x), (b_next, x_next)])
    send(logit_send.at[1, chip], logit_got.at[me], 2, logit_sem, (blk, x * 2 + other))
    for c, turn in ((0, core), (1, other)):
        send(logit_send.at[turn, b_next * X + x_next], logit_got.at[me], 2, logit_sem, (b_next, x_next * 2 + c))
    logit_got[me] = logit_send[0, chip]

    @pl.loop(1, NC // 2)
    def _(u):
        wait_for(got_index.at[pl.ds(0, 4)], index_sem.at[u])
        wait_for(got_values.at[pl.ds(0, 4)], value_sem.at[u])
        places = [chip_from(2 * u), chip_from(2 * u + 1)]
        logits_of(places)
        for b_to, x_to in places:
            for c, turn in ((0, core), (1, other)):
                send(logit_send.at[turn, b_to * X + x_to], logit_got.at[me], 2, logit_sem, (b_to, x_to * 2 + c))

    wait_for(logit_got.at[pl.ds(0, ND - 1)], logit_sem)
    eight = lax.broadcasted_iota(jnp.int32, (NH, 128), 0)
    for p in range(NP):
        mine = eight == lax.shift_right_logical(example_v[p], 7)
        term = jnp.where(mine, merged(logit_got, p), 0.0)
        top = term.astype(BF16).astype(F32)
        spread[:, p * 128:(p + 1) * 128] = jnp.concatenate([top, term - top], axis=0).astype(BF16)
    wide = mm(spread[...], slot_hot[...])
    prob = jax.nn.sigmoid(wide[:NH] + wide[NH:] + deep_v[...])
    prob_o[...] = prob
    residual = prob - labels_v[...].astype(F32)
    dlogit = residual.astype(BF16).astype(F32)

    upright = jnp.concatenate([dlogit, jnp.zeros((128 - NH, 128), F32)], axis=0).T
    for q in range(NH):
        span = slice(q * 128, (q + 1) * 128)
        column = upright[:, q:q + 1]
        d_two_v[span, :] = (scale_two[span, :] * column).astype(BF16)
        d_one_v[span, :] = (scale_one[span, :] * column).astype(BF16)

    half_one, half_two = DIN // 2, H1 // 2
    rep_other = x * 2 + other

    def cut_one(q):
        return slice(q // j1 * c1, (q // j1 + 1) * c1), slice(q % j1 * 128, (q % j1 + 1) * 128)

    def cut_two(q):
        return slice(q // j2 * c2, (q // j2 + 1) * c2), slice(q % j2 * 128, (q % j2 + 1) * 128)

    grad_one = mm(dense_t[pl.ds(pl.multiple_of(other * half_one, half_one), half_one), :], d_one_v[...])
    grad_two = mm(hid_one_t[pl.ds(pl.multiple_of(other * half_two, half_two), half_two), :], d_two_v[...])
    for q in range(NC):
        part[q, 0:c1, :] = grad_one[cut_one(q)].astype(BF16)
        part[q, c1:c1 + c2, :] = grad_two[cut_two(q)].astype(BF16)
    send(part, pair, 3, pair_sem, (blk, rep_other))
    own_one[...] = mm(dense_t[pl.ds(pl.multiple_of(core * half_one, half_one), half_one), :], d_one_v[...])
    own_two[...] = mm(hid_one_t[pl.ds(pl.multiple_of(core * half_two, half_two), half_two), :], d_two_v[...])
    wait_for(pair, pair_sem)
    for q in range(NC):
        summed[q, 0:c1, :] = (own_one[cut_one(q)] + pair[q, 0:c1, :].astype(F32)).astype(BF16)
        summed[q, c1:c1 + c2, :] = (own_two[cut_two(q)] + pair[q, c1:c1 + c2, :].astype(F32)).astype(BF16)

    for m in range(1, NC):
        b_to, x_to = chip_at(m)
        send(summed.at[b_to * X + x_to], got.at[chip], 4, rs_sem, (b_to, x_to * 2 + core))
    own_piece = pltpu.make_async_copy(summed.at[chip], got.at[chip], own_sem.at[1])
    own_piece.start()

    table = jnp.concatenate([dlogit, jnp.zeros_like(dlogit)], axis=0).astype(BF16)
    picked[...] = mm(table, low_hot[...])
    for p in range(NP):
        mine = eight == lax.shift_right_logical(example_v[p], 7)
        row = jnp.sum(jnp.where(mine, picked[0:NH, p * 128:(p + 1) * 128], 0.0), axis=0, keepdims=True)
        res_send[0, p] = row
        res_send[1, p] = flipped(row)
    for m in range(NC):
        b_to, x_to = chip_at(m)
        q = b_to * X + x_to
        if m == 0:
            send(res_send.at[1, q], res_got.at[me], 5, res_sem, (b_to, x_to * 2 + other))
        else:
            for c, turn in ((0, core), (1, other)):
                send(res_send.at[turn, q], res_got.at[me], 5, res_sem, (b_to, x_to * 2 + c))
    res_got[me] = res_send[0, chip]

    grad_head = jnp.zeros((8, H2), F32)
    for q in range(NH):
        grad_head += mm(jnp.broadcast_to(dlogit[q:q + 1, :], (8, 128)).astype(BF16), hid_two_v[q * 128:(q + 1) * 128, :])
    ones = jnp.ones((8, E), BF16)
    bias_one = mm(ones, d_one_v[...])
    bias_two = mm(ones, d_two_v[...])
    small_v[...] = jnp.zeros_like(small_v)
    for q in range(j1):
        small_v[q:q + 1, :] = bias_one[0:1, q * 128:(q + 1) * 128]
    for q in range(j2):
        small_v[j1 + q:j1 + q + 1, :] = bias_two[0:1, q * 128:(q + 1) * 128]
        small_v[j1 + j2 + q:j1 + j2 + q + 1, :] = grad_head[0:1, q * 128:(q + 1) * 128]
    for k in range(1, R):
        send(small_v, small_rep.at[rep], 6, small_sem.at[0], (blk, lax.rem(rep + k, R)))
    small_rep[rep] = small_v[...]

    own_piece.wait()
    wait_for(got.at[pl.ds(0, NC - 1)], rs_sem)
    final[...] = lax.fori_loop(
        1, NC, lambda q, a: a + got[q].astype(F32), got[0].astype(F32)
    ).astype(BF16)
    for m in range(1, NC):
        b_to, x_to = chip_at(m)
        send(final, full.at[core, chip], 7, ag_sem.at[m // 4], (b_to, x_to * 2 + core))
    send(final, full.at[core, chip], 8, fw_sem, (blk, rep_other))
    own_final = pltpu.make_async_copy(final, full.at[core, chip], own_sem.at[2])
    own_final.start()

    wait_for(small_rep.at[pl.ds(0, R - 1)], small_sem.at[0])
    acc = small_rep[0]
    for r in range(1, R):
        acc = acc + small_rep[r]
    small_sum[...] = acc
    for k in range(1, B):
        send(small_sum, small_blk.at[blk], 9, small_sem.at[1], (lax.rem(blk + k, B), rep))
    small_blk[blk] = acc

    wait_for(res_got.at[pl.ds(0, ND - 1)], res_sem)
    total[...] = jnp.zeros_like(total)

    @pl.loop(0, B)
    def _(g):
        for h in range(X):
            p = g * X + h
            hit = lax.broadcasted_iota(jnp.int32, (BD, 128), 0) == merged(got_index, p)
            block_hot[:, h * 128:(h + 1) * 128] = jnp.where(hit, merged(res_got, p), 0.0).astype(BF16)
        values = got_values[pl.ds(g * R, R)].reshape(R * CAP, W)
        total[...] += mm(block_hot[...], values)

    grad = total[...]
    n_old = n_v[...]
    n_new = n_old + grad * grad
    n_out_v[...] = n_new
    z_out_v[...] = z_v[...] + grad - (jnp.sqrt(n_new) - jnp.sqrt(n_old)) / 0.5 * weight_v[...]
    out_z = pltpu.make_async_copy(z_out_v, z_o, out_sem.at[0])
    out_z.start()
    out_n = pltpu.make_async_copy(n_out_v, n_o, out_sem.at[1])
    out_n.start()

    own_final.wait()

    def pass_on(m):
        b_from, x_from = chip_from(m)
        q = b_from * X + x_from
        send(full.at[core, q], full.at[core, q], 8, fw_sem, (blk, rep_other))

    wait_for(got.at[pl.ds(0, 3)], ag_sem.at[0])
    for m in range(1, 4):
        pass_on(m)

    @pl.loop(1, NC // 4)
    def _(g):
        wait_for(got.at[pl.ds(0, 4)], ag_sem.at[g])
        for i in range(4):
            pass_on(4 * g + i)

    out_a = pltpu.make_async_copy(full.at[core], grads_o.at[core], out_sem.at[2])
    out_a.start()
    wait_for(small_blk.at[pl.ds(0, B - 1)], small_sem.at[1])
    acc = small_blk[0]
    for r in range(1, B):
        acc = acc + small_blk[r]
    small_o[...] = acc
    wait_for(got, fw_sem)
    out_b = pltpu.make_async_copy(full.at[other], grads_o.at[other], out_sem.at[3])
    out_b.start()

    wait_for(got_index.at[pl.ds(0, ND - 1)], send_sem.at[0])
    wait_for(got_values.at[pl.ds(0, ND - 1)], send_sem.at[1])
    wait_for(logit_got.at[pl.ds(0, ND - 1)], send_sem.at[2])
    wait_for(part, send_sem.at[3])
    wait_for(got.at[pl.ds(0, NC - 1)], send_sem.at[4])
    wait_for(res_got.at[pl.ds(0, ND - 1)], send_sem.at[5])
    wait_for(small_rep.at[pl.ds(0, R - 1)], send_sem.at[6])
    wait_for(got.at[pl.ds(0, NC - 1)], send_sem.at[7])
    wait_for(got, send_sem.at[8])
    wait_for(small_blk.at[pl.ds(0, B - 1)], send_sem.at[9])
    for copy in (out_z, out_n, out_a, out_b):
        copy.wait()


def finish_kernel(
    c1, c2, grads_h, small_h, prob_h, z_h, n_h, prob_o, z_o, n_o, g_one_o, b_one_o, g_two_o, b_two_o, head_o,
    grads_v, z_v, n_v, one_v, two_v, in_sem, out_sem,
):
    NC = grads_v.shape[1]
    DIN, H1 = one_v.shape
    H2 = two_v.shape[1]
    j1, j2 = H1 // 128, H2 // 128
    parts = 2
    step = NC // parts
    ins = [
        pltpu.make_async_copy(grads_h.at[h, pl.ds(i * step, step)], grads_v.at[h, pl.ds(i * step, step)], in_sem.at[h * parts + i])
        for h in range(2) for i in range(parts)
    ]
    in_z = pltpu.make_async_copy(z_h, z_v, in_sem.at[2 * parts])
    in_n = pltpu.make_async_copy(n_h, n_v, in_sem.at[2 * parts + 1])
    for copy in (*ins, in_z, in_n):
        copy.start()
    prob_o[...] = prob_h[...]
    for q in range(j1):
        b_one_o[:, q * 128:(q + 1) * 128] = small_h[q:q + 1, :]
    for q in range(j2):
        b_two_o[:, q * 128:(q + 1) * 128] = small_h[j1 + q:j1 + q + 1, :]
        head_o[:, q * 128:(q + 1) * 128] = small_h[j1 + j2 + q:j1 + j2 + q + 1, :]
    outs = []
    for h in range(2):
        for i in range(parts):
            ins[h * parts + i].wait()
            for q in range(i * step, (i + 1) * step):
                r1 = h * (DIN // 2) + q // j1 * c1
                r2 = h * (H1 // 2) + q // j2 * c2
                one_v[r1:r1 + c1, q % j1 * 128:(q % j1 + 1) * 128] = grads_v[h, q, 0:c1, :].astype(F32)
                two_v[r2:r2 + c2, q % j2 * 128:(q % j2 + 1) * 128] = grads_v[h, q, c1:c1 + c2, :].astype(F32)
            n1, n2 = DIN // (2 * parts), H1 // (2 * parts)
            s1, s2 = (h * parts + i) * n1, (h * parts + i) * n2
            outs.append(pltpu.make_async_copy(one_v.at[pl.ds(s1, n1)], g_one_o.at[pl.ds(s1, n1)], out_sem.at[2 * (h * parts + i)]))
            outs.append(pltpu.make_async_copy(two_v.at[pl.ds(s2, n2)], g_two_o.at[pl.ds(s2, n2)], out_sem.at[2 * (h * parts + i) + 1]))
            outs[-2].start()
            outs[-1].start()
        if h == 0:
            in_z.wait()
            outs.append(pltpu.make_async_copy(z_v, z_o, out_sem.at[4 * parts]))
            outs[-1].start()
            in_n.wait()
            outs.append(pltpu.make_async_copy(n_v, n_o, out_sem.at[4 * parts + 1]))
            outs[-1].start()
    for copy in outs:
        copy.wait()


def solution(mesh):
    B, R = mesh.shape["blk"], mesh.shape["rep"]
    ND = B * R
    NC = ND // 2

    def per_device(
        dense, labels, tile_values, tile_block, tile_example, tile_count, z_state, n_state,
        w_one, b_one, w_two, b_two, head,
    ):
        E, DIN = dense.shape
        _, CAP, W = tile_values.shape
        BD = z_state.shape[0]
        H1, H2 = w_two.shape
        NH = E // 128
        NP = ND // 2
        c1 = DIN * H1 // (128 * ND)
        c2 = H1 * H2 // (128 * ND)
        hbm = pl.BlockSpec(memory_space=pl.ANY)
        vmem = pl.BlockSpec(memory_space=pltpu.VMEM)
        I32 = jnp.int32

        def V(shape, kind=F32):
            return pltpu.VMEM(shape, kind)

        dma = pltpu.SemaphoreType.DMA
        scratch = [
            V((E, DIN), BF16), V((NH, 128), I32), V((CAP, ND), I32), V((CAP, ND), I32), V((1, ND), I32),
            V((BD, W)), V((BD, W)), V((DIN, H1), BF16), V((1, H1)), V((H1, H2), BF16), V((1, H2)), V((H2 // 128, 128), BF16),
            V((ND, 128), I32), V((ND, 1, 128), I32), V((NP, 1, 128), I32),
            V((ND, CAP, W), BF16), V((ND, 1, 128), I32), V((BD, W)), V((BD, 2 * W), BF16),
            V((E, H2), BF16), V((DIN, E), BF16), V((H1, E), BF16), V((E, H1)), V((E, H2)),
            V((NH, 128)), V((128, ND * CAP), BF16), V((ND * CAP, 128), BF16),
            V((2, NP, 1, 128)), V((ND, 1, 128)), V((2 * NH, ND * CAP), BF16), V((2 * NH, ND * CAP)),
            V((2, NP, 1, 128)), V((ND, 1, 128)),
            V((BD, R * CAP), BF16), V((BD, W)), V((BD, W)), V((BD, W)),
            V((E, H1), BF16), V((E, H2), BF16), V((DIN // 2, H1)), V((H1 // 2, H2)),
            V((NC, c1 + c2, 128), BF16), V((NC, c1 + c2, 128), BF16), V((NC, c1 + c2, 128), BF16),
            V((NC, c1 + c2, 128), BF16), V((c1 + c2, 128), BF16), V((2, NC, c1 + c2, 128), BF16),
            V((8, 128)), V((R, 8, 128)), V((8, 128)), V((B, 8, 128)),
            dma((12,)), dma((3,)), pltpu.SemaphoreType.REGULAR, dma((NC // 2,)), dma((NC // 2,)), dma(()), dma(()),
            dma(()), dma(()), dma((NC // 4,)), dma(()), dma((2,)),
            dma((10,)), dma((4,)),
        ]
        shape = jax.ShapeDtypeStruct
        prob, z_new, n_new, grads, small = pl.pallas_call(
            functools.partial(step_kernel, B, R),
            out_shape=(
                shape((NH, 128), F32), shape((BD, W), F32), shape((BD, W), F32),
                shape((2, NC, c1 + c2, 128), BF16), shape((8, 128), F32),
            ),
            in_specs=[hbm] * 13,
            out_specs=(vmem, hbm, hbm, hbm, vmem),
            scratch_shapes=scratch,
            compiler_params=pltpu.CompilerParams(
                collective_id=0, has_side_effects=True, vmem_limit_bytes=60 * 1024 * 1024
            ),
        )(
            dense, labels.reshape(NH, 128), tile_values, tile_block.T, tile_example.T, tile_count.reshape(1, ND),
            z_state, n_state, w_one, b_one.reshape(1, H1), w_two, b_two.reshape(1, H2), head.reshape(H2 // 128, 128),
        )
        prob, z_new, n_new, g_one, g_b_one, g_two, g_b_two, g_head = pl.pallas_call(
            functools.partial(finish_kernel, c1, c2),
            out_shape=(
                shape((NH, 128), F32), shape((BD, W), F32), shape((BD, W), F32), shape((DIN, H1), F32),
                shape((1, H1), F32), shape((H1, H2), F32), shape((1, H2), F32), shape((1, H2), F32),
            ),
            in_specs=[hbm, vmem, vmem, hbm, hbm],
            out_specs=(vmem, hbm, hbm, hbm, vmem, hbm, vmem, vmem),
            scratch_shapes=[
                V((2, NC, c1 + c2, 128), BF16), V((BD, W)), V((BD, W)), V((DIN, H1)), V((H1, H2)), dma((6,)), dma((10,)),
            ],
            compiler_params=pltpu.CompilerParams(vmem_limit_bytes=32 * 1024 * 1024),
        )(grads, small, prob, z_new, n_new)
        return (
            prob.reshape(E), z_new, n_new, g_one, g_b_one.reshape(H1), g_two, g_b_two.reshape(H2), g_head.reshape(H2),
        )

    every = ("blk", "rep")
    return jax.shard_map(
        per_device,
        mesh=mesh,
        in_specs=(
            P(every, None), P(every), P(every, None, None), P(every, None), P(every, None), P(every),
            P(every, None), P(every, None), P(), P(), P(), P(), P(),
        ),
        out_specs=(P(every), P(every, None), P(every, None), P(), P(), P(), P(), P()),
        check_vma=False,
    )
```

```python
import functools

import jax
import jax.numpy as jnp
from jax import lax
from jax.experimental import pallas as pl
from jax.experimental.pallas import tpu as pltpu
from jax.sharding import PartitionSpec as P

MESH = pl.DeviceIdType.MESH
F32 = jnp.float32
BF16 = jnp.bfloat16
NT = (((1,), (1,)), ((), ()))
STRIDE = 27


def mm(a, b):
    return jnp.dot(a, b, preferred_element_type=F32)


def mm_nt(a, b):
    return lax.dot_general(a, b, NT, preferred_element_type=F32)


def step_kernel(
    B, R,
    dense_h, labels_h, values_h, block_h, example_h, count_h, z_h, n_h,
    w_one_h, b_one_h, w_two_h, b_two_h, head_h,
    prob_o, z_o, n_o, grad_a_o, grad_b_o, small_o,
    dense_v, labels_v, block_v, example_t, count_v, z_v, n_v, w_one_v, b_one_v, w_two_v, b_two_v, head_v,
    table_v, index_send, example_v,
    got_values, got_index, weight_v, weight_pair,
    hid_two_v, dense_t, hid_one_t, scale_one, scale_two, deep_v, low_hot, slot_hot,
    logit_send, logit_got, spread, picked, res_send, res_got,
    block_hot, total, z_out_v, n_out_v,
    d_one_v, d_two_v, own_one, own_two,
    part_a, pair_a, sum_a, got_a, final_a, full_a, part_b, pair_b, sum_b, got_b, final_b, full_b,
    small_v, small_rep, small_sum, small_blk,
    load_sem, own_sem, ready_sem, index_sem, value_sem, logit_sem, res_sem,
    pair_sem, rs_sem, ag_sem, fw_sem, small_sem,
    send_sem, out_sem,
):
    ND = B * R
    NC = ND // 2
    X = R // 2
    Z = 4 if B % 4 == 0 else B
    Y = B // Z
    E, DIN = dense_v.shape
    H1 = w_one_v.shape[1]
    H2 = w_two_v.shape[1]
    CAP, W = got_values.shape[1], got_values.shape[2]
    BD = z_v.shape[0]
    NH = E // 128
    NP = ND // 2
    c1 = DIN * H1 // (128 * ND)
    c2 = H1 * H2 // (128 * ND)
    j1 = H1 // 128
    j2 = H2 // 128
    blk = lax.axis_index("blk")
    rep = lax.axis_index("rep")
    y, zz = lax.div(blk, Z), lax.rem(blk, Z)
    x, core = lax.div(rep, 2), lax.rem(rep, 2)
    other = 1 - core
    me = blk * R + rep
    chip = blk * X + x
    y_at = [lax.rem(y + i, Y) * Z for i in range(Y)]
    z_at = [lax.rem(zz + i, Z) for i in range(Z)]
    x_at = [lax.rem(x + i, X) for i in range(X)]

    def chip_at(m):
        spot = (m * STRIDE) % NC
        dy, dz, dx = spot // (Z * X), spot // X % Z, spot % X
        return y_at[dy] + z_at[dz], x_at[dx]

    def chip_from(m):
        spot = lax.rem(m * STRIDE, NC)
        dy, dz, dx = lax.div(spot, Z * X), lax.rem(lax.div(spot, X), Z), lax.rem(spot, X)
        return lax.rem(y + Y - dy, Y) * Z + lax.rem(zz + Z - dz, Z), lax.rem(x + X - dx, X)

    loads = [
        (block_h, block_v), (count_h, count_v), (example_h, example_t), (z_h, z_v), (n_h, n_v), (dense_h, dense_v),
        (w_one_h, w_one_v), (b_one_h, b_one_v), (w_two_h, w_two_v), (b_two_h, b_two_v), (head_h, head_v),
        (labels_h, labels_v),
    ]
    copies = [pltpu.make_async_copy(s, d, load_sem.at[i]) for i, (s, d) in enumerate(loads)]
    for copy in copies:
        copy.start()

    def send(src, dst, sem_at, recv, where):
        pltpu.make_async_remote_copy(
            src_ref=src, dst_ref=dst, send_sem=send_sem.at[sem_at], recv_sem=recv,
            device_id=where, device_id_type=MESH,
        ).start()

    def wait_for(ref, sem):
        pltpu.make_async_copy(ref, ref, sem).wait()

    barrier = pltpu.get_barrier_semaphore()
    for k in range(1, B):
        pl.semaphore_signal(barrier, inc=1, device_id=(lax.rem(blk + k, B), rep), device_id_type=MESH)
    for k in range(1, R):
        pl.semaphore_signal(barrier, inc=1, device_id=(blk, lax.rem(rep + k, R)), device_id_type=MESH)
    own_value = pltpu.make_async_copy(values_h.at[me], got_values.at[me], own_sem.at[0])
    own_value.start()

    first_half = lax.broadcasted_iota(jnp.int32, (1, 128), 1) < CAP
    copies[0].wait()
    copies[1].wait()
    live = lax.broadcasted_iota(jnp.int32, (CAP, ND), 0) < count_v[...]
    named = jnp.where(live, block_v[...], -1).astype(F32)
    table_v[...] = jnp.concatenate([named, named], axis=0).T.astype(jnp.int32)
    for o in range(ND):
        index_send[o] = table_v[o:o + 1, :]

    pl.semaphore_wait(barrier, B + R - 2)
    for k in range(1, R):
        pl.semaphore_signal(ready_sem, inc=1, device_id=(blk, lax.rem(rep + k, R)), device_id_type=MESH)

    def give(m, c):
        blk_to, x_to = chip_at(m)
        rep_to = x_to * 2 + c
        to = blk_to * R + rep_to
        send(index_send.at[to], got_index.at[me], 0, index_sem.at[m // 2], (blk_to, rep_to))
        send(values_h.at[to], got_values.at[me], 1, value_sem.at[m // 2], (blk_to, rep_to))

    give(0, other)
    for m in range(1, NC):
        spot = (m * STRIDE) % NC
        if spot < X:
            give(m, 0)
            give(m, 1)
        elif spot % X == 0:
            give(m, core)
    copies[2].wait()
    named = example_t[...].astype(F32)
    table_v[...] = jnp.concatenate([named, named], axis=0).T.astype(jnp.int32)
    for p in range(NP):
        example_v[p] = jnp.where(first_half, table_v[2 * p:2 * p + 1, :], table_v[2 * p + 1:2 * p + 2, :])
    pl.semaphore_wait(ready_sem, R - 1)

    for m in range(1, NC):
        spot = (m * STRIDE) % NC
        if spot >= X and spot % X == 0:
            give(m, other)
        elif spot >= X:
            give(m, 0)
            give(m, 1)
    got_index[me] = index_send[me]

    copies[3].wait()
    copies[4].wait()
    z = z_v[...]
    shrunk = z - jnp.where(z > 0, 0.5, -0.5)
    weight = jnp.where(jnp.abs(z) > 0.5, -shrunk / ((1.0 + jnp.sqrt(n_v[...])) / 0.5 + 0.1), 0.0)
    weight_v[...] = weight
    high = weight.astype(BF16)
    weight_pair[:, :W] = high
    weight_pair[:, W:] = (weight - high.astype(F32)).astype(BF16)

    for copy in copies[5:]:
        copy.wait()
    rows = 256
    head_row = jnp.concatenate([head_v[q:q + 1, :] for q in range(j2)], axis=1)
    head_rows = jnp.broadcast_to(head_row, (8, H2))

    @pl.loop(0, E // rows)
    def _(i):
        at = pl.multiple_of(i * rows, rows)
        dense = dense_v[pl.ds(at, rows), :]
        pre_one = mm(dense, w_one_v[...]) + b_one_v[...]
        gate_one = jax.nn.sigmoid(pre_one)
        hid_one = (pre_one * gate_one).astype(BF16)
        pre_two = mm(hid_one, w_two_v[...]) + b_two_v[...]
        gate_two = jax.nn.sigmoid(pre_two)
        hid_two = (pre_two * gate_two).astype(BF16)
        hid_two_v[pl.ds(at, rows), :] = hid_two
        two = head_row.astype(F32) * (gate_two * (1.0 + pre_two * (1.0 - gate_two)))
        scale_two[pl.ds(at, rows), :] = two
        back = mm_nt(two.astype(BF16), w_two_v[...])
        scale_one[pl.ds(at, rows), :] = back * (gate_one * (1.0 + pre_one * (1.0 - gate_one)))
        deep = mm_nt(head_rows, hid_two)
        for q in range(rows // 128):
            deep_v[pl.ds(i * (rows // 128) + q, 1), :] = deep[0:1, q * 128:(q + 1) * 128]
        dense_t[:, pl.ds(at, rows)] = dense.T
        hid_one_t[:, pl.ds(at, rows)] = hid_one.T

    @pl.loop(0, NP)
    def _(p):
        at = pl.multiple_of(p * 128, 128)
        low = lax.bitwise_and(example_v[p], 127)
        hot = (lax.broadcasted_iota(jnp.int32, (128, 128), 0) == low).astype(F32)
        low_hot[:, pl.ds(at, 128)] = hot.astype(BF16)
        slot_hot[pl.ds(at, 128), :] = hot.T.astype(BF16)

    def merged(ref, p):
        return jnp.where(first_half, ref[2 * p], ref[2 * p + 1])

    def flipped(row):
        return pltpu.roll(jnp.broadcast_to(row, (8, 128)), CAP, axis=1)[0:1]

    def logits_of(places):
        spots = [b * X + xs for b, xs in places]
        four = jnp.concatenate([got_values[pl.ds(2 * q, 2)].reshape(2 * CAP, W) for q in spots], axis=0)
        score = mm_nt(weight_pair[...], jnp.concatenate([four, four], axis=1))
        for i, q in enumerate(spots):
            hit = lax.broadcasted_iota(jnp.int32, (BD, 128), 0) == merged(got_index, q)
            row = jnp.sum(jnp.where(hit, score[:, i * 128:(i + 1) * 128], 0.0), axis=0, keepdims=True)
            logit_send[0, q] = row
            logit_send[1, q] = flipped(row)

    own_value.wait()
    wait_for(got_index.at[pl.ds(0, 3)], index_sem.at[0])
    wait_for(got_values.at[pl.ds(0, 3)], value_sem.at[0])
    b_next, x_next = chip_from(1)
    logits_of([(blk, x), (b_next, x_next)])
    send(logit_send.at[1, chip], logit_got.at[me], 2, logit_sem, (blk, x * 2 + other))
    for c, turn in ((0, core), (1, other)):
        send(logit_send.at[turn, b_next * X + x_next], logit_got.at[me], 2, logit_sem, (b_next, x_next * 2 + c))
    logit_got[me] = logit_send[0, chip]

    @pl.loop(1, NC // 2)
    def _(u):
        wait_for(got_index.at[pl.ds(0, 4)], index_sem.at[u])
        wait_for(got_values.at[pl.ds(0, 4)], value_sem.at[u])
        places = [chip_from(2 * u), chip_from(2 * u + 1)]
        logits_of(places)
        for b_to, x_to in places:
            for c, turn in ((0, core), (1, other)):
                send(logit_send.at[turn, b_to * X + x_to], logit_got.at[me], 2, logit_sem, (b_to, x_to * 2 + c))

    wait_for(logit_got.at[pl.ds(0, ND - 1)], logit_sem)
    eight = lax.broadcasted_iota(jnp.int32, (NH, 128), 0)
    for p in range(NP):
        mine = eight == lax.shift_right_logical(example_v[p], 7)
        term = jnp.where(mine, merged(logit_got, p), 0.0)
        top = term.astype(BF16).astype(F32)
        spread[:, p * 128:(p + 1) * 128] = jnp.concatenate([top, term - top], axis=0).astype(BF16)
    wide = mm(spread[...], slot_hot[...])
    prob = jax.nn.sigmoid(wide[:NH] + wide[NH:] + deep_v[...])
    prob_o[...] = prob
    residual = prob - labels_v[...].astype(F32)
    dlogit = residual.astype(BF16).astype(F32)

    upright = jnp.concatenate([dlogit, jnp.zeros((128 - NH, 128), F32)], axis=0).T
    for q in range(NH):
        span = slice(q * 128, (q + 1) * 128)
        column = upright[:, q:q + 1]
        d_two_v[span, :] = (scale_two[span, :] * column).astype(BF16)
        d_one_v[span, :] = (scale_one[span, :] * column).astype(BF16)

    half_one, half_two = DIN // 2, H1 // 2
    quarter = DIN // 4
    rep_other = x * 2 + other
    ca = c1 // 2

    def cut(q, height, across):
        return slice(q // across * height, (q // across + 1) * height), slice(q % across * 128, (q % across + 1) * 128)

    def grad_one(which, piece):
        return mm(dense_t[pl.ds(pl.multiple_of(which * half_one + piece * quarter, quarter), quarter), :], d_one_v[...])

    def grad_two(which):
        return mm(hid_one_t[pl.ds(pl.multiple_of(which * half_two, half_two), half_two), :], d_two_v[...])

    one = grad_one(other, 0)
    for q in range(NC):
        part_a[q] = one[cut(q, ca, j1)].astype(BF16)
    send(part_a, pair_a, 3, pair_sem.at[0], (blk, rep_other))
    one = grad_one(other, 1)
    two = grad_two(other)
    for q in range(NC):
        part_b[q, 0:ca, :] = one[cut(q, ca, j1)].astype(BF16)
        part_b[q, ca:ca + c2, :] = two[cut(q, c2, j2)].astype(BF16)
    send(part_b, pair_b, 10, pair_sem.at[1], (blk, rep_other))

    own_one[...] = grad_one(core, 0)
    wait_for(pair_a, pair_sem.at[0])
    for q in range(NC):
        sum_a[q] = (own_one[cut(q, ca, j1)] + pair_a[q].astype(F32)).astype(BF16)
    for m in range(1, NC):
        b_to, x_to = chip_at(m)
        send(sum_a.at[b_to * X + x_to], got_a.at[chip], 4, rs_sem.at[0], (b_to, x_to * 2 + core))
    own_a = pltpu.make_async_copy(sum_a.at[chip], got_a.at[chip], own_sem.at[1])
    own_a.start()

    own_one[...] = grad_one(core, 1)
    own_two[...] = grad_two(core)
    wait_for(pair_b, pair_sem.at[1])
    for q in range(NC):
        sum_b[q, 0:ca, :] = (own_one[cut(q, ca, j1)] + pair_b[q, 0:ca, :].astype(F32)).astype(BF16)
        sum_b[q, ca:ca + c2, :] = (own_two[cut(q, c2, j2)] + pair_b[q, ca:ca + c2, :].astype(F32)).astype(BF16)
    for m in range(1, NC):
        b_to, x_to = chip_at(m)
        send(sum_b.at[b_to * X + x_to], got_b.at[chip], 11, rs_sem.at[1], (b_to, x_to * 2 + core))
    own_b = pltpu.make_async_copy(sum_b.at[chip], got_b.at[chip], own_sem.at[2])
    own_b.start()

    table = jnp.concatenate([dlogit, jnp.zeros_like(dlogit)], axis=0).astype(BF16)
    picked[...] = mm(table, low_hot[...])
    for p in range(NP):
        mine = eight == lax.shift_right_logical(example_v[p], 7)
        row = jnp.sum(jnp.where(mine, picked[0:NH, p * 128:(p + 1) * 128], 0.0), axis=0, keepdims=True)
        res_send[0, p] = row
        res_send[1, p] = flipped(row)
    for m in range(NC):
        b_to, x_to = chip_at(m)
        q = b_to * X + x_to
        if m == 0:
            send(res_send.at[1, q], res_got.at[me], 5, res_sem, (b_to, x_to * 2 + other))
        else:
            for c, turn in ((0, core), (1, other)):
                send(res_send.at[turn, q], res_got.at[me], 5, res_sem, (b_to, x_to * 2 + c))
    res_got[me] = res_send[0, chip]

    grad_head = jnp.zeros((8, H2), F32)
    for q in range(NH):
        grad_head += mm(jnp.broadcast_to(dlogit[q:q + 1, :], (8, 128)).astype(BF16), hid_two_v[q * 128:(q + 1) * 128, :])
    ones = jnp.ones((8, E), BF16)
    bias_one = mm(ones, d_one_v[...])
    bias_two = mm(ones, d_two_v[...])
    small_v[...] = jnp.zeros_like(small_v)
    for q in range(j1):
        small_v[q:q + 1, :] = bias_one[0:1, q * 128:(q + 1) * 128]
    for q in range(j2):
        small_v[j1 + q:j1 + q + 1, :] = bias_two[0:1, q * 128:(q + 1) * 128]
        small_v[j1 + j2 + q:j1 + j2 + q + 1, :] = grad_head[0:1, q * 128:(q + 1) * 128]
    for k in range(1, R):
        send(small_v, small_rep.at[rep], 6, small_sem.at[0], (blk, lax.rem(rep + k, R)))
    small_rep[rep] = small_v[...]

    def hand_out(own, got, final, full, piece, sem_at):
        own.wait()
        wait_for(got.at[pl.ds(0, NC - 1)], rs_sem.at[piece])
        final[...] = lax.fori_loop(
            1, NC, lambda q, a: a + got[q].astype(F32), got[0].astype(F32)
        ).astype(BF16)
        for m in range(1, NC):
            b_to, x_to = chip_at(m)
            send(final, full.at[core, chip], sem_at, ag_sem.at[piece, m // 4], (b_to, x_to * 2 + core))
        send(final, full.at[core, chip], 8 + 5 * piece, fw_sem.at[piece], (blk, rep_other))
        copy = pltpu.make_async_copy(final, full.at[core, chip], own_sem.at[3 + piece])
        copy.start()
        return copy

    own_final_a = hand_out(own_a, got_a, final_a, full_a, 0, 7)
    own_final_b = hand_out(own_b, got_b, final_b, full_b, 1, 12)

    wait_for(small_rep.at[pl.ds(0, R - 1)], small_sem.at[0])
    acc = small_rep[0]
    for r in range(1, R):
        acc = acc + small_rep[r]
    small_sum[...] = acc
    for k in range(1, B):
        send(small_sum, small_blk.at[blk], 9, small_sem.at[1], (lax.rem(blk + k, B), rep))
    small_blk[blk] = acc

    wait_for(res_got.at[pl.ds(0, ND - 1)], res_sem)
    total[...] = jnp.zeros_like(total)

    @pl.loop(0, B)
    def _(g):
        for h in range(X):
            p = g * X + h
            hit = lax.broadcasted_iota(jnp.int32, (BD, 128), 0) == merged(got_index, p)
            block_hot[:, h * 128:(h + 1) * 128] = jnp.where(hit, merged(res_got, p), 0.0).astype(BF16)
        values = got_values[pl.ds(g * R, R)].reshape(R * CAP, W)
        total[...] += mm(block_hot[...], values)

    grad = total[...]
    n_old = n_v[...]
    n_new = n_old + grad * grad
    n_out_v[...] = n_new
    z_out_v[...] = z_v[...] + grad - (jnp.sqrt(n_new) - jnp.sqrt(n_old)) / 0.5 * weight_v[...]
    out_z = pltpu.make_async_copy(z_out_v, z_o, out_sem.at[0])
    out_z.start()
    out_n = pltpu.make_async_copy(n_out_v, n_o, out_sem.at[1])
    out_n.start()

    def pass_all(own, got, full, out_h, piece):
        own.wait()

        def pass_on(m):
            b_from, x_from = chip_from(m)
            q = b_from * X + x_from
            send(full.at[core, q], full.at[core, q], 8 + 5 * piece, fw_sem.at[piece], (blk, rep_other))

        wait_for(got.at[pl.ds(0, 3)], ag_sem.at[piece, 0])
        for m in range(1, 4):
            pass_on(m)

        @pl.loop(1, NC // 4)
        def _(g):
            wait_for(got.at[pl.ds(0, 4)], ag_sem.at[piece, g])
            for i in range(4):
                pass_on(4 * g + i)

        copy = pltpu.make_async_copy(full.at[core], out_h.at[core], out_sem.at[2 + piece])
        copy.start()
        return copy

    out_a = pass_all(own_final_a, got_a, full_a, grad_a_o, 0)
    out_b = pass_all(own_final_b, got_b, full_b, grad_b_o, 1)
    wait_for(small_blk.at[pl.ds(0, B - 1)], small_sem.at[1])
    acc = small_blk[0]
    for r in range(1, B):
        acc = acc + small_blk[r]
    small_o[...] = acc
    wait_for(got_a, fw_sem.at[0])
    out_c = pltpu.make_async_copy(full_a.at[other], grad_a_o.at[other], out_sem.at[4])
    out_c.start()
    wait_for(got_b, fw_sem.at[1])
    out_d = pltpu.make_async_copy(full_b.at[other], grad_b_o.at[other], out_sem.at[5])
    out_d.start()

    wait_for(got_index.at[pl.ds(0, ND - 1)], send_sem.at[0])
    wait_for(got_values.at[pl.ds(0, ND - 1)], send_sem.at[1])
    wait_for(logit_got.at[pl.ds(0, ND - 1)], send_sem.at[2])
    wait_for(part_a, send_sem.at[3])
    wait_for(got_a.at[pl.ds(0, NC - 1)], send_sem.at[4])
    wait_for(res_got.at[pl.ds(0, ND - 1)], send_sem.at[5])
    wait_for(small_rep.at[pl.ds(0, R - 1)], send_sem.at[6])
    wait_for(got_a.at[pl.ds(0, NC - 1)], send_sem.at[7])
    wait_for(got_a, send_sem.at[8])
    wait_for(part_b, send_sem.at[10])
    wait_for(got_b.at[pl.ds(0, NC - 1)], send_sem.at[11])
    wait_for(got_b.at[pl.ds(0, NC - 1)], send_sem.at[12])
    wait_for(got_b, send_sem.at[13])
    wait_for(small_blk.at[pl.ds(0, B - 1)], send_sem.at[9])
    for copy in (out_z, out_n, out_a, out_b, out_c, out_d):
        copy.wait()


def finish_kernel(
    c1, c2, grad_a_h, grad_b_h, small_h, prob_h, z_h, n_h, prob_o, z_o, n_o, g_one_o, b_one_o, g_two_o, b_two_o, head_o,
    grad_a_v, grad_b_v, z_v, n_v, one_v, two_v, in_sem, out_sem,
):
    NC = grad_a_v.shape[1]
    DIN, H1 = one_v.shape
    H2 = two_v.shape[1]
    j1, j2 = H1 // 128, H2 // 128
    ca = c1 // 2
    quarter = DIN // 4
    ins = []
    for h in range(2):
        ins.append(pltpu.make_async_copy(grad_a_h.at[h], grad_a_v.at[h], in_sem.at[2 * h]))
        ins.append(pltpu.make_async_copy(grad_b_h.at[h], grad_b_v.at[h], in_sem.at[2 * h + 1]))
    in_z = pltpu.make_async_copy(z_h, z_v, in_sem.at[4])
    in_n = pltpu.make_async_copy(n_h, n_v, in_sem.at[5])
    for copy in (*ins, in_z, in_n):
        copy.start()
    prob_o[...] = prob_h[...]
    for q in range(j1):
        b_one_o[:, q * 128:(q + 1) * 128] = small_h[q:q + 1, :]
    for q in range(j2):
        b_two_o[:, q * 128:(q + 1) * 128] = small_h[j1 + q:j1 + q + 1, :]
        head_o[:, q * 128:(q + 1) * 128] = small_h[j1 + j2 + q:j1 + j2 + q + 1, :]
    outs = []

    def out(src, dst):
        outs.append(pltpu.make_async_copy(src, dst, out_sem.at[len(outs)]))
        outs[-1].start()

    for h in range(2):
        for piece, ref in ((0, grad_a_v), (1, grad_b_v)):
            ins[2 * h + piece].wait()
            top = h * (DIN // 2) + piece * quarter
            for q in range(NC):
                r1 = top + q // j1 * ca
                one_v[r1:r1 + ca, q % j1 * 128:(q % j1 + 1) * 128] = ref[h, q, 0:ca, :].astype(F32)
                if piece == 1:
                    r2 = h * (H1 // 2) + q // j2 * c2
                    two_v[r2:r2 + c2, q % j2 * 128:(q % j2 + 1) * 128] = ref[h, q, ca:ca + c2, :].astype(F32)
            out(one_v.at[pl.ds(top, quarter)], g_one_o.at[pl.ds(top, quarter)])
            if piece == 1:
                out(two_v.at[pl.ds(h * (H1 // 2), H1 // 2)], g_two_o.at[pl.ds(h * (H1 // 2), H1 // 2)])
        if h == 0:
            in_z.wait()
            out(z_v, z_o)
            in_n.wait()
            out(n_v, n_o)
    for copy in outs:
        copy.wait()


def solution(mesh):
    B, R = mesh.shape["blk"], mesh.shape["rep"]
    ND = B * R
    NC = ND // 2

    def per_device(
        dense, labels, tile_values, tile_block, tile_example, tile_count, z_state, n_state,
        w_one, b_one, w_two, b_two, head,
    ):
        E, DIN = dense.shape
        _, CAP, W = tile_values.shape
        BD = z_state.shape[0]
        H1, H2 = w_two.shape
        NH = E // 128
        NP = ND // 2
        c1 = DIN * H1 // (128 * ND)
        c2 = H1 * H2 // (128 * ND)
        hbm = pl.BlockSpec(memory_space=pl.ANY)
        vmem = pl.BlockSpec(memory_space=pltpu.VMEM)
        I32 = jnp.int32

        def V(shape, kind=F32):
            return pltpu.VMEM(shape, kind)

        def slabs(high):
            each = V((NC, high, 128), BF16)
            return each, each, each, each, V((high, 128), BF16), V((2, NC, high, 128), BF16)

        dma = pltpu.SemaphoreType.DMA
        scratch = [
            V((E, DIN), BF16), V((NH, 128), I32), V((CAP, ND), I32), V((CAP, ND), I32), V((1, ND), I32),
            V((BD, W)), V((BD, W)), V((DIN, H1), BF16), V((1, H1)), V((H1, H2), BF16), V((1, H2)), V((H2 // 128, 128), BF16),
            V((ND, 128), I32), V((ND, 1, 128), I32), V((NP, 1, 128), I32),
            V((ND, CAP, W), BF16), V((ND, 1, 128), I32), V((BD, W)), V((BD, 2 * W), BF16),
            V((E, H2), BF16), V((DIN, E), BF16), V((H1, E), BF16), V((E, H1)), V((E, H2)),
            V((NH, 128)), V((128, ND * CAP), BF16), V((ND * CAP, 128), BF16),
            V((2, NP, 1, 128)), V((ND, 1, 128)), V((2 * NH, ND * CAP), BF16), V((2 * NH, ND * CAP)),
            V((2, NP, 1, 128)), V((ND, 1, 128)),
            V((BD, R * CAP), BF16), V((BD, W)), V((BD, W)), V((BD, W)),
            V((E, H1), BF16), V((E, H2), BF16), V((DIN // 4, H1)), V((H1 // 2, H2)),
            *slabs(c1 // 2), *slabs(c1 // 2 + c2),
            V((8, 128)), V((R, 8, 128)), V((8, 128)), V((B, 8, 128)),
            dma((12,)), dma((5,)), pltpu.SemaphoreType.REGULAR, dma((NC // 2,)), dma((NC // 2,)), dma(()), dma(()),
            dma((2,)), dma((2,)), dma((2, NC // 4)), dma((2,)), dma((2,)),
            dma((14,)), dma((6,)),
        ]
        shape = jax.ShapeDtypeStruct
        prob, z_new, n_new, grad_a, grad_b, small = pl.pallas_call(
            functools.partial(step_kernel, B, R),
            out_shape=(
                shape((NH, 128), F32), shape((BD, W), F32), shape((BD, W), F32),
                shape((2, NC, c1 // 2, 128), BF16), shape((2, NC, c1 // 2 + c2, 128), BF16), shape((8, 128), F32),
            ),
            in_specs=[hbm] * 13,
            out_specs=(vmem, hbm, hbm, hbm, hbm, vmem),
            scratch_shapes=scratch,
            compiler_params=pltpu.CompilerParams(
                collective_id=0, has_side_effects=True, vmem_limit_bytes=60 * 1024 * 1024
            ),
        )(
            dense, labels.reshape(NH, 128), tile_values, tile_block.T, tile_example.T, tile_count.reshape(1, ND),
            z_state, n_state, w_one, b_one.reshape(1, H1), w_two, b_two.reshape(1, H2), head.reshape(H2 // 128, 128),
        )
        prob, z_new, n_new, g_one, g_b_one, g_two, g_b_two, g_head = pl.pallas_call(
            functools.partial(finish_kernel, c1, c2),
            out_shape=(
                shape((NH, 128), F32), shape((BD, W), F32), shape((BD, W), F32), shape((DIN, H1), F32),
                shape((1, H1), F32), shape((H1, H2), F32), shape((1, H2), F32), shape((1, H2), F32),
            ),
            in_specs=[hbm, hbm, vmem, vmem, hbm, hbm],
            out_specs=(vmem, hbm, hbm, hbm, vmem, hbm, vmem, vmem),
            scratch_shapes=[
                V((2, NC, c1 // 2, 128), BF16), V((2, NC, c1 // 2 + c2, 128), BF16), V((BD, W)), V((BD, W)),
                V((DIN, H1)), V((H1, H2)), dma((6,)), dma((8,)),
            ],
            compiler_params=pltpu.CompilerParams(vmem_limit_bytes=63 * 1024 * 1024),
        )(grad_a, grad_b, small, prob, z_new, n_new)
        return (
            prob.reshape(E), z_new, n_new, g_one, g_b_one.reshape(H1), g_two, g_b_two.reshape(H2), g_head.reshape(H2),
        )

    every = ("blk", "rep")
    return jax.shard_map(
        per_device,
        mesh=mesh,
        in_specs=(
            P(every, None), P(every), P(every, None, None), P(every, None), P(every, None), P(every),
            P(every, None), P(every, None), P(), P(), P(), P(), P(),
        ),
        out_specs=(P(every), P(every, None), P(every, None), P(), P(), P(), P(), P()),
        check_vma=False,
    )
```

```python
import functools

import jax
import jax.numpy as jnp
from jax import lax
from jax.experimental import pallas as pl
from jax.experimental.pallas import tpu as pltpu
from jax.sharding import PartitionSpec as P

MESH = pl.DeviceIdType.MESH
F32 = jnp.float32
BF16 = jnp.bfloat16
NT = (((1,), (1,)), ((), ()))
STRIDE = 27


def mm(a, b):
    return jnp.dot(a, b, preferred_element_type=F32)


def mm_nt(a, b):
    return lax.dot_general(a, b, NT, preferred_element_type=F32)


def step_kernel(
    B, R,
    dense_h, labels_h, values_h, block_h, example_h, count_h, z_h, n_h,
    w_one_h, b_one_h, w_two_h, b_two_h, head_h,
    prob_o, z_o, n_o, grad_a_o, grad_b_o, small_o,
    dense_v, labels_v, block_v, example_t, count_v, z_v, n_v, w_one_v, b_one_v, w_two_v, b_two_v, head_v,
    table_v, index_send, example_v,
    got_values, got_index, weight_v, weight_pair,
    hid_two_v, dense_t, hid_one_t, scale_one, scale_two, deep_v, low_hot, slot_hot,
    logit_send, logit_got, spread, picked, res_send, res_got,
    hot_v, value_two, block_hot, total, z_out_v, n_out_v,
    d_one_v, d_two_v, own_one, own_two,
    part_a, pair_a, sum_a, got_a, final_a, full_a, part_b, pair_b, sum_b, got_b, final_b, full_b,
    small_v, small_rep, small_sum, small_blk,
    load_sem, own_sem, ready_sem, index_sem, value_sem, logit_sem, res_sem,
    pair_sem, rs_sem, ag_sem, fw_sem, small_sem,
    send_sem, out_sem,
):
    ND = B * R
    NC = ND // 2
    X = R // 2
    Z = 4 if B % 4 == 0 else B
    Y = B // Z
    E, DIN = dense_v.shape
    H1 = w_one_v.shape[1]
    H2 = w_two_v.shape[1]
    CAP, W = got_values.shape[1], got_values.shape[2]
    BD = z_v.shape[0]
    NH = E // 128
    NP = ND // 2
    c1 = DIN * H1 // (128 * ND)
    c2 = H1 * H2 // (128 * ND)
    j1 = H1 // 128
    j2 = H2 // 128
    blk = lax.axis_index("blk")
    rep = lax.axis_index("rep")
    y, zz = lax.div(blk, Z), lax.rem(blk, Z)
    x, core = lax.div(rep, 2), lax.rem(rep, 2)
    other = 1 - core
    me = blk * R + rep
    chip = blk * X + x
    y_at = [lax.rem(y + i, Y) * Z for i in range(Y)]
    z_at = [lax.rem(zz + i, Z) for i in range(Z)]
    x_at = [lax.rem(x + i, X) for i in range(X)]

    def chip_at(m):
        spot = (m * STRIDE) % NC
        dy, dz, dx = spot // (Z * X), spot // X % Z, spot % X
        return y_at[dy] + z_at[dz], x_at[dx]

    def chip_from(m):
        spot = lax.rem(m * STRIDE, NC)
        dy, dz, dx = lax.div(spot, Z * X), lax.rem(lax.div(spot, X), Z), lax.rem(spot, X)
        return lax.rem(y + Y - dy, Y) * Z + lax.rem(zz + Z - dz, Z), lax.rem(x + X - dx, X)

    loads = [
        (block_h, block_v), (count_h, count_v), (example_h, example_t), (z_h, z_v), (n_h, n_v), (dense_h, dense_v),
        (w_one_h, w_one_v), (b_one_h, b_one_v), (w_two_h, w_two_v), (b_two_h, b_two_v), (head_h, head_v),
        (labels_h, labels_v),
    ]
    copies = [pltpu.make_async_copy(s, d, load_sem.at[i]) for i, (s, d) in enumerate(loads)]
    for copy in copies:
        copy.start()

    def send(src, dst, sem_at, recv, where):
        pltpu.make_async_remote_copy(
            src_ref=src, dst_ref=dst, send_sem=send_sem.at[sem_at], recv_sem=recv,
            device_id=where, device_id_type=MESH,
        ).start()

    def wait_for(ref, sem):
        pltpu.make_async_copy(ref, ref, sem).wait()

    barrier = pltpu.get_barrier_semaphore()
    for k in range(1, B):
        pl.semaphore_signal(barrier, inc=1, device_id=(lax.rem(blk + k, B), rep), device_id_type=MESH)
    for k in range(1, R):
        pl.semaphore_signal(barrier, inc=1, device_id=(blk, lax.rem(rep + k, R)), device_id_type=MESH)
    own_value = pltpu.make_async_copy(values_h.at[me], got_values.at[me], own_sem.at[0])
    own_value.start()

    first_half = lax.broadcasted_iota(jnp.int32, (1, 128), 1) < CAP
    copies[0].wait()
    copies[1].wait()
    live = lax.broadcasted_iota(jnp.int32, (CAP, ND), 0) < count_v[...]
    named = jnp.where(live, block_v[...], -1).astype(F32)
    table_v[...] = jnp.concatenate([named, named], axis=0).T.astype(jnp.int32)
    for o in range(ND):
        index_send[o] = table_v[o:o + 1, :]

    pl.semaphore_wait(barrier, B + R - 2)
    for k in range(1, R):
        pl.semaphore_signal(ready_sem, inc=1, device_id=(blk, lax.rem(rep + k, R)), device_id_type=MESH)

    def give(m, c):
        blk_to, x_to = chip_at(m)
        rep_to = x_to * 2 + c
        to = blk_to * R + rep_to
        send(index_send.at[to], got_index.at[me], 0, index_sem.at[m // 2], (blk_to, rep_to))
        send(values_h.at[to], got_values.at[me], 1, value_sem.at[m // 2], (blk_to, rep_to))

    give(0, other)
    for m in range(1, NC):
        spot = (m * STRIDE) % NC
        if spot < X:
            give(m, 0)
            give(m, 1)
        elif spot % X == 0:
            give(m, core)
    copies[2].wait()
    named = example_t[...].astype(F32)
    table_v[...] = jnp.concatenate([named, named], axis=0).T.astype(jnp.int32)
    for p in range(NP):
        example_v[p] = jnp.where(first_half, table_v[2 * p:2 * p + 1, :], table_v[2 * p + 1:2 * p + 2, :])
    pl.semaphore_wait(ready_sem, R - 1)

    for m in range(1, NC):
        spot = (m * STRIDE) % NC
        if spot >= X and spot % X == 0:
            give(m, other)
        elif spot >= X:
            give(m, 0)
            give(m, 1)
    got_index[me] = index_send[me]

    copies[3].wait()
    copies[4].wait()
    z = z_v[...]
    shrunk = z - jnp.where(z > 0, 0.5, -0.5)
    weight = jnp.where(jnp.abs(z) > 0.5, -shrunk / ((1.0 + jnp.sqrt(n_v[...])) / 0.5 + 0.1), 0.0)
    weight_v[...] = weight
    high = weight.astype(BF16)
    weight_pair[:, :W] = high
    weight_pair[:, W:] = (weight - high.astype(F32)).astype(BF16)

    for copy in copies[5:]:
        copy.wait()
    rows = 256
    head_row = jnp.concatenate([head_v[q:q + 1, :] for q in range(j2)], axis=1)
    head_rows = jnp.broadcast_to(head_row, (8, H2))

    @pl.loop(0, E // rows)
    def _(i):
        at = pl.multiple_of(i * rows, rows)
        dense = dense_v[pl.ds(at, rows), :]
        pre_one = mm(dense, w_one_v[...]) + b_one_v[...]
        gate_one = jax.nn.sigmoid(pre_one)
        hid_one = (pre_one * gate_one).astype(BF16)
        pre_two = mm(hid_one, w_two_v[...]) + b_two_v[...]
        gate_two = jax.nn.sigmoid(pre_two)
        hid_two = (pre_two * gate_two).astype(BF16)
        hid_two_v[pl.ds(at, rows), :] = hid_two
        two = head_row.astype(F32) * (gate_two * (1.0 + pre_two * (1.0 - gate_two)))
        scale_two[pl.ds(at, rows), :] = two
        back = mm_nt(two.astype(BF16), w_two_v[...])
        scale_one[pl.ds(at, rows), :] = back * (gate_one * (1.0 + pre_one * (1.0 - gate_one)))
        deep = mm_nt(head_rows, hid_two)
        for q in range(rows // 128):
            deep_v[pl.ds(i * (rows // 128) + q, 1), :] = deep[0:1, q * 128:(q + 1) * 128]
        dense_t[:, pl.ds(at, rows)] = dense.T
        hid_one_t[:, pl.ds(at, rows)] = hid_one.T

    @pl.loop(0, NP)
    def _(p):
        at = pl.multiple_of(p * 128, 128)
        low = lax.bitwise_and(example_v[p], 127)
        hot = (lax.broadcasted_iota(jnp.int32, (128, 128), 0) == low).astype(F32)
        low_hot[:, pl.ds(at, 128)] = hot.astype(BF16)
        slot_hot[pl.ds(at, 128), :] = hot.T.astype(BF16)

    def merged(ref, p):
        return jnp.where(first_half, ref[2 * p], ref[2 * p + 1])

    def flipped(row):
        return pltpu.roll(jnp.broadcast_to(row, (8, 128)), CAP, axis=1)[0:1]

    def logits_of(places):
        spots = [b * X + xs for b, xs in places]
        four = jnp.concatenate([got_values[pl.ds(2 * q, 2)].reshape(2 * CAP, W) for q in spots], axis=0)
        score = mm_nt(weight_pair[...], jnp.concatenate([four, four], axis=1))
        for i, q in enumerate(spots):
            hit = lax.broadcasted_iota(jnp.int32, (BD, 128), 0) == merged(got_index, q)
            row = jnp.sum(jnp.where(hit, score[:, i * 128:(i + 1) * 128], 0.0), axis=0, keepdims=True)
            logit_send[0, q] = row
            logit_send[1, q] = flipped(row)

    own_value.wait()
    wait_for(got_index.at[pl.ds(0, 3)], index_sem.at[0])
    wait_for(got_values.at[pl.ds(0, 3)], value_sem.at[0])
    b_next, x_next = chip_from(1)
    logits_of([(blk, x), (b_next, x_next)])
    send(logit_send.at[1, chip], logit_got.at[me], 2, logit_sem, (blk, x * 2 + other))
    for c, turn in ((0, core), (1, other)):
        send(logit_send.at[turn, b_next * X + x_next], logit_got.at[me], 2, logit_sem, (b_next, x_next * 2 + c))
    logit_got[me] = logit_send[0, chip]

    @pl.loop(1, NC // 2)
    def _(u):
        wait_for(got_index.at[pl.ds(0, 4)], index_sem.at[u])
        wait_for(got_values.at[pl.ds(0, 4)], value_sem.at[u])
        places = [chip_from(2 * u), chip_from(2 * u + 1)]
        logits_of(places)
        for b_to, x_to in places:
            for c, turn in ((0, core), (1, other)):
                send(logit_send.at[turn, b_to * X + x_to], logit_got.at[me], 2, logit_sem, (b_to, x_to * 2 + c))

    half_table = BD // 2

    @pl.loop(0, NP)
    def _(p):
        name = merged(got_index, p)
        low = jnp.where(name < 0, -1, lax.bitwise_and(name, half_table - 1))
        hot_v[p] = (lax.broadcasted_iota(jnp.int32, (half_table, 128), 0) == low).astype(F32).astype(BF16)

    wait_for(logit_got.at[pl.ds(0, ND - 1)], logit_sem)
    eight = lax.broadcasted_iota(jnp.int32, (NH, 128), 0)
    for p in range(NP):
        mine = eight == lax.shift_right_logical(example_v[p], 7)
        term = jnp.where(mine, merged(logit_got, p), 0.0)
        top = term.astype(BF16).astype(F32)
        spread[:, p * 128:(p + 1) * 128] = jnp.concatenate([top, term - top], axis=0).astype(BF16)
    wide = mm(spread[...], slot_hot[...])
    prob = jax.nn.sigmoid(wide[:NH] + wide[NH:] + deep_v[...])
    prob_o[...] = prob
    residual = prob - labels_v[...].astype(F32)
    dlogit = residual.astype(BF16).astype(F32)

    upright = jnp.concatenate([dlogit, jnp.zeros((128 - NH, 128), F32)], axis=0).T
    for q in range(NH):
        span = slice(q * 128, (q + 1) * 128)
        column = upright[:, q:q + 1]
        d_two_v[span, :] = (scale_two[span, :] * column).astype(BF16)
        d_one_v[span, :] = (scale_one[span, :] * column).astype(BF16)

    half_one, half_two = DIN // 2, H1 // 2
    quarter = DIN // 4
    rep_other = x * 2 + other
    ca = c1 // 2

    def cut(q, height, across):
        return slice(q // across * height, (q // across + 1) * height), slice(q % across * 128, (q % across + 1) * 128)

    def grad_one(which, piece):
        return mm(dense_t[pl.ds(pl.multiple_of(which * half_one + piece * quarter, quarter), quarter), :], d_one_v[...])

    def grad_two(which):
        return mm(hid_one_t[pl.ds(pl.multiple_of(which * half_two, half_two), half_two), :], d_two_v[...])

    one = grad_one(other, 0)
    for q in range(NC):
        part_a[q] = one[cut(q, ca, j1)].astype(BF16)
    send(part_a, pair_a, 3, pair_sem.at[0], (blk, rep_other))
    one = grad_one(other, 1)
    two = grad_two(other)
    for q in range(NC):
        part_b[q, 0:ca, :] = one[cut(q, ca, j1)].astype(BF16)
        part_b[q, ca:ca + c2, :] = two[cut(q, c2, j2)].astype(BF16)
    send(part_b, pair_b, 10, pair_sem.at[1], (blk, rep_other))

    own_one[...] = grad_one(core, 0)
    wait_for(pair_a, pair_sem.at[0])
    for q in range(NC):
        sum_a[q] = (own_one[cut(q, ca, j1)] + pair_a[q].astype(F32)).astype(BF16)
    for m in range(1, NC):
        b_to, x_to = chip_at(m)
        send(sum_a.at[b_to * X + x_to], got_a.at[chip], 4, rs_sem.at[0], (b_to, x_to * 2 + core))
    own_a = pltpu.make_async_copy(sum_a.at[chip], got_a.at[chip], own_sem.at[1])
    own_a.start()

    own_one[...] = grad_one(core, 1)
    own_two[...] = grad_two(core)
    wait_for(pair_b, pair_sem.at[1])
    for q in range(NC):
        sum_b[q, 0:ca, :] = (own_one[cut(q, ca, j1)] + pair_b[q, 0:ca, :].astype(F32)).astype(BF16)
        sum_b[q, ca:ca + c2, :] = (own_two[cut(q, c2, j2)] + pair_b[q, ca:ca + c2, :].astype(F32)).astype(BF16)
    for m in range(1, NC):
        b_to, x_to = chip_at(m)
        send(sum_b.at[b_to * X + x_to], got_b.at[chip], 11, rs_sem.at[1], (b_to, x_to * 2 + core))
    own_b = pltpu.make_async_copy(sum_b.at[chip], got_b.at[chip], own_sem.at[2])
    own_b.start()

    table = jnp.concatenate([dlogit, jnp.zeros_like(dlogit)], axis=0).astype(BF16)
    picked[...] = mm(table, low_hot[...])
    for p in range(NP):
        mine = eight == lax.shift_right_logical(example_v[p], 7)
        row = jnp.sum(jnp.where(mine, picked[0:NH, p * 128:(p + 1) * 128], 0.0), axis=0, keepdims=True)
        res_send[0, p] = row
        res_send[1, p] = flipped(row)
    for m in range(NC):
        b_to, x_to = chip_at(m)
        q = b_to * X + x_to
        if m == 0:
            send(res_send.at[1, q], res_got.at[me], 5, res_sem, (b_to, x_to * 2 + other))
        else:
            for c, turn in ((0, core), (1, other)):
                send(res_send.at[turn, q], res_got.at[me], 5, res_sem, (b_to, x_to * 2 + c))
    res_got[me] = res_send[0, chip]

    grad_head = jnp.zeros((8, H2), F32)
    for q in range(NH):
        grad_head += mm(jnp.broadcast_to(dlogit[q:q + 1, :], (8, 128)).astype(BF16), hid_two_v[q * 128:(q + 1) * 128, :])
    ones = jnp.ones((8, E), BF16)
    bias_one = mm(ones, d_one_v[...])
    bias_two = mm(ones, d_two_v[...])
    small_v[...] = jnp.zeros_like(small_v)
    for q in range(j1):
        small_v[q:q + 1, :] = bias_one[0:1, q * 128:(q + 1) * 128]
    for q in range(j2):
        small_v[j1 + q:j1 + q + 1, :] = bias_two[0:1, q * 128:(q + 1) * 128]
        small_v[j1 + j2 + q:j1 + j2 + q + 1, :] = grad_head[0:1, q * 128:(q + 1) * 128]
    for k in range(1, R):
        send(small_v, small_rep.at[rep], 6, small_sem.at[0], (blk, lax.rem(rep + k, R)))
    small_rep[rep] = small_v[...]

    @pl.loop(0, NP)
    def _(p):
        upper = jnp.broadcast_to((merged(got_index, p) >= half_table).astype(F32), (128, 128)).T
        values = got_values[pl.ds(2 * p, 2)].reshape(2 * CAP, W).astype(F32)
        above = values * upper
        at = pl.multiple_of(p * 128, 128)
        value_two[pl.ds(at, 128), :] = jnp.concatenate([values - above, above], axis=1).astype(BF16)

    def hand_out(own, got, final, full, out_h, piece, sem_at):
        own.wait()
        wait_for(got.at[pl.ds(0, NC - 1)], rs_sem.at[piece])
        final[...] = lax.fori_loop(
            1, NC, lambda q, a: a + got[q].astype(F32), got[0].astype(F32)
        ).astype(BF16)
        for m in range(1, NC):
            b_to, x_to = chip_at(m)
            send(final, full.at[chip], sem_at, ag_sem.at[piece, m // 4], (b_to, x_to * 2 + core))
        send(final, out_h.at[core, chip], 8 + 5 * piece, fw_sem.at[piece], (blk, rep_other))
        copy = pltpu.make_async_copy(final, full.at[chip], own_sem.at[3 + piece])
        copy.start()
        return copy

    own_final_a = hand_out(own_a, got_a, final_a, full_a, grad_a_o, 0, 7)
    own_final_b = hand_out(own_b, got_b, final_b, full_b, grad_b_o, 1, 12)

    wait_for(small_rep.at[pl.ds(0, R - 1)], small_sem.at[0])
    acc = small_rep[0]
    for r in range(1, R):
        acc = acc + small_rep[r]
    small_sum[...] = acc
    for k in range(1, B):
        send(small_sum, small_blk.at[blk], 9, small_sem.at[1], (lax.rem(blk + k, B), rep))
    small_blk[blk] = acc

    wait_for(res_got.at[pl.ds(0, ND - 1)], res_sem)
    total[...] = jnp.zeros_like(total)

    @pl.loop(0, NP // 8)
    def _(g):
        for h in range(8):
            p = g * 8 + h
            block_hot[:, h * 128:(h + 1) * 128] = hot_v[p] * merged(res_got, p).astype(BF16)
        total[...] += mm(block_hot[...], value_two[pl.ds(pl.multiple_of(g * 1024, 1024), 1024), :])

    for h in range(2):
        span = slice(h * half_table, (h + 1) * half_table)
        grad = total[:, h * W:(h + 1) * W]
        n_old = n_v[span, :]
        n_new = n_old + grad * grad
        n_out_v[span, :] = n_new
        z_out_v[span, :] = z_v[span, :] + grad - (jnp.sqrt(n_new) - jnp.sqrt(n_old)) / 0.5 * weight_v[span, :]
    out_z = pltpu.make_async_copy(z_out_v, z_o, out_sem.at[0])
    out_z.start()
    out_n = pltpu.make_async_copy(n_out_v, n_o, out_sem.at[1])
    out_n.start()

    def pass_all(own, got, full, out_h, piece):
        own.wait()

        def pass_on(m):
            b_from, x_from = chip_from(m)
            q = b_from * X + x_from
            send(full.at[q], out_h.at[core, q], 8 + 5 * piece, fw_sem.at[piece], (blk, rep_other))

        wait_for(got.at[pl.ds(0, 3)], ag_sem.at[piece, 0])
        for m in range(1, 4):
            pass_on(m)

        @pl.loop(1, NC // 4)
        def _(g):
            wait_for(got.at[pl.ds(0, 4)], ag_sem.at[piece, g])
            for i in range(4):
                pass_on(4 * g + i)

        copy = pltpu.make_async_copy(full, out_h.at[core], out_sem.at[2 + piece])
        copy.start()
        return copy

    out_a = pass_all(own_final_a, got_a, full_a, grad_a_o, 0)
    out_b = pass_all(own_final_b, got_b, full_b, grad_b_o, 1)
    wait_for(small_blk.at[pl.ds(0, B - 1)], small_sem.at[1])
    acc = small_blk[0]
    for r in range(1, B):
        acc = acc + small_blk[r]
    small_o[...] = acc
    wait_for(got_a, fw_sem.at[0])
    wait_for(got_b, fw_sem.at[1])

    wait_for(got_index.at[pl.ds(0, ND - 1)], send_sem.at[0])
    wait_for(got_values.at[pl.ds(0, ND - 1)], send_sem.at[1])
    wait_for(logit_got.at[pl.ds(0, ND - 1)], send_sem.at[2])
    wait_for(part_a, send_sem.at[3])
    wait_for(got_a.at[pl.ds(0, NC - 1)], send_sem.at[4])
    wait_for(res_got.at[pl.ds(0, ND - 1)], send_sem.at[5])
    wait_for(small_rep.at[pl.ds(0, R - 1)], send_sem.at[6])
    wait_for(got_a.at[pl.ds(0, NC - 1)], send_sem.at[7])
    wait_for(got_a, send_sem.at[8])
    wait_for(part_b, send_sem.at[10])
    wait_for(got_b.at[pl.ds(0, NC - 1)], send_sem.at[11])
    wait_for(got_b.at[pl.ds(0, NC - 1)], send_sem.at[12])
    wait_for(got_b, send_sem.at[13])
    wait_for(small_blk.at[pl.ds(0, B - 1)], send_sem.at[9])
    for copy in (out_z, out_n, out_a, out_b):
        copy.wait()


def finish_kernel(
    c1, c2, grad_a_h, grad_b_h, small_h, prob_h, z_h, n_h, prob_o, z_o, n_o, g_one_o, b_one_o, g_two_o, b_two_o, head_o,
    grad_a_v, grad_b_v, z_v, n_v, one_v, two_v, in_sem, out_sem,
):
    NC = grad_a_v.shape[1]
    DIN, H1 = one_v.shape
    H2 = two_v.shape[1]
    j1, j2 = H1 // 128, H2 // 128
    ca = c1 // 2
    quarter = DIN // 4
    ins = []
    for h in range(2):
        ins.append(pltpu.make_async_copy(grad_a_h.at[h], grad_a_v.at[h], in_sem.at[2 * h]))
        ins.append(pltpu.make_async_copy(grad_b_h.at[h], grad_b_v.at[h], in_sem.at[2 * h + 1]))
    in_z = pltpu.make_async_copy(z_h, z_v, in_sem.at[4])
    in_n = pltpu.make_async_copy(n_h, n_v, in_sem.at[5])
    for copy in (*ins, in_z, in_n):
        copy.start()
    prob_o[...] = prob_h[...]
    for q in range(j1):
        b_one_o[:, q * 128:(q + 1) * 128] = small_h[q:q + 1, :]
    for q in range(j2):
        b_two_o[:, q * 128:(q + 1) * 128] = small_h[j1 + q:j1 + q + 1, :]
        head_o[:, q * 128:(q + 1) * 128] = small_h[j1 + j2 + q:j1 + j2 + q + 1, :]
    outs = []

    def out(src, dst):
        outs.append(pltpu.make_async_copy(src, dst, out_sem.at[len(outs)]))
        outs[-1].start()

    for h in range(2):
        for piece, ref in ((0, grad_a_v), (1, grad_b_v)):
            ins[2 * h + piece].wait()
            top = h * (DIN // 2) + piece * quarter
            for q in range(NC):
                r1 = top + q // j1 * ca
                one_v[r1:r1 + ca, q % j1 * 128:(q % j1 + 1) * 128] = ref[h, q, 0:ca, :].astype(F32)
                if piece == 1:
                    r2 = h * (H1 // 2) + q // j2 * c2
                    two_v[r2:r2 + c2, q % j2 * 128:(q % j2 + 1) * 128] = ref[h, q, ca:ca + c2, :].astype(F32)
            out(one_v.at[pl.ds(top, quarter)], g_one_o.at[pl.ds(top, quarter)])
            if piece == 1:
                out(two_v.at[pl.ds(h * (H1 // 2), H1 // 2)], g_two_o.at[pl.ds(h * (H1 // 2), H1 // 2)])
        if h == 0:
            in_z.wait()
            out(z_v, z_o)
            in_n.wait()
            out(n_v, n_o)
    for copy in outs:
        copy.wait()


def solution(mesh):
    B, R = mesh.shape["blk"], mesh.shape["rep"]
    ND = B * R
    NC = ND // 2

    def per_device(
        dense, labels, tile_values, tile_block, tile_example, tile_count, z_state, n_state,
        w_one, b_one, w_two, b_two, head,
    ):
        E, DIN = dense.shape
        _, CAP, W = tile_values.shape
        BD = z_state.shape[0]
        H1, H2 = w_two.shape
        NH = E // 128
        NP = ND // 2
        c1 = DIN * H1 // (128 * ND)
        c2 = H1 * H2 // (128 * ND)
        hbm = pl.BlockSpec(memory_space=pl.ANY)
        vmem = pl.BlockSpec(memory_space=pltpu.VMEM)
        I32 = jnp.int32

        def V(shape, kind=F32):
            return pltpu.VMEM(shape, kind)

        def slabs(high):
            each = V((NC, high, 128), BF16)
            return each, each, each, each, V((high, 128), BF16), each

        dma = pltpu.SemaphoreType.DMA
        scratch = [
            V((E, DIN), BF16), V((NH, 128), I32), V((CAP, ND), I32), V((CAP, ND), I32), V((1, ND), I32),
            V((BD, W)), V((BD, W)), V((DIN, H1), BF16), V((1, H1)), V((H1, H2), BF16), V((1, H2)), V((H2 // 128, 128), BF16),
            V((ND, 128), I32), V((ND, 1, 128), I32), V((NP, 1, 128), I32),
            V((ND, CAP, W), BF16), V((ND, 1, 128), I32), V((BD, W)), V((BD, 2 * W), BF16),
            V((E, H2), BF16), V((DIN, E), BF16), V((H1, E), BF16), V((E, H1)), V((E, H2)),
            V((NH, 128)), V((128, ND * CAP), BF16), V((ND * CAP, 128), BF16),
            V((2, NP, 1, 128)), V((ND, 1, 128)), V((2 * NH, ND * CAP), BF16), V((2 * NH, ND * CAP)),
            V((2, NP, 1, 128)), V((ND, 1, 128)),
            V((NP, BD // 2, 128), BF16), V((ND * CAP, 2 * W), BF16), V((BD // 2, 1024), BF16), V((BD // 2, 2 * W)), V((BD, W)), V((BD, W)),
            V((E, H1), BF16), V((E, H2), BF16), V((DIN // 4, H1)), V((H1 // 2, H2)),
            *slabs(c1 // 2), *slabs(c1 // 2 + c2),
            V((8, 128)), V((R, 8, 128)), V((8, 128)), V((B, 8, 128)),
            dma((12,)), dma((5,)), pltpu.SemaphoreType.REGULAR, dma((NC // 2,)), dma((NC // 2,)), dma(()), dma(()),
            dma((2,)), dma((2,)), dma((2, NC // 4)), dma((2,)), dma((2,)),
            dma((14,)), dma((4,)),
        ]
        shape = jax.ShapeDtypeStruct
        prob, z_new, n_new, grad_a, grad_b, small = pl.pallas_call(
            functools.partial(step_kernel, B, R),
            out_shape=(
                shape((NH, 128), F32), shape((BD, W), F32), shape((BD, W), F32),
                shape((2, NC, c1 // 2, 128), BF16), shape((2, NC, c1 // 2 + c2, 128), BF16), shape((8, 128), F32),
            ),
            in_specs=[hbm] * 13,
            out_specs=(vmem, hbm, hbm, hbm, hbm, vmem),
            scratch_shapes=scratch,
            compiler_params=pltpu.CompilerParams(
                collective_id=0, has_side_effects=True, vmem_limit_bytes=60 * 1024 * 1024
            ),
        )(
            dense, labels.reshape(NH, 128), tile_values, tile_block.T, tile_example.T, tile_count.reshape(1, ND),
            z_state, n_state, w_one, b_one.reshape(1, H1), w_two, b_two.reshape(1, H2), head.reshape(H2 // 128, 128),
        )
        prob, z_new, n_new, g_one, g_b_one, g_two, g_b_two, g_head = pl.pallas_call(
            functools.partial(finish_kernel, c1, c2),
            out_shape=(
                shape((NH, 128), F32), shape((BD, W), F32), shape((BD, W), F32), shape((DIN, H1), F32),
                shape((1, H1), F32), shape((H1, H2), F32), shape((1, H2), F32), shape((1, H2), F32),
            ),
            in_specs=[hbm, hbm, vmem, vmem, hbm, hbm],
            out_specs=(vmem, hbm, hbm, hbm, vmem, hbm, vmem, vmem),
            scratch_shapes=[
                V((2, NC, c1 // 2, 128), BF16), V((2, NC, c1 // 2 + c2, 128), BF16), V((BD, W)), V((BD, W)),
                V((DIN, H1)), V((H1, H2)), dma((6,)), dma((8,)),
            ],
            compiler_params=pltpu.CompilerParams(vmem_limit_bytes=63 * 1024 * 1024),
        )(grad_a, grad_b, small, prob, z_new, n_new)
        return (
            prob.reshape(E), z_new, n_new, g_one, g_b_one.reshape(H1), g_two, g_b_two.reshape(H2), g_head.reshape(H2),
        )

    every = ("blk", "rep")
    return jax.shard_map(
        per_device,
        mesh=mesh,
        in_specs=(
            P(every, None), P(every), P(every, None, None), P(every, None), P(every, None), P(every),
            P(every, None), P(every, None), P(), P(), P(), P(), P(),
        ),
        out_specs=(P(every), P(every, None), P(every, None), P(), P(), P(), P(), P()),
        check_vma=False,
    )
```

```python
import functools

import jax
import jax.numpy as jnp
from jax import lax
from jax.experimental import pallas as pl
from jax.experimental.pallas import tpu as pltpu
from jax.sharding import PartitionSpec as P

MESH = pl.DeviceIdType.MESH
F32 = jnp.float32
BF16 = jnp.bfloat16
NT = (((1,), (1,)), ((), ()))
STRIDE = 27


def mm(a, b):
    return jnp.dot(a, b, preferred_element_type=F32)


def mm_nt(a, b):
    return lax.dot_general(a, b, NT, preferred_element_type=F32)


def step_kernel(
    B, R,
    dense_h, labels_h, values_h, block_h, example_h, count_h, z_h, n_h,
    w_one_h, b_one_h, w_two_h, b_two_h, head_h,
    prob_o, z_o, n_o, grad_a_o, grad_b_o, small_o,
    dense_v, labels_v, block_v, example_t, count_v, z_v, n_v, w_one_v, b_one_v, w_two_v, b_two_v, head_v,
    table_v, index_send, example_v,
    got_values, got_index, weight_v, weight_pair,
    hid_two_v, dense_t, hid_one_t, scale_one, scale_two, deep_v, low_hot, slot_hot,
    logit_send, logit_got, spread, picked, res_send, res_got,
    names_v, hot_v, value_two, block_hot, total, z_out_v, n_out_v,
    d_one_v, d_two_v, own_one, own_two,
    part_a, pair_a, sum_a, got_a, final_a, full_a, part_b, pair_b, sum_b, got_b, final_b, full_b,
    small_v, small_rep, small_sum, small_blk, small_all, prob_v,
    load_sem, own_sem, ready_sem, index_sem, value_sem, logit_sem, res_sem,
    pair_sem, rs_sem, ag_sem, fw_sem, small_sem,
    send_sem, out_sem,
):
    ND = B * R
    NC = ND // 2
    X = R // 2
    Z = 4 if B % 4 == 0 else B
    Y = B // Z
    E, DIN = dense_v.shape
    H1 = w_one_v.shape[1]
    H2 = w_two_v.shape[1]
    CAP, W = got_values.shape[1], got_values.shape[2]
    BD = z_v.shape[0]
    NH = E // 128
    NP = ND // 2
    c1 = DIN * H1 // (128 * ND)
    c2 = H1 * H2 // (128 * ND)
    j1 = H1 // 128
    j2 = H2 // 128
    blk = lax.axis_index("blk")
    rep = lax.axis_index("rep")
    y, zz = lax.div(blk, Z), lax.rem(blk, Z)
    x, core = lax.div(rep, 2), lax.rem(rep, 2)
    other = 1 - core
    me = blk * R + rep
    chip = blk * X + x
    y_at = [lax.rem(y + i, Y) * Z for i in range(Y)]
    z_at = [lax.rem(zz + i, Z) for i in range(Z)]
    x_at = [lax.rem(x + i, X) for i in range(X)]

    def spread_of(spot):
        return spot // (Z * X), spot // X % Z, spot % X

    def hops(spot):
        return sum(min(d, n - d) for d, n in zip(spread_of(spot), (Y, Z, X)))

    strided = [(m * STRIDE) % NC for m in range(NC)]
    order = [q for q in strided if q < X] + sorted([q for q in strided if q >= X], key=lambda q: -hops(q))

    def chip_at(m):
        dy, dz, dx = spread_of(order[m])
        return y_at[dy] + z_at[dz], x_at[dx]

    def chip_from(m):
        dy, dz, dx = spread_of(order[m])
        return y_at[(Y - dy) % Y] + z_at[(Z - dz) % Z], x_at[(X - dx) % X]

    loads = [
        (block_h, block_v), (count_h, count_v), (example_h, example_t), (z_h, z_v), (n_h, n_v), (dense_h, dense_v),
        (w_one_h, w_one_v), (b_one_h, b_one_v), (w_two_h, w_two_v), (b_two_h, b_two_v), (head_h, head_v),
        (labels_h, labels_v),
    ]
    copies = [pltpu.make_async_copy(s, d, load_sem.at[i]) for i, (s, d) in enumerate(loads)]
    for copy in copies:
        copy.start()

    def send(src, dst, sem_at, recv, where):
        pltpu.make_async_remote_copy(
            src_ref=src, dst_ref=dst, send_sem=send_sem.at[sem_at], recv_sem=recv,
            device_id=where, device_id_type=MESH,
        ).start()

    def wait_for(ref, sem):
        pltpu.make_async_copy(ref, ref, sem).wait()

    barrier = pltpu.get_barrier_semaphore()
    for k in range(1, B):
        pl.semaphore_signal(barrier, inc=1, device_id=(lax.rem(blk + k, B), rep), device_id_type=MESH)
    for k in range(1, R):
        pl.semaphore_signal(barrier, inc=1, device_id=(blk, lax.rem(rep + k, R)), device_id_type=MESH)
    own_value = pltpu.make_async_copy(values_h.at[me], got_values.at[me], own_sem.at[0])
    own_value.start()

    first_half = lax.broadcasted_iota(jnp.int32, (1, 128), 1) < CAP
    copies[0].wait()
    copies[1].wait()
    live = lax.broadcasted_iota(jnp.int32, (CAP, ND), 0) < count_v[...]
    named = jnp.where(live, block_v[...], -1).astype(F32)
    table_v[...] = jnp.concatenate([named, named], axis=0).T.astype(jnp.int32)
    for o in range(ND):
        index_send[o] = table_v[o:o + 1, :]

    pl.semaphore_wait(barrier, B + R - 2)
    for k in range(1, R):
        pl.semaphore_signal(ready_sem, inc=1, device_id=(blk, lax.rem(rep + k, R)), device_id_type=MESH)

    def give(m, c):
        blk_to, x_to = chip_at(m)
        rep_to = x_to * 2 + c
        to = blk_to * R + rep_to
        send(index_send.at[to], got_index.at[me], 0, index_sem.at[m // 2], (blk_to, rep_to))
        send(values_h.at[to], got_values.at[me], 1, value_sem.at[m // 2], (blk_to, rep_to))

    give(0, other)
    for m in range(1, NC):
        spot = order[m]
        if spot < X:
            give(m, 0)
            give(m, 1)
        elif spot % X == 0:
            give(m, core)
    copies[2].wait()
    named = example_t[...].astype(F32)
    table_v[...] = jnp.concatenate([named, named], axis=0).T.astype(jnp.int32)
    for p in range(NP):
        example_v[p] = jnp.where(first_half, table_v[2 * p:2 * p + 1, :], table_v[2 * p + 1:2 * p + 2, :])
    pl.semaphore_wait(ready_sem, R - 1)

    for m in range(1, NC):
        spot = order[m]
        if spot >= X and spot % X == 0:
            give(m, other)
        elif spot >= X:
            give(m, 0)
            give(m, 1)
    got_index[me] = index_send[me]

    copies[3].wait()
    copies[4].wait()
    z = z_v[...]
    shrunk = z - jnp.where(z > 0, 0.5, -0.5)
    weight = jnp.where(jnp.abs(z) > 0.5, -shrunk / ((1.0 + jnp.sqrt(n_v[...])) / 0.5 + 0.1), 0.0)
    weight_v[...] = weight
    high = weight.astype(BF16)
    weight_pair[:, :W] = high
    weight_pair[:, W:] = (weight - high.astype(F32)).astype(BF16)

    for copy in copies[5:]:
        copy.wait()
    rows = 256
    head_row = jnp.concatenate([head_v[q:q + 1, :] for q in range(j2)], axis=1)
    head_rows = jnp.broadcast_to(head_row, (8, H2))

    @pl.loop(0, E // rows)
    def _(i):
        at = pl.multiple_of(i * rows, rows)
        dense = dense_v[pl.ds(at, rows), :]
        pre_one = mm(dense, w_one_v[...]) + b_one_v[...]
        gate_one = jax.nn.sigmoid(pre_one)
        hid_one = (pre_one * gate_one).astype(BF16)
        pre_two = mm(hid_one, w_two_v[...]) + b_two_v[...]
        gate_two = jax.nn.sigmoid(pre_two)
        hid_two = (pre_two * gate_two).astype(BF16)
        hid_two_v[pl.ds(at, rows), :] = hid_two
        two = head_row.astype(F32) * (gate_two * (1.0 + pre_two * (1.0 - gate_two)))
        scale_two[pl.ds(at, rows), :] = two
        back = mm_nt(two.astype(BF16), w_two_v[...])
        scale_one[pl.ds(at, rows), :] = back * (gate_one * (1.0 + pre_one * (1.0 - gate_one)))
        deep = mm_nt(head_rows, hid_two)
        for q in range(rows // 128):
            deep_v[pl.ds(i * (rows // 128) + q, 1), :] = deep[0:1, q * 128:(q + 1) * 128]
        dense_t[:, pl.ds(at, rows)] = dense.T
        hid_one_t[:, pl.ds(at, rows)] = hid_one.T

    @pl.loop(0, NP)
    def _(p):
        at = pl.multiple_of(p * 128, 128)
        low = lax.bitwise_and(example_v[p], 127)
        hot = (lax.broadcasted_iota(jnp.int32, (128, 128), 0) == low).astype(F32)
        low_hot[:, pl.ds(at, 128)] = hot.astype(BF16)
        slot_hot[pl.ds(at, 128), :] = hot.T.astype(BF16)

    def merged(ref, p):
        return jnp.where(first_half, ref[2 * p], ref[2 * p + 1])

    def flipped(row):
        return pltpu.roll(jnp.broadcast_to(row, (8, 128)), CAP, axis=1)[0:1]

    def logits_of(places):
        spots = [b * X + xs for b, xs in places]
        four = jnp.concatenate([got_values[pl.ds(2 * q, 2)].reshape(2 * CAP, W) for q in spots], axis=0)
        score = mm_nt(weight_pair[...], jnp.concatenate([four, four], axis=1))
        for i, q in enumerate(spots):
            hit = lax.broadcasted_iota(jnp.int32, (BD, 128), 0) == merged(got_index, q)
            row = jnp.sum(jnp.where(hit, score[:, i * 128:(i + 1) * 128], 0.0), axis=0, keepdims=True)
            logit_send[0, q] = row
            logit_send[1, q] = flipped(row)

    own_value.wait()
    wait_for(got_index.at[pl.ds(0, 3)], index_sem.at[0])
    wait_for(got_values.at[pl.ds(0, 3)], value_sem.at[0])
    b_next, x_next = chip_from(1)
    logits_of([(blk, x), (b_next, x_next)])
    send(logit_send.at[1, chip], logit_got.at[me], 2, logit_sem, (blk, x * 2 + other))
    for c, turn in ((0, core), (1, other)):
        send(logit_send.at[turn, b_next * X + x_next], logit_got.at[me], 2, logit_sem, (b_next, x_next * 2 + c))
    logit_got[me] = logit_send[0, chip]

    for u in range(1, NC // 2):
        wait_for(got_index.at[pl.ds(0, 4)], index_sem.at[u])
        wait_for(got_values.at[pl.ds(0, 4)], value_sem.at[u])
        places = [chip_from(2 * u), chip_from(2 * u + 1)]
        logits_of(places)
        for b_to, x_to in places:
            for c, turn in ((0, core), (1, other)):
                send(logit_send.at[turn, b_to * X + x_to], logit_got.at[me], 2, logit_sem, (b_to, x_to * 2 + c))

    half_table = BD // 2

    @pl.loop(0, NP)
    def _(p):
        name = merged(got_index, p)
        low = jnp.where(name < 0, -1, lax.bitwise_and(name, half_table - 1))
        hot_v[p] = (lax.broadcasted_iota(jnp.int32, (half_table, 128), 0) == low).astype(F32).astype(BF16)

    for p in range(NP):
        names_v[p:p + 1, :] = (merged(got_index, p) >= half_table).astype(F32)
    upper = names_v[...].T
    for p in range(NP):
        values = got_values[2 * p:2 * p + 2].reshape(2 * CAP, W).astype(F32)
        above = values * upper[:, p:p + 1]
        value_two[p * 128:(p + 1) * 128, 0:W] = (values - above).astype(BF16)
        value_two[p * 128:(p + 1) * 128, W:2 * W] = above.astype(BF16)

    wait_for(logit_got.at[pl.ds(0, ND - 1)], logit_sem)
    eight = lax.broadcasted_iota(jnp.int32, (NH, 128), 0)
    for p in range(NP):
        mine = eight == lax.shift_right_logical(example_v[p], 7)
        term = jnp.where(mine, merged(logit_got, p), 0.0)
        top = term.astype(BF16).astype(F32)
        spread[:, p * 128:(p + 1) * 128] = jnp.concatenate([top, term - top], axis=0).astype(BF16)
    wide = mm(spread[...], slot_hot[...])
    prob = jax.nn.sigmoid(wide[:NH] + wide[NH:] + deep_v[...])
    prob_v[...] = prob
    out_prob = pltpu.make_async_copy(prob_v, prob_o, out_sem.at[4])
    out_prob.start()
    residual = prob - labels_v[...].astype(F32)
    dlogit = residual.astype(BF16).astype(F32)

    upright = jnp.concatenate([dlogit, jnp.zeros((128 - NH, 128), F32)], axis=0).T
    for q in range(NH):
        span = slice(q * 128, (q + 1) * 128)
        column = upright[:, q:q + 1]
        d_two_v[span, :] = (scale_two[span, :] * column).astype(BF16)
        d_one_v[span, :] = (scale_one[span, :] * column).astype(BF16)

    half_one, half_two = DIN // 2, H1 // 2
    quarter = DIN // 4
    rep_other = x * 2 + other
    ca = c1 // 2

    def cut(q, height, across):
        return slice(q // across * height, (q // across + 1) * height), slice(q % across * 128, (q % across + 1) * 128)

    def grad_one(which, piece):
        return mm(dense_t[pl.ds(pl.multiple_of(which * half_one + piece * quarter, quarter), quarter), :], d_one_v[...])

    def grad_two(which):
        return mm(hid_one_t[pl.ds(pl.multiple_of(which * half_two, half_two), half_two), :], d_two_v[...])

    one = grad_one(other, 0)
    for q in range(NC):
        part_a[q] = one[cut(q, ca, j1)].astype(BF16)
    send(part_a, pair_a, 3, pair_sem.at[0], (blk, rep_other))
    one = grad_one(other, 1)
    two = grad_two(other)
    for q in range(NC):
        part_b[q, 0:ca, :] = one[cut(q, ca, j1)].astype(BF16)
        part_b[q, ca:ca + c2, :] = two[cut(q, c2, j2)].astype(BF16)
    send(part_b, pair_b, 10, pair_sem.at[1], (blk, rep_other))

    own_one[...] = grad_one(core, 0)
    wait_for(pair_a, pair_sem.at[0])
    for q in range(NC):
        sum_a[q] = (own_one[cut(q, ca, j1)] + pair_a[q].astype(F32)).astype(BF16)
    for m in range(1, NC):
        b_to, x_to = chip_at(m)
        send(sum_a.at[b_to * X + x_to], got_a.at[chip], 4, rs_sem.at[0], (b_to, x_to * 2 + core))
    own_a = pltpu.make_async_copy(sum_a.at[chip], got_a.at[chip], own_sem.at[1])
    own_a.start()

    own_one[...] = grad_one(core, 1)
    own_two[...] = grad_two(core)
    wait_for(pair_b, pair_sem.at[1])
    for q in range(NC):
        sum_b[q, 0:ca, :] = (own_one[cut(q, ca, j1)] + pair_b[q, 0:ca, :].astype(F32)).astype(BF16)
        sum_b[q, ca:ca + c2, :] = (own_two[cut(q, c2, j2)] + pair_b[q, ca:ca + c2, :].astype(F32)).astype(BF16)
    for m in range(1, NC):
        b_to, x_to = chip_at(m)
        send(sum_b.at[b_to * X + x_to], got_b.at[chip], 11, rs_sem.at[1], (b_to, x_to * 2 + core))
    own_b = pltpu.make_async_copy(sum_b.at[chip], got_b.at[chip], own_sem.at[2])
    own_b.start()

    table = jnp.concatenate([dlogit, jnp.zeros_like(dlogit)], axis=0).astype(BF16)
    picked[...] = mm(table, low_hot[...])
    for p in range(NP):
        mine = eight == lax.shift_right_logical(example_v[p], 7)
        row = jnp.sum(jnp.where(mine, picked[0:NH, p * 128:(p + 1) * 128], 0.0), axis=0, keepdims=True)
        res_send[0, p] = row
        res_send[1, p] = flipped(row)
    for m in range(NC):
        b_to, x_to = chip_at(m)
        q = b_to * X + x_to
        if m == 0:
            send(res_send.at[1, q], res_got.at[me], 5, res_sem, (b_to, x_to * 2 + other))
        else:
            for c, turn in ((0, core), (1, other)):
                send(res_send.at[turn, q], res_got.at[me], 5, res_sem, (b_to, x_to * 2 + c))
    res_got[me] = res_send[0, chip]

    grad_head = jnp.zeros((8, H2), F32)
    for q in range(NH):
        grad_head += mm(jnp.broadcast_to(dlogit[q:q + 1, :], (8, 128)).astype(BF16), hid_two_v[q * 128:(q + 1) * 128, :])
    ones = jnp.ones((8, E), BF16)
    bias_one = mm(ones, d_one_v[...])
    bias_two = mm(ones, d_two_v[...])
    small_v[...] = jnp.zeros_like(small_v)
    for q in range(j1):
        small_v[q:q + 1, :] = bias_one[0:1, q * 128:(q + 1) * 128]
    for q in range(j2):
        small_v[j1 + q:j1 + q + 1, :] = bias_two[0:1, q * 128:(q + 1) * 128]
        small_v[j1 + j2 + q:j1 + j2 + q + 1, :] = grad_head[0:1, q * 128:(q + 1) * 128]
    for k in range(1, R):
        send(small_v, small_rep.at[rep], 6, small_sem.at[0], (blk, lax.rem(rep + k, R)))
    small_rep[rep] = small_v[...]

    def hand_out(own, got, final, full, out_h, piece, sem_at):
        own.wait()
        wait_for(got.at[pl.ds(0, NC - 1)], rs_sem.at[piece])
        final[...] = lax.fori_loop(
            1, NC, lambda q, a: a + got[q].astype(F32), got[0].astype(F32)
        ).astype(BF16)
        for m in range(1, NC):
            b_to, x_to = chip_at(m)
            send(final, full.at[chip], sem_at, ag_sem.at[piece, m // 4], (b_to, x_to * 2 + core))
        send(final, out_h.at[core, chip], 8 + 5 * piece, fw_sem.at[piece], (blk, rep_other))
        copy = pltpu.make_async_copy(final, full.at[chip], own_sem.at[3 + piece])
        copy.start()
        return copy

    own_final_a = hand_out(own_a, got_a, final_a, full_a, grad_a_o, 0, 7)
    own_final_b = hand_out(own_b, got_b, final_b, full_b, grad_b_o, 1, 12)

    wait_for(small_rep.at[pl.ds(0, R - 1)], small_sem.at[0])
    acc = small_rep[0]
    for r in range(1, R):
        acc = acc + small_rep[r]
    small_sum[...] = acc
    for k in range(1, B):
        send(small_sum, small_blk.at[blk], 9, small_sem.at[1], (lax.rem(blk + k, B), rep))
    small_blk[blk] = acc

    wait_for(res_got.at[pl.ds(0, ND - 1)], res_sem)
    total[...] = jnp.zeros_like(total)

    @pl.loop(0, NP // 8)
    def _(g):
        for h in range(8):
            p = g * 8 + h
            block_hot[:, h * 128:(h + 1) * 128] = hot_v[p] * merged(res_got, p).astype(BF16)
        total[...] += mm(block_hot[...], value_two[pl.ds(pl.multiple_of(g * 1024, 1024), 1024), :])

    for h in range(2):
        span = slice(h * half_table, (h + 1) * half_table)
        grad = total[:, h * W:(h + 1) * W]
        n_old = n_v[span, :]
        n_new = n_old + grad * grad
        n_out_v[span, :] = n_new
        z_out_v[span, :] = z_v[span, :] + grad - (jnp.sqrt(n_new) - jnp.sqrt(n_old)) / 0.5 * weight_v[span, :]
    out_z = pltpu.make_async_copy(z_out_v, z_o, out_sem.at[0])
    out_z.start()
    out_n = pltpu.make_async_copy(n_out_v, n_o, out_sem.at[1])
    out_n.start()

    wait_for(small_blk.at[pl.ds(0, B - 1)], small_sem.at[1])
    acc = small_blk[0]
    for r in range(1, B):
        acc = acc + small_blk[r]
    small_all[...] = acc
    out_small = pltpu.make_async_copy(small_all, small_o, out_sem.at[5])
    out_small.start()

    def pass_all(own, got, full, out_h, piece):
        own.wait()

        def pass_on(m):
            b_from, x_from = chip_from(m)
            q = b_from * X + x_from
            send(full.at[q], out_h.at[core, q], 8 + 5 * piece, fw_sem.at[piece], (blk, rep_other))

        wait_for(got.at[pl.ds(0, 3)], ag_sem.at[piece, 0])
        for m in range(1, 4):
            pass_on(m)

        for g in range(1, NC // 4):
            wait_for(got.at[pl.ds(0, 4)], ag_sem.at[piece, g])
            for i in range(4):
                pass_on(4 * g + i)

        copy = pltpu.make_async_copy(full, out_h.at[core], out_sem.at[2 + piece])
        copy.start()
        return copy

    out_a = pass_all(own_final_a, got_a, full_a, grad_a_o, 0)
    out_b = pass_all(own_final_b, got_b, full_b, grad_b_o, 1)
    wait_for(got_a, fw_sem.at[0])
    wait_for(got_b, fw_sem.at[1])

    wait_for(got_index.at[pl.ds(0, ND - 1)], send_sem.at[0])
    wait_for(got_values.at[pl.ds(0, ND - 1)], send_sem.at[1])
    wait_for(logit_got.at[pl.ds(0, ND - 1)], send_sem.at[2])
    wait_for(part_a, send_sem.at[3])
    wait_for(got_a.at[pl.ds(0, NC - 1)], send_sem.at[4])
    wait_for(res_got.at[pl.ds(0, ND - 1)], send_sem.at[5])
    wait_for(small_rep.at[pl.ds(0, R - 1)], send_sem.at[6])
    wait_for(got_a.at[pl.ds(0, NC - 1)], send_sem.at[7])
    wait_for(got_a, send_sem.at[8])
    wait_for(part_b, send_sem.at[10])
    wait_for(got_b.at[pl.ds(0, NC - 1)], send_sem.at[11])
    wait_for(got_b.at[pl.ds(0, NC - 1)], send_sem.at[12])
    wait_for(got_b, send_sem.at[13])
    wait_for(small_blk.at[pl.ds(0, B - 1)], send_sem.at[9])
    for copy in (out_z, out_n, out_a, out_b, out_prob, out_small):
        copy.wait()


def finish_kernel(
    c1, c2, grad_a_h, grad_b_h, small_h, prob_h, z_h, n_h, prob_o, z_o, n_o, g_one_o, b_one_o, g_two_o, b_two_o, head_o,
    grad_a_v, grad_b_v, z_v, n_v, one_v, two_v, small_v, prob_v, b_one_v, b_two_v, head_v, in_sem, out_sem,
):
    NC = grad_a_v.shape[1]
    DIN, H1 = one_v.shape
    H2 = two_v.shape[1]
    j1, j2 = H1 // 128, H2 // 128
    ca = c1 // 2
    quarter = DIN // 4
    ins = []
    for h in range(2):
        ins.append(pltpu.make_async_copy(grad_a_h.at[h], grad_a_v.at[h], in_sem.at[2 * h]))
        ins.append(pltpu.make_async_copy(grad_b_h.at[h], grad_b_v.at[h], in_sem.at[2 * h + 1]))
    in_z = pltpu.make_async_copy(z_h, z_v, in_sem.at[4])
    in_n = pltpu.make_async_copy(n_h, n_v, in_sem.at[5])
    in_prob = pltpu.make_async_copy(prob_h, prob_v, in_sem.at[6])
    in_small = pltpu.make_async_copy(small_h, small_v, in_sem.at[7])
    for copy in (*ins, in_z, in_n, in_prob, in_small):
        copy.start()
    outs = []

    def out(src, dst):
        outs.append(pltpu.make_async_copy(src, dst, out_sem.at[len(outs)]))
        outs[-1].start()

    for h in range(2):
        for piece, ref in ((0, grad_a_v), (1, grad_b_v)):
            ins[2 * h + piece].wait()
            top = h * (DIN // 2) + piece * quarter
            for q in range(NC):
                r1 = top + q // j1 * ca
                one_v[r1:r1 + ca, q % j1 * 128:(q % j1 + 1) * 128] = ref[h, q, 0:ca, :].astype(F32)
                if piece == 1:
                    r2 = h * (H1 // 2) + q // j2 * c2
                    two_v[r2:r2 + c2, q % j2 * 128:(q % j2 + 1) * 128] = ref[h, q, ca:ca + c2, :].astype(F32)
            out(one_v.at[pl.ds(top, quarter)], g_one_o.at[pl.ds(top, quarter)])
            if piece == 1:
                out(two_v.at[pl.ds(h * (H1 // 2), H1 // 2)], g_two_o.at[pl.ds(h * (H1 // 2), H1 // 2)])
        if h == 0:
            in_z.wait()
            out(z_v, z_o)
            in_n.wait()
            out(n_v, n_o)
        if h == 0:
            in_prob.wait()
            out(prob_v, prob_o)
            in_small.wait()
            for q in range(j1):
                b_one_v[:, q * 128:(q + 1) * 128] = small_v[q:q + 1, :]
            for q in range(j2):
                b_two_v[:, q * 128:(q + 1) * 128] = small_v[j1 + q:j1 + q + 1, :]
                head_v[:, q * 128:(q + 1) * 128] = small_v[j1 + j2 + q:j1 + j2 + q + 1, :]
            out(b_one_v, b_one_o)
            out(b_two_v, b_two_o)
            out(head_v, head_o)
    for copy in outs:
        copy.wait()


def solution(mesh):
    B, R = mesh.shape["blk"], mesh.shape["rep"]
    ND = B * R
    NC = ND // 2

    def per_device(
        dense, labels, tile_values, tile_block, tile_example, tile_count, z_state, n_state,
        w_one, b_one, w_two, b_two, head,
    ):
        E, DIN = dense.shape
        _, CAP, W = tile_values.shape
        BD = z_state.shape[0]
        H1, H2 = w_two.shape
        NH = E // 128
        NP = ND // 2
        c1 = DIN * H1 // (128 * ND)
        c2 = H1 * H2 // (128 * ND)
        hbm = pl.BlockSpec(memory_space=pl.ANY)
        I32 = jnp.int32

        def V(shape, kind=F32):
            return pltpu.VMEM(shape, kind)

        def slabs(high):
            each = V((NC, high, 128), BF16)
            return each, each, each, each, V((high, 128), BF16), each

        dma = pltpu.SemaphoreType.DMA
        scratch = [
            V((E, DIN), BF16), V((NH, 128), I32), V((CAP, ND), I32), V((CAP, ND), I32), V((1, ND), I32),
            V((BD, W)), V((BD, W)), V((DIN, H1), BF16), V((1, H1)), V((H1, H2), BF16), V((1, H2)), V((H2 // 128, 128), BF16),
            V((ND, 128), I32), V((ND, 1, 128), I32), V((NP, 1, 128), I32),
            V((ND, CAP, W), BF16), V((ND, 1, 128), I32), V((BD, W)), V((BD, 2 * W), BF16),
            V((E, H2), BF16), V((DIN, E), BF16), V((H1, E), BF16), V((E, H1)), V((E, H2)),
            V((NH, 128)), V((128, ND * CAP), BF16), V((ND * CAP, 128), BF16),
            V((2, NP, 1, 128)), V((ND, 1, 128)), V((2 * NH, ND * CAP), BF16), V((2 * NH, ND * CAP)),
            V((2, NP, 1, 128)), V((ND, 1, 128)),
            V((NP, 128)), V((NP, BD // 2, 128), BF16), V((ND * CAP, 2 * W), BF16), V((BD // 2, 1024), BF16), V((BD // 2, 2 * W)), V((BD, W)), V((BD, W)),
            V((E, H1), BF16), V((E, H2), BF16), V((DIN // 4, H1)), V((H1 // 2, H2)),
            *slabs(c1 // 2), *slabs(c1 // 2 + c2),
            V((8, 128)), V((R, 8, 128)), V((8, 128)), V((B, 8, 128)), V((8, 128)), V((NH, 128)),
            dma((12,)), dma((5,)), pltpu.SemaphoreType.REGULAR, dma((NC // 2,)), dma((NC // 2,)), dma(()), dma(()),
            dma((2,)), dma((2,)), dma((2, NC // 4)), dma((2,)), dma((2,)),
            dma((14,)), dma((6,)),
        ]
        shape = jax.ShapeDtypeStruct
        prob, z_new, n_new, grad_a, grad_b, small = pl.pallas_call(
            functools.partial(step_kernel, B, R),
            out_shape=(
                shape((NH, 128), F32), shape((BD, W), F32), shape((BD, W), F32),
                shape((2, NC, c1 // 2, 128), BF16), shape((2, NC, c1 // 2 + c2, 128), BF16), shape((8, 128), F32),
            ),
            in_specs=[hbm] * 13,
            out_specs=(hbm,) * 6,
            scratch_shapes=scratch,
            compiler_params=pltpu.CompilerParams(
                collective_id=0, has_side_effects=True, vmem_limit_bytes=60 * 1024 * 1024
            ),
        )(
            dense, labels.reshape(NH, 128), tile_values, tile_block.T, tile_example.T, tile_count.reshape(1, ND),
            z_state, n_state, w_one, b_one.reshape(1, H1), w_two, b_two.reshape(1, H2), head.reshape(H2 // 128, 128),
        )
        prob, z_new, n_new, g_one, g_b_one, g_two, g_b_two, g_head = pl.pallas_call(
            functools.partial(finish_kernel, c1, c2),
            out_shape=(
                shape((NH, 128), F32), shape((BD, W), F32), shape((BD, W), F32), shape((DIN, H1), F32),
                shape((1, H1), F32), shape((H1, H2), F32), shape((1, H2), F32), shape((1, H2), F32),
            ),
            in_specs=[hbm] * 6,
            out_specs=(hbm,) * 8,
            scratch_shapes=[
                V((2, NC, c1 // 2, 128), BF16), V((2, NC, c1 // 2 + c2, 128), BF16), V((BD, W)), V((BD, W)),
                V((DIN, H1)), V((H1, H2)), V((8, 128)), V((NH, 128)), V((1, H1)), V((1, H2)), V((1, H2)),
                dma((8,)), dma((12,)),
            ],
            compiler_params=pltpu.CompilerParams(vmem_limit_bytes=63 * 1024 * 1024),
        )(grad_a, grad_b, small, prob, z_new, n_new)
        return (
            prob.reshape(E), z_new, n_new, g_one, g_b_one.reshape(H1), g_two, g_b_two.reshape(H2), g_head.reshape(H2),
        )

    every = ("blk", "rep")
    return jax.shard_map(
        per_device,
        mesh=mesh,
        in_specs=(
            P(every, None), P(every), P(every, None, None), P(every, None), P(every, None), P(every),
            P(every, None), P(every, None), P(), P(), P(), P(), P(),
        ),
        out_specs=(P(every), P(every, None), P(every, None), P(), P(), P(), P(), P()),
        check_vma=False,
    )
```

```python
import functools

import jax
import jax.numpy as jnp
from jax import lax
from jax.experimental import pallas as pl
from jax.experimental.pallas import tpu as pltpu
from jax.sharding import PartitionSpec as P

MESH = pl.DeviceIdType.MESH
F32 = jnp.float32
BF16 = jnp.bfloat16
NT = (((1,), (1,)), ((), ()))
STRIDE = 27


def mm(a, b):
    return jnp.dot(a, b, preferred_element_type=F32)


def mm_nt(a, b):
    return lax.dot_general(a, b, NT, preferred_element_type=F32)


def step_kernel(
    B, R,
    dense_h, labels_h, values_h, block_h, example_h, count_h, z_h, n_h,
    w_one_h, b_one_h, w_two_h, b_two_h, head_h,
    prob_o, z_o, n_o, grad_a_o, grad_b_o, small_o,
    dense_v, labels_v, block_v, example_t, count_v, z_v, n_v, w_one_v, b_one_v, w_two_v, b_two_v, head_v,
    table_v, index_send, example_v,
    got_values, got_index, weight_v, weight_pair,
    hid_two_v, dense_t, hid_one_t, scale_one, scale_two, deep_v, low_hot, slot_hot,
    logit_send, logit_got, spread, picked, res_send, res_got,
    names_v, value_two, block_hot, total, z_out_v, n_out_v,
    d_one_v, d_two_v, own_one, own_two,
    part_a, pair_a, sum_a, got_a, final_a, full_a, part_b, pair_b, sum_b, got_b, final_b, full_b,
    small_v, small_rep, small_sum, small_blk, small_all, prob_v,
    load_sem, own_sem, ready_sem, index_sem, value_sem, logit_sem, res_sem,
    pair_sem, rs_sem, ag_sem, fw_sem, small_sem,
    send_sem, out_sem,
):
    ND = B * R
    NC = ND // 2
    X = R // 2
    Z = 4 if B % 4 == 0 else B
    Y = B // Z
    E, DIN = dense_v.shape
    H1 = w_one_v.shape[1]
    H2 = w_two_v.shape[1]
    CAP, W = got_values.shape[1], got_values.shape[2]
    BD = z_v.shape[0]
    NH = E // 128
    NP = ND // 2
    c1 = DIN * H1 // (128 * ND)
    c2 = H1 * H2 // (128 * ND)
    j1 = H1 // 128
    j2 = H2 // 128
    blk = lax.axis_index("blk")
    rep = lax.axis_index("rep")
    y, zz = lax.div(blk, Z), lax.rem(blk, Z)
    x, core = lax.div(rep, 2), lax.rem(rep, 2)
    other = 1 - core
    me = blk * R + rep
    chip = blk * X + x
    y_at = [lax.rem(y + i, Y) * Z for i in range(Y)]
    z_at = [lax.rem(zz + i, Z) for i in range(Z)]
    x_at = [lax.rem(x + i, X) for i in range(X)]

    order = [(m * STRIDE) % NC for m in range(NC)]

    def spread_of(spot):
        return spot // (Z * X), spot // X % Z, spot % X

    def chip_at(m):
        dy, dz, dx = spread_of(order[m])
        return y_at[dy] + z_at[dz], x_at[dx]

    def chip_from(m):
        dy, dz, dx = spread_of(order[m])
        return y_at[(Y - dy) % Y] + z_at[(Z - dz) % Z], x_at[(X - dx) % X]

    loads = [
        (block_h, block_v), (count_h, count_v), (example_h, example_t), (z_h, z_v), (n_h, n_v), (dense_h, dense_v),
        (w_one_h, w_one_v), (b_one_h, b_one_v), (w_two_h, w_two_v), (b_two_h, b_two_v), (head_h, head_v),
        (labels_h, labels_v),
    ]
    copies = [pltpu.make_async_copy(s, d, load_sem.at[i]) for i, (s, d) in enumerate(loads)]
    for copy in copies:
        copy.start()

    def send(src, dst, sem_at, recv, where):
        pltpu.make_async_remote_copy(
            src_ref=src, dst_ref=dst, send_sem=send_sem.at[sem_at], recv_sem=recv,
            device_id=where, device_id_type=MESH,
        ).start()

    def wait_for(ref, sem):
        pltpu.make_async_copy(ref, ref, sem).wait()

    barrier = pltpu.get_barrier_semaphore()
    for k in range(1, B):
        pl.semaphore_signal(barrier, inc=1, device_id=(lax.rem(blk + k, B), rep), device_id_type=MESH)
    for k in range(1, R):
        pl.semaphore_signal(barrier, inc=1, device_id=(blk, lax.rem(rep + k, R)), device_id_type=MESH)
    own_value = pltpu.make_async_copy(values_h.at[me], got_values.at[me], own_sem.at[0])
    own_value.start()

    first_half = lax.broadcasted_iota(jnp.int32, (1, 128), 1) < CAP
    copies[0].wait()
    copies[1].wait()
    live = lax.broadcasted_iota(jnp.int32, (CAP, ND), 0) < count_v[...]
    named = jnp.where(live, block_v[...], -1).astype(F32)
    table_v[...] = jnp.concatenate([named, named], axis=0).T.astype(jnp.int32)
    for o in range(ND):
        index_send[o] = table_v[o:o + 1, :]

    pl.semaphore_wait(barrier, B + R - 2)
    for k in range(1, R):
        pl.semaphore_signal(ready_sem, inc=1, device_id=(blk, lax.rem(rep + k, R)), device_id_type=MESH)

    def give(m, c):
        blk_to, x_to = chip_at(m)
        rep_to = x_to * 2 + c
        to = blk_to * R + rep_to
        send(index_send.at[to], got_index.at[me], 0, index_sem.at[m // 2], (blk_to, rep_to))
        send(values_h.at[to], got_values.at[me], 1, value_sem.at[m // 2], (blk_to, rep_to))

    give(0, other)
    for m in range(1, NC):
        spot = order[m]
        if spot < X:
            give(m, 0)
            give(m, 1)
        elif spot % X == 0:
            give(m, core)
    copies[2].wait()
    named = example_t[...].astype(F32)
    table_v[...] = jnp.concatenate([named, named], axis=0).T.astype(jnp.int32)
    for p in range(NP):
        example_v[p] = jnp.where(first_half, table_v[2 * p:2 * p + 1, :], table_v[2 * p + 1:2 * p + 2, :])
    pl.semaphore_wait(ready_sem, R - 1)

    for m in range(1, NC):
        spot = order[m]
        if spot >= X and spot % X == 0:
            give(m, other)
        elif spot >= X:
            give(m, 0)
            give(m, 1)
    got_index[me] = index_send[me]

    copies[3].wait()
    copies[4].wait()
    z = z_v[...]
    shrunk = z - jnp.where(z > 0, 0.5, -0.5)
    weight = jnp.where(jnp.abs(z) > 0.5, -shrunk / ((1.0 + jnp.sqrt(n_v[...])) / 0.5 + 0.1), 0.0)
    weight_v[...] = weight
    high = weight.astype(BF16)
    weight_pair[:, :W] = high
    weight_pair[:, W:] = (weight - high.astype(F32)).astype(BF16)

    for copy in copies[5:]:
        copy.wait()
    rows = 256
    head_row = jnp.concatenate([head_v[q:q + 1, :] for q in range(j2)], axis=1)
    head_rows = jnp.broadcast_to(head_row, (8, H2))

    @pl.loop(0, E // rows)
    def _(i):
        at = pl.multiple_of(i * rows, rows)
        dense = dense_v[pl.ds(at, rows), :]
        pre_one = mm(dense, w_one_v[...]) + b_one_v[...]
        gate_one = jax.nn.sigmoid(pre_one)
        hid_one = (pre_one * gate_one).astype(BF16)
        pre_two = mm(hid_one, w_two_v[...]) + b_two_v[...]
        gate_two = jax.nn.sigmoid(pre_two)
        hid_two = (pre_two * gate_two).astype(BF16)
        hid_two_v[pl.ds(at, rows), :] = hid_two
        two = head_row.astype(F32) * (gate_two * (1.0 + pre_two * (1.0 - gate_two)))
        scale_two[pl.ds(at, rows), :] = two
        back = mm_nt(two.astype(BF16), w_two_v[...])
        scale_one[pl.ds(at, rows), :] = back * (gate_one * (1.0 + pre_one * (1.0 - gate_one)))
        deep = mm_nt(head_rows, hid_two)
        for q in range(rows // 128):
            deep_v[pl.ds(i * (rows // 128) + q, 1), :] = deep[0:1, q * 128:(q + 1) * 128]
        dense_t[:, pl.ds(at, rows)] = dense.T
        hid_one_t[:, pl.ds(at, rows)] = hid_one.T

    @pl.loop(0, NP)
    def _(p):
        at = pl.multiple_of(p * 128, 128)
        low = lax.bitwise_and(example_v[p], 127)
        hot = (lax.broadcasted_iota(jnp.int32, (128, 128), 0) == low).astype(F32)
        low_hot[:, pl.ds(at, 128)] = hot.astype(BF16)
        slot_hot[pl.ds(at, 128), :] = hot.T.astype(BF16)

    def merged(ref, p):
        return jnp.where(first_half, ref[2 * p], ref[2 * p + 1])

    def flipped(row):
        return pltpu.roll(jnp.broadcast_to(row, (8, 128)), CAP, axis=1)[0:1]

    def logits_of(places):
        spots = [b * X + xs for b, xs in places]
        four = jnp.concatenate([got_values[pl.ds(2 * q, 2)].reshape(2 * CAP, W) for q in spots], axis=0)
        score = mm_nt(weight_pair[...], jnp.concatenate([four, four], axis=1))
        for i, q in enumerate(spots):
            hit = lax.broadcasted_iota(jnp.int32, (BD, 128), 0) == merged(got_index, q)
            row = jnp.sum(jnp.where(hit, score[:, i * 128:(i + 1) * 128], 0.0), axis=0, keepdims=True)
            logit_send[0, q] = row
            logit_send[1, q] = flipped(row)

    own_value.wait()
    wait_for(got_index.at[pl.ds(0, 3)], index_sem.at[0])
    wait_for(got_values.at[pl.ds(0, 3)], value_sem.at[0])
    b_next, x_next = chip_from(1)
    logits_of([(blk, x), (b_next, x_next)])
    send(logit_send.at[1, chip], logit_got.at[me], 2, logit_sem, (blk, x * 2 + other))
    for c, turn in ((0, core), (1, other)):
        send(logit_send.at[turn, b_next * X + x_next], logit_got.at[me], 2, logit_sem, (b_next, x_next * 2 + c))
    logit_got[me] = logit_send[0, chip]

    for u in range(1, NC // 2):
        wait_for(got_index.at[pl.ds(0, 4)], index_sem.at[u])
        wait_for(got_values.at[pl.ds(0, 4)], value_sem.at[u])
        places = [chip_from(2 * u), chip_from(2 * u + 1)]
        logits_of(places)
        for b_to, x_to in places:
            for c, turn in ((0, core), (1, other)):
                send(logit_send.at[turn, b_to * X + x_to], logit_got.at[me], 2, logit_sem, (b_to, x_to * 2 + c))

    half_table = BD // 2

    wait_for(logit_got.at[pl.ds(0, ND - 1)], logit_sem)
    eight = lax.broadcasted_iota(jnp.int32, (NH, 128), 0)
    for p in range(NP):
        mine = eight == lax.shift_right_logical(example_v[p], 7)
        term = jnp.where(mine, merged(logit_got, p), 0.0)
        top = term.astype(BF16).astype(F32)
        spread[:, p * 128:(p + 1) * 128] = jnp.concatenate([top, term - top], axis=0).astype(BF16)
    wide = mm(spread[...], slot_hot[...])
    prob = jax.nn.sigmoid(wide[:NH] + wide[NH:] + deep_v[...])
    prob_v[...] = prob
    out_prob = pltpu.make_async_copy(prob_v, prob_o, out_sem.at[4])
    out_prob.start()
    residual = prob - labels_v[...].astype(F32)
    dlogit = residual.astype(BF16).astype(F32)

    upright = jnp.concatenate([dlogit, jnp.zeros((128 - NH, 128), F32)], axis=0).T
    for q in range(NH):
        span = slice(q * 128, (q + 1) * 128)
        column = upright[:, q:q + 1]
        d_two_v[span, :] = (scale_two[span, :] * column).astype(BF16)
        d_one_v[span, :] = (scale_one[span, :] * column).astype(BF16)

    half_one, half_two = DIN // 2, H1 // 2
    quarter = DIN // 4
    rep_other = x * 2 + other
    ca = c1 // 2

    def cut(q, height, across):
        return slice(q // across * height, (q // across + 1) * height), slice(q % across * 128, (q % across + 1) * 128)

    def grad_one(which, piece):
        return mm(dense_t[pl.ds(pl.multiple_of(which * half_one + piece * quarter, quarter), quarter), :], d_one_v[...])

    def grad_two(which):
        return mm(hid_one_t[pl.ds(pl.multiple_of(which * half_two, half_two), half_two), :], d_two_v[...])

    one = grad_one(other, 0)
    for q in range(NC):
        part_a[q] = one[cut(q, ca, j1)].astype(BF16)
    send(part_a, pair_a, 3, pair_sem.at[0], (blk, rep_other))
    one = grad_one(other, 1)
    two = grad_two(other)
    for q in range(NC):
        part_b[q, 0:ca, :] = one[cut(q, ca, j1)].astype(BF16)
        part_b[q, ca:ca + c2, :] = two[cut(q, c2, j2)].astype(BF16)
    send(part_b, pair_b, 10, pair_sem.at[1], (blk, rep_other))

    own_one[...] = grad_one(core, 0)
    wait_for(pair_a, pair_sem.at[0])
    for q in range(NC):
        sum_a[q] = (own_one[cut(q, ca, j1)] + pair_a[q].astype(F32)).astype(BF16)
    for m in range(1, NC):
        b_to, x_to = chip_at(m)
        send(sum_a.at[b_to * X + x_to], got_a.at[chip], 4, rs_sem.at[0], (b_to, x_to * 2 + core))
    own_a = pltpu.make_async_copy(sum_a.at[chip], got_a.at[chip], own_sem.at[1])
    own_a.start()

    own_one[...] = grad_one(core, 1)
    own_two[...] = grad_two(core)
    wait_for(pair_b, pair_sem.at[1])
    for q in range(NC):
        sum_b[q, 0:ca, :] = (own_one[cut(q, ca, j1)] + pair_b[q, 0:ca, :].astype(F32)).astype(BF16)
        sum_b[q, ca:ca + c2, :] = (own_two[cut(q, c2, j2)] + pair_b[q, ca:ca + c2, :].astype(F32)).astype(BF16)
    for m in range(1, NC):
        b_to, x_to = chip_at(m)
        send(sum_b.at[b_to * X + x_to], got_b.at[chip], 11, rs_sem.at[1], (b_to, x_to * 2 + core))
    own_b = pltpu.make_async_copy(sum_b.at[chip], got_b.at[chip], own_sem.at[2])
    own_b.start()

    table = jnp.concatenate([dlogit, jnp.zeros_like(dlogit)], axis=0).astype(BF16)
    picked[...] = mm(table, low_hot[...])
    for p in range(NP):
        mine = eight == lax.shift_right_logical(example_v[p], 7)
        row = jnp.sum(jnp.where(mine, picked[0:NH, p * 128:(p + 1) * 128], 0.0), axis=0, keepdims=True)
        res_send[0, p] = row
        res_send[1, p] = flipped(row)
    for m in range(NC):
        b_to, x_to = chip_at(m)
        q = b_to * X + x_to
        if m == 0:
            send(res_send.at[1, q], res_got.at[me], 5, res_sem, (b_to, x_to * 2 + other))
        else:
            for c, turn in ((0, core), (1, other)):
                send(res_send.at[turn, q], res_got.at[me], 5, res_sem, (b_to, x_to * 2 + c))
    res_got[me] = res_send[0, chip]

    grad_head = jnp.zeros((8, H2), F32)
    for q in range(NH):
        grad_head += mm(jnp.broadcast_to(dlogit[q:q + 1, :], (8, 128)).astype(BF16), hid_two_v[q * 128:(q + 1) * 128, :])
    ones = jnp.ones((8, E), BF16)
    bias_one = mm(ones, d_one_v[...])
    bias_two = mm(ones, d_two_v[...])
    small_v[...] = jnp.zeros_like(small_v)
    for q in range(j1):
        small_v[q:q + 1, :] = bias_one[0:1, q * 128:(q + 1) * 128]
    for q in range(j2):
        small_v[j1 + q:j1 + q + 1, :] = bias_two[0:1, q * 128:(q + 1) * 128]
        small_v[j1 + j2 + q:j1 + j2 + q + 1, :] = grad_head[0:1, q * 128:(q + 1) * 128]
    for k in range(1, R):
        send(small_v, small_rep.at[rep], 6, small_sem.at[0], (blk, lax.rem(rep + k, R)))
    small_rep[rep] = small_v[...]

    def hand_out(own, got, final, full, out_h, piece, sem_at):
        own.wait()
        wait_for(got.at[pl.ds(0, NC - 1)], rs_sem.at[piece])
        final[...] = lax.fori_loop(
            1, NC, lambda q, a: a + got[q].astype(F32), got[0].astype(F32)
        ).astype(BF16)
        for m in range(1, NC):
            b_to, x_to = chip_at(m)
            send(final, full.at[chip], sem_at, ag_sem.at[piece, m // 4], (b_to, x_to * 2 + core))
        send(final, out_h.at[core, chip], 8 + 5 * piece, fw_sem.at[piece], (blk, rep_other))
        copy = pltpu.make_async_copy(final, full.at[chip], own_sem.at[3 + piece])
        copy.start()
        return copy

    own_final_a = hand_out(own_a, got_a, final_a, full_a, grad_a_o, 0, 7)
    own_final_b = hand_out(own_b, got_b, final_b, full_b, grad_b_o, 1, 12)

    wait_for(small_rep.at[pl.ds(0, R - 1)], small_sem.at[0])
    acc = small_rep[0]
    for r in range(1, R):
        acc = acc + small_rep[r]
    small_sum[...] = acc
    for k in range(1, B):
        send(small_sum, small_blk.at[blk], 9, small_sem.at[1], (lax.rem(blk + k, B), rep))
    small_blk[blk] = acc

    for p in range(NP):
        names_v[p:p + 1, :] = (merged(got_index, p) >= half_table).astype(F32)
    upper = names_v[...].T
    for p in range(NP):
        values = got_values[2 * p:2 * p + 2].reshape(2 * CAP, W)
        above = values * jnp.broadcast_to(upper[:, p:p + 1], (2 * CAP, W)).astype(BF16)
        value_two[p * 128:(p + 1) * 128, 0:W] = values - above
        value_two[p * 128:(p + 1) * 128, W:2 * W] = above

    wait_for(res_got.at[pl.ds(0, ND - 1)], res_sem)
    total[...] = jnp.zeros_like(total)

    @pl.loop(0, NP // 8)
    def _(g):
        for h in range(8):
            p = g * 8 + h
            name = merged(got_index, p)
            low = jnp.where(name < 0, -1, lax.bitwise_and(name, half_table - 1))
            hit = lax.broadcasted_iota(jnp.int32, (half_table, 128), 0) == low
            block_hot[:, h * 128:(h + 1) * 128] = jnp.where(hit, merged(res_got, p), 0.0).astype(BF16)
        total[...] += mm(block_hot[...], value_two[pl.ds(pl.multiple_of(g * 1024, 1024), 1024), :])

    for h in range(2):
        span = slice(h * half_table, (h + 1) * half_table)
        grad = total[:, h * W:(h + 1) * W]
        n_old = n_v[span, :]
        n_new = n_old + grad * grad
        n_out_v[span, :] = n_new
        z_out_v[span, :] = z_v[span, :] + grad - (jnp.sqrt(n_new) - jnp.sqrt(n_old)) / 0.5 * weight_v[span, :]
    out_z = pltpu.make_async_copy(z_out_v, z_o, out_sem.at[0])
    out_z.start()
    out_n = pltpu.make_async_copy(n_out_v, n_o, out_sem.at[1])
    out_n.start()

    wait_for(small_blk.at[pl.ds(0, B - 1)], small_sem.at[1])
    acc = small_blk[0]
    for r in range(1, B):
        acc = acc + small_blk[r]
    small_all[...] = acc
    out_small = pltpu.make_async_copy(small_all, small_o, out_sem.at[5])
    out_small.start()

    def pass_all(own, got, full, out_h, piece):
        own.wait()

        def pass_on(m):
            b_from, x_from = chip_from(m)
            q = b_from * X + x_from
            send(full.at[q], out_h.at[core, q], 8 + 5 * piece, fw_sem.at[piece], (blk, rep_other))

        wait_for(got.at[pl.ds(0, 3)], ag_sem.at[piece, 0])
        for m in range(1, 4):
            pass_on(m)

        for g in range(1, NC // 4):
            wait_for(got.at[pl.ds(0, 4)], ag_sem.at[piece, g])
            for i in range(4):
                pass_on(4 * g + i)

        copy = pltpu.make_async_copy(full, out_h.at[core], out_sem.at[2 + piece])
        copy.start()
        return copy

    out_a = pass_all(own_final_a, got_a, full_a, grad_a_o, 0)
    out_b = pass_all(own_final_b, got_b, full_b, grad_b_o, 1)
    wait_for(got_a, fw_sem.at[0])
    wait_for(got_b, fw_sem.at[1])

    wait_for(got_index.at[pl.ds(0, ND - 1)], send_sem.at[0])
    wait_for(got_values.at[pl.ds(0, ND - 1)], send_sem.at[1])
    wait_for(logit_got.at[pl.ds(0, ND - 1)], send_sem.at[2])
    wait_for(part_a, send_sem.at[3])
    wait_for(got_a.at[pl.ds(0, NC - 1)], send_sem.at[4])
    wait_for(res_got.at[pl.ds(0, ND - 1)], send_sem.at[5])
    wait_for(small_rep.at[pl.ds(0, R - 1)], send_sem.at[6])
    wait_for(got_a.at[pl.ds(0, NC - 1)], send_sem.at[7])
    wait_for(got_a, send_sem.at[8])
    wait_for(part_b, send_sem.at[10])
    wait_for(got_b.at[pl.ds(0, NC - 1)], send_sem.at[11])
    wait_for(got_b.at[pl.ds(0, NC - 1)], send_sem.at[12])
    wait_for(got_b, send_sem.at[13])
    wait_for(small_blk.at[pl.ds(0, B - 1)], send_sem.at[9])
    for copy in (out_z, out_n, out_a, out_b, out_prob, out_small):
        copy.wait()


def finish_kernel(
    c1, c2, grad_a_h, grad_b_h, small_h, prob_h, z_h, n_h, prob_o, z_o, n_o, g_one_o, b_one_o, g_two_o, b_two_o, head_o,
    grad_a_v, grad_b_v, z_v, n_v, one_v, two_v, small_v, prob_v, b_one_v, b_two_v, head_v, in_sem, out_sem,
):
    NC = grad_a_v.shape[1]
    DIN, H1 = one_v.shape
    H2 = two_v.shape[1]
    j1, j2 = H1 // 128, H2 // 128
    ca = c1 // 2
    quarter = DIN // 4
    ins = []
    for h in range(2):
        ins.append(pltpu.make_async_copy(grad_a_h.at[h], grad_a_v.at[h], in_sem.at[2 * h]))
        ins.append(pltpu.make_async_copy(grad_b_h.at[h], grad_b_v.at[h], in_sem.at[2 * h + 1]))
    in_z = pltpu.make_async_copy(z_h, z_v, in_sem.at[4])
    in_n = pltpu.make_async_copy(n_h, n_v, in_sem.at[5])
    in_prob = pltpu.make_async_copy(prob_h, prob_v, in_sem.at[6])
    in_small = pltpu.make_async_copy(small_h, small_v, in_sem.at[7])
    for copy in (*ins, in_z, in_n, in_prob, in_small):
        copy.start()
    outs = []

    def out(src, dst):
        outs.append(pltpu.make_async_copy(src, dst, out_sem.at[len(outs)]))
        outs[-1].start()

    for h in range(2):
        for piece, ref in ((0, grad_a_v), (1, grad_b_v)):
            ins[2 * h + piece].wait()
            top = h * (DIN // 2) + piece * quarter
            for q in range(NC):
                r1 = top + q // j1 * ca
                one_v[r1:r1 + ca, q % j1 * 128:(q % j1 + 1) * 128] = ref[h, q, 0:ca, :].astype(F32)
                if piece == 1:
                    r2 = h * (H1 // 2) + q // j2 * c2
                    two_v[r2:r2 + c2, q % j2 * 128:(q % j2 + 1) * 128] = ref[h, q, ca:ca + c2, :].astype(F32)
            out(one_v.at[pl.ds(top, quarter)], g_one_o.at[pl.ds(top, quarter)])
            if piece == 1:
                out(two_v.at[pl.ds(h * (H1 // 2), H1 // 2)], g_two_o.at[pl.ds(h * (H1 // 2), H1 // 2)])
        if h == 0:
            in_z.wait()
            out(z_v, z_o)
            in_n.wait()
            out(n_v, n_o)
        if h == 0:
            in_prob.wait()
            out(prob_v, prob_o)
            in_small.wait()
            for q in range(j1):
                b_one_v[:, q * 128:(q + 1) * 128] = small_v[q:q + 1, :]
            for q in range(j2):
                b_two_v[:, q * 128:(q + 1) * 128] = small_v[j1 + q:j1 + q + 1, :]
                head_v[:, q * 128:(q + 1) * 128] = small_v[j1 + j2 + q:j1 + j2 + q + 1, :]
            out(b_one_v, b_one_o)
            out(b_two_v, b_two_o)
            out(head_v, head_o)
    for copy in outs:
        copy.wait()


def solution(mesh):
    B, R = mesh.shape["blk"], mesh.shape["rep"]
    ND = B * R
    NC = ND // 2

    def per_device(
        dense, labels, tile_values, tile_block, tile_example, tile_count, z_state, n_state,
        w_one, b_one, w_two, b_two, head,
    ):
        E, DIN = dense.shape
        _, CAP, W = tile_values.shape
        BD = z_state.shape[0]
        H1, H2 = w_two.shape
        NH = E // 128
        NP = ND // 2
        c1 = DIN * H1 // (128 * ND)
        c2 = H1 * H2 // (128 * ND)
        hbm = pl.BlockSpec(memory_space=pl.ANY)
        I32 = jnp.int32

        def V(shape, kind=F32):
            return pltpu.VMEM(shape, kind)

        def slabs(high):
            each = V((NC, high, 128), BF16)
            return each, each, each, each, V((high, 128), BF16), each

        dma = pltpu.SemaphoreType.DMA
        scratch = [
            V((E, DIN), BF16), V((NH, 128), I32), V((CAP, ND), I32), V((CAP, ND), I32), V((1, ND), I32),
            V((BD, W)), V((BD, W)), V((DIN, H1), BF16), V((1, H1)), V((H1, H2), BF16), V((1, H2)), V((H2 // 128, 128), BF16),
            V((ND, 128), I32), V((ND, 1, 128), I32), V((NP, 1, 128), I32),
            V((ND, CAP, W), BF16), V((ND, 1, 128), I32), V((BD, W)), V((BD, 2 * W), BF16),
            V((E, H2), BF16), V((DIN, E), BF16), V((H1, E), BF16), V((E, H1)), V((E, H2)),
            V((NH, 128)), V((128, ND * CAP), BF16), V((ND * CAP, 128), BF16),
            V((2, NP, 1, 128)), V((ND, 1, 128)), V((2 * NH, ND * CAP), BF16), V((2 * NH, ND * CAP)),
            V((2, NP, 1, 128)), V((ND, 1, 128)),
            V((NP, 128)), V((ND * CAP, 2 * W), BF16), V((BD // 2, 1024), BF16), V((BD // 2, 2 * W)), V((BD, W)), V((BD, W)),
            V((E, H1), BF16), V((E, H2), BF16), V((DIN // 4, H1)), V((H1 // 2, H2)),
            *slabs(c1 // 2), *slabs(c1 // 2 + c2),
            V((8, 128)), V((R, 8, 128)), V((8, 128)), V((B, 8, 128)), V((8, 128)), V((NH, 128)),
            dma((12,)), dma((5,)), pltpu.SemaphoreType.REGULAR, dma((NC // 2,)), dma((NC // 2,)), dma(()), dma(()),
            dma((2,)), dma((2,)), dma((2, NC // 4)), dma((2,)), dma((2,)),
            dma((14,)), dma((6,)),
        ]
        shape = jax.ShapeDtypeStruct
        prob, z_new, n_new, grad_a, grad_b, small = pl.pallas_call(
            functools.partial(step_kernel, B, R),
            out_shape=(
                shape((NH, 128), F32), shape((BD, W), F32), shape((BD, W), F32),
                shape((2, NC, c1 // 2, 128), BF16), shape((2, NC, c1 // 2 + c2, 128), BF16), shape((8, 128), F32),
            ),
            in_specs=[hbm] * 13,
            out_specs=(hbm,) * 6,
            scratch_shapes=scratch,
            compiler_params=pltpu.CompilerParams(
                collective_id=0, has_side_effects=True, vmem_limit_bytes=60 * 1024 * 1024
            ),
        )(
            dense, labels.reshape(NH, 128), tile_values, tile_block.T, tile_example.T, tile_count.reshape(1, ND),
            z_state, n_state, w_one, b_one.reshape(1, H1), w_two, b_two.reshape(1, H2), head.reshape(H2 // 128, 128),
        )
        prob, z_new, n_new, g_one, g_b_one, g_two, g_b_two, g_head = pl.pallas_call(
            functools.partial(finish_kernel, c1, c2),
            out_shape=(
                shape((NH, 128), F32), shape((BD, W), F32), shape((BD, W), F32), shape((DIN, H1), F32),
                shape((1, H1), F32), shape((H1, H2), F32), shape((1, H2), F32), shape((1, H2), F32),
            ),
            in_specs=[hbm] * 6,
            out_specs=(hbm,) * 8,
            scratch_shapes=[
                V((2, NC, c1 // 2, 128), BF16), V((2, NC, c1 // 2 + c2, 128), BF16), V((BD, W)), V((BD, W)),
                V((DIN, H1)), V((H1, H2)), V((8, 128)), V((NH, 128)), V((1, H1)), V((1, H2)), V((1, H2)),
                dma((8,)), dma((12,)),
            ],
            compiler_params=pltpu.CompilerParams(vmem_limit_bytes=63 * 1024 * 1024),
        )(grad_a, grad_b, small, prob, z_new, n_new)
        return (
            prob.reshape(E), z_new, n_new, g_one, g_b_one.reshape(H1), g_two, g_b_two.reshape(H2), g_head.reshape(H2),
        )

    every = ("blk", "rep")
    return jax.shard_map(
        per_device,
        mesh=mesh,
        in_specs=(
            P(every, None), P(every), P(every, None, None), P(every, None), P(every, None), P(every),
            P(every, None), P(every, None), P(), P(), P(), P(), P(),
        ),
        out_specs=(P(every), P(every, None), P(every, None), P(), P(), P(), P(), P()),
        check_vma=False,
    )
```

```python
import functools

import jax
import jax.numpy as jnp
from jax import lax
from jax.experimental import pallas as pl
from jax.experimental.pallas import tpu as pltpu
from jax.sharding import PartitionSpec as P

MESH = pl.DeviceIdType.MESH
F32 = jnp.float32
BF16 = jnp.bfloat16
NT = (((1,), (1,)), ((), ()))
STRIDE = 27


def mm(a, b):
    return jnp.dot(a, b, preferred_element_type=F32)


def mm_nt(a, b):
    return lax.dot_general(a, b, NT, preferred_element_type=F32)


def step_kernel(
    B, R,
    dense_h, labels_h, values_h, block_h, example_h, count_h, z_h, n_h,
    w_one_h, b_one_h, w_two_h, b_two_h, head_h,
    prob_o, z_o, n_o, grad_a_o, grad_b_o, small_o,
    dense_v, labels_v, block_v, example_t, count_v, z_v, n_v, w_one_v, b_one_v, w_two_v, b_two_v, head_v,
    table_v, index_send, example_v,
    got_values, got_index, weight_v, weight_pair,
    hid_two_v, dense_t, hid_one_t, scale_one, scale_two, deep_v, low_hot, slot_hot,
    logit_send, logit_got, spread, picked, res_send, res_got,
    names_v, value_two, block_hot, total, z_out_v, n_out_v,
    d_one_v, d_two_v, own_one, own_two,
    part_a, pair_a, sum_a, got_a, final_a, full_a, part_b, pair_b, sum_b, got_b, final_b, full_b,
    small_v, small_rep, small_sum, small_blk, small_all, prob_v,
    load_sem, own_sem, ready_sem, index_sem, value_sem, logit_sem, res_sem,
    pair_sem, rs_sem, ag_sem, fw_sem, small_sem,
    send_sem, out_sem,
):
    ND = B * R
    NC = ND // 2
    X = R // 2
    Z = 4 if B % 4 == 0 else B
    Y = B // Z
    E, DIN = dense_v.shape
    H1 = w_one_v.shape[1]
    H2 = w_two_v.shape[1]
    CAP, W = got_values.shape[1], got_values.shape[2]
    BD = z_v.shape[0]
    NH = E // 128
    NP = ND // 2
    c1 = DIN * H1 // (128 * ND)
    c2 = H1 * H2 // (128 * ND)
    j1 = H1 // 128
    j2 = H2 // 128
    blk = lax.axis_index("blk")
    rep = lax.axis_index("rep")
    y, zz = lax.div(blk, Z), lax.rem(blk, Z)
    x, core = lax.div(rep, 2), lax.rem(rep, 2)
    other = 1 - core
    me = blk * R + rep
    chip = blk * X + x
    y_at = [lax.rem(y + i, Y) * Z for i in range(Y)]
    z_at = [lax.rem(zz + i, Z) for i in range(Z)]
    x_at = [lax.rem(x + i, X) for i in range(X)]

    order = [(m * STRIDE) % NC for m in range(NC)]

    def spread_of(spot):
        return spot // (Z * X), spot // X % Z, spot % X

    def chip_at(m):
        dy, dz, dx = spread_of(order[m])
        return y_at[dy] + z_at[dz], x_at[dx]

    def chip_from(m):
        spot = lax.rem(m * STRIDE, NC)
        dy, dz, dx = lax.div(spot, Z * X), lax.rem(lax.div(spot, X), Z), lax.rem(spot, X)
        return lax.rem(y + Y - dy, Y) * Z + lax.rem(zz + Z - dz, Z), lax.rem(x + X - dx, X)

    loads = [
        (block_h, block_v), (count_h, count_v), (example_h, example_t), (z_h, z_v), (n_h, n_v), (dense_h, dense_v),
        (w_one_h, w_one_v), (b_one_h, b_one_v), (w_two_h, w_two_v), (b_two_h, b_two_v), (head_h, head_v),
        (labels_h, labels_v),
    ]
    copies = [pltpu.make_async_copy(s, d, load_sem.at[i]) for i, (s, d) in enumerate(loads)]
    for copy in copies:
        copy.start()

    def send(src, dst, sem_at, recv, where):
        pltpu.make_async_remote_copy(
            src_ref=src, dst_ref=dst, send_sem=send_sem.at[sem_at], recv_sem=recv,
            device_id=where, device_id_type=MESH,
        ).start()

    def wait_for(ref, sem):
        pltpu.make_async_copy(ref, ref, sem).wait()

    barrier = pltpu.get_barrier_semaphore()
    for k in range(1, B):
        pl.semaphore_signal(barrier, inc=1, device_id=(lax.rem(blk + k, B), rep), device_id_type=MESH)
    for k in range(1, R):
        pl.semaphore_signal(barrier, inc=1, device_id=(blk, lax.rem(rep + k, R)), device_id_type=MESH)
    own_value = pltpu.make_async_copy(values_h.at[me], got_values.at[me], own_sem.at[0])
    own_value.start()

    first_half = lax.broadcasted_iota(jnp.int32, (1, 128), 1) < CAP
    copies[0].wait()
    copies[1].wait()
    live = lax.broadcasted_iota(jnp.int32, (CAP, ND), 0) < count_v[...]
    named = jnp.where(live, block_v[...], -1).astype(F32)
    table_v[...] = jnp.concatenate([named, named], axis=0).T.astype(jnp.int32)
    for o in range(ND):
        index_send[o] = table_v[o:o + 1, :]

    pl.semaphore_wait(barrier, B + R - 2)
    for k in range(1, R):
        pl.semaphore_signal(ready_sem, inc=1, device_id=(blk, lax.rem(rep + k, R)), device_id_type=MESH)

    def give(m, c):
        blk_to, x_to = chip_at(m)
        rep_to = x_to * 2 + c
        to = blk_to * R + rep_to
        send(index_send.at[to], got_index.at[me], 0, index_sem.at[m // 2], (blk_to, rep_to))
        send(values_h.at[to], got_values.at[me], 1, value_sem.at[m // 2], (blk_to, rep_to))

    give(0, other)
    for m in range(1, NC):
        spot = order[m]
        if spot < X:
            give(m, 0)
            give(m, 1)
        elif spot % X == 0:
            give(m, core)
    copies[2].wait()
    named = example_t[...].astype(F32)
    table_v[...] = jnp.concatenate([named, named], axis=0).T.astype(jnp.int32)
    for p in range(NP):
        example_v[p] = jnp.where(first_half, table_v[2 * p:2 * p + 1, :], table_v[2 * p + 1:2 * p + 2, :])
    pl.semaphore_wait(ready_sem, R - 1)

    for m in range(1, NC):
        spot = order[m]
        if spot >= X and spot % X == 0:
            give(m, other)
        elif spot >= X:
            give(m, 0)
            give(m, 1)
    got_index[me] = index_send[me]

    copies[3].wait()
    copies[4].wait()
    z = z_v[...]
    shrunk = z - jnp.where(z > 0, 0.5, -0.5)
    weight = jnp.where(jnp.abs(z) > 0.5, -shrunk / ((1.0 + jnp.sqrt(n_v[...])) / 0.5 + 0.1), 0.0)
    weight_v[...] = weight
    high = weight.astype(BF16)
    weight_pair[:, :W] = high
    weight_pair[:, W:] = (weight - high.astype(F32)).astype(BF16)

    for copy in copies[5:]:
        copy.wait()
    rows = 256
    head_row = jnp.concatenate([head_v[q:q + 1, :] for q in range(j2)], axis=1)
    head_rows = jnp.broadcast_to(head_row, (8, H2))

    @pl.loop(0, E // rows)
    def _(i):
        at = pl.multiple_of(i * rows, rows)
        dense = dense_v[pl.ds(at, rows), :]
        pre_one = mm(dense, w_one_v[...]) + b_one_v[...]
        gate_one = jax.nn.sigmoid(pre_one)
        hid_one = (pre_one * gate_one).astype(BF16)
        pre_two = mm(hid_one, w_two_v[...]) + b_two_v[...]
        gate_two = jax.nn.sigmoid(pre_two)
        hid_two = (pre_two * gate_two).astype(BF16)
        hid_two_v[pl.ds(at, rows), :] = hid_two
        two = head_row.astype(F32) * (gate_two * (1.0 + pre_two * (1.0 - gate_two)))
        scale_two[pl.ds(at, rows), :] = two
        back = mm_nt(two.astype(BF16), w_two_v[...])
        scale_one[pl.ds(at, rows), :] = back * (gate_one * (1.0 + pre_one * (1.0 - gate_one)))
        deep = mm_nt(head_rows, hid_two)
        for q in range(rows // 128):
            deep_v[pl.ds(i * (rows // 128) + q, 1), :] = deep[0:1, q * 128:(q + 1) * 128]
        dense_t[:, pl.ds(at, rows)] = dense.T
        hid_one_t[:, pl.ds(at, rows)] = hid_one.T

    @pl.loop(0, NP)
    def _(p):
        at = pl.multiple_of(p * 128, 128)
        low = lax.bitwise_and(example_v[p], 127)
        hot = (lax.broadcasted_iota(jnp.int32, (128, 128), 0) == low).astype(F32)
        low_hot[:, pl.ds(at, 128)] = hot.astype(BF16)
        slot_hot[pl.ds(at, 128), :] = hot.T.astype(BF16)

    def merged(ref, p):
        return jnp.where(first_half, ref[2 * p], ref[2 * p + 1])

    def flipped(row):
        return pltpu.roll(jnp.broadcast_to(row, (8, 128)), CAP, axis=1)[0:1]

    def logits_of(places):
        spots = [b * X + xs for b, xs in places]
        four = jnp.concatenate([got_values[pl.ds(2 * q, 2)].reshape(2 * CAP, W) for q in spots], axis=0)
        score = mm_nt(weight_pair[...], jnp.concatenate([four, four], axis=1))
        for i, q in enumerate(spots):
            hit = lax.broadcasted_iota(jnp.int32, (BD, 128), 0) == merged(got_index, q)
            row = jnp.sum(jnp.where(hit, score[:, i * 128:(i + 1) * 128], 0.0), axis=0, keepdims=True)
            logit_send[0, q] = row
            logit_send[1, q] = flipped(row)

    own_value.wait()
    wait_for(got_index.at[pl.ds(0, 3)], index_sem.at[0])
    wait_for(got_values.at[pl.ds(0, 3)], value_sem.at[0])
    b_next, x_next = chip_from(1)
    logits_of([(blk, x), (b_next, x_next)])
    send(logit_send.at[1, chip], logit_got.at[me], 2, logit_sem, (blk, x * 2 + other))
    for c, turn in ((0, core), (1, other)):
        send(logit_send.at[turn, b_next * X + x_next], logit_got.at[me], 2, logit_sem, (b_next, x_next * 2 + c))
    logit_got[me] = logit_send[0, chip]

    @pl.loop(1, NC // 2)
    def _(u):
        wait_for(got_index.at[pl.ds(0, 4)], index_sem.at[u])
        wait_for(got_values.at[pl.ds(0, 4)], value_sem.at[u])
        places = [chip_from(2 * u), chip_from(2 * u + 1)]
        logits_of(places)
        for b_to, x_to in places:
            for c, turn in ((0, core), (1, other)):
                send(logit_send.at[turn, b_to * X + x_to], logit_got.at[me], 2, logit_sem, (b_to, x_to * 2 + c))

    half_table = BD // 2

    wait_for(logit_got.at[pl.ds(0, ND - 1)], logit_sem)
    eight = lax.broadcasted_iota(jnp.int32, (NH, 128), 0)
    for p in range(NP):
        mine = eight == lax.shift_right_logical(example_v[p], 7)
        term = jnp.where(mine, merged(logit_got, p), 0.0)
        top = term.astype(BF16).astype(F32)
        spread[:, p * 128:(p + 1) * 128] = jnp.concatenate([top, term - top], axis=0).astype(BF16)
    wide = mm(spread[...], slot_hot[...])
    prob = jax.nn.sigmoid(wide[:NH] + wide[NH:] + deep_v[...])
    prob_v[...] = prob
    out_prob = pltpu.make_async_copy(prob_v, prob_o, out_sem.at[4])
    out_prob.start()
    residual = prob - labels_v[...].astype(F32)
    dlogit = residual.astype(BF16).astype(F32)

    upright = jnp.concatenate([dlogit, jnp.zeros((128 - NH, 128), F32)], axis=0).T
    for q in range(NH):
        span = slice(q * 128, (q + 1) * 128)
        column = upright[:, q:q + 1]
        d_two_v[span, :] = (scale_two[span, :] * column).astype(BF16)
        d_one_v[span, :] = (scale_one[span, :] * column).astype(BF16)

    half_one, half_two = DIN // 2, H1 // 2
    quarter = DIN // 4
    rep_other = x * 2 + other
    ca = c1 // 2

    def cut(q, height, across):
        return slice(q // across * height, (q // across + 1) * height), slice(q % across * 128, (q % across + 1) * 128)

    def grad_one(which, piece):
        return mm(dense_t[pl.ds(pl.multiple_of(which * half_one + piece * quarter, quarter), quarter), :], d_one_v[...])

    def grad_two(which):
        return mm(hid_one_t[pl.ds(pl.multiple_of(which * half_two, half_two), half_two), :], d_two_v[...])

    one = grad_one(other, 0)
    for q in range(NC):
        part_a[q] = one[cut(q, ca, j1)].astype(BF16)
    send(part_a, pair_a, 3, pair_sem.at[0], (blk, rep_other))
    one = grad_one(other, 1)
    two = grad_two(other)
    for q in range(NC):
        part_b[q, 0:ca, :] = one[cut(q, ca, j1)].astype(BF16)
        part_b[q, ca:ca + c2, :] = two[cut(q, c2, j2)].astype(BF16)
    send(part_b, pair_b, 10, pair_sem.at[1], (blk, rep_other))

    own_one[...] = grad_one(core, 0)
    wait_for(pair_a, pair_sem.at[0])
    for q in range(NC):
        sum_a[q] = (own_one[cut(q, ca, j1)] + pair_a[q].astype(F32)).astype(BF16)
    for m in range(1, NC):
        b_to, x_to = chip_at(m)
        send(sum_a.at[b_to * X + x_to], got_a.at[chip], 4, rs_sem.at[0], (b_to, x_to * 2 + core))
    own_a = pltpu.make_async_copy(sum_a.at[chip], got_a.at[chip], own_sem.at[1])
    own_a.start()

    own_one[...] = grad_one(core, 1)
    own_two[...] = grad_two(core)
    wait_for(pair_b, pair_sem.at[1])
    for q in range(NC):
        sum_b[q, 0:ca, :] = (own_one[cut(q, ca, j1)] + pair_b[q, 0:ca, :].astype(F32)).astype(BF16)
        sum_b[q, ca:ca + c2, :] = (own_two[cut(q, c2, j2)] + pair_b[q, ca:ca + c2, :].astype(F32)).astype(BF16)
    for m in range(1, NC):
        b_to, x_to = chip_at(m)
        send(sum_b.at[b_to * X + x_to], got_b.at[chip], 11, rs_sem.at[1], (b_to, x_to * 2 + core))
    own_b = pltpu.make_async_copy(sum_b.at[chip], got_b.at[chip], own_sem.at[2])
    own_b.start()

    table = jnp.concatenate([dlogit, jnp.zeros_like(dlogit)], axis=0).astype(BF16)
    picked[...] = mm(table, low_hot[...])
    for p in range(NP):
        mine = eight == lax.shift_right_logical(example_v[p], 7)
        row = jnp.sum(jnp.where(mine, picked[0:NH, p * 128:(p + 1) * 128], 0.0), axis=0, keepdims=True)
        res_send[0, p] = row
        res_send[1, p] = flipped(row)
    for m in range(NC):
        b_to, x_to = chip_at(m)
        q = b_to * X + x_to
        if m == 0:
            send(res_send.at[1, q], res_got.at[me], 5, res_sem, (b_to, x_to * 2 + other))
        else:
            for c, turn in ((0, core), (1, other)):
                send(res_send.at[turn, q], res_got.at[me], 5, res_sem, (b_to, x_to * 2 + c))
    res_got[me] = res_send[0, chip]

    grad_head = jnp.zeros((8, H2), F32)
    for q in range(NH):
        grad_head += mm(jnp.broadcast_to(dlogit[q:q + 1, :], (8, 128)).astype(BF16), hid_two_v[q * 128:(q + 1) * 128, :])
    ones = jnp.ones((8, E), BF16)
    bias_one = mm(ones, d_one_v[...])
    bias_two = mm(ones, d_two_v[...])
    small_v[...] = jnp.zeros_like(small_v)
    for q in range(j1):
        small_v[q:q + 1, :] = bias_one[0:1, q * 128:(q + 1) * 128]
    for q in range(j2):
        small_v[j1 + q:j1 + q + 1, :] = bias_two[0:1, q * 128:(q + 1) * 128]
        small_v[j1 + j2 + q:j1 + j2 + q + 1, :] = grad_head[0:1, q * 128:(q + 1) * 128]
    for k in range(1, R):
        send(small_v, small_rep.at[rep], 6, small_sem.at[0], (blk, lax.rem(rep + k, R)))
    small_rep[rep] = small_v[...]

    def hand_out(own, got, final, full, out_h, piece, sem_at):
        own.wait()
        wait_for(got.at[pl.ds(0, NC - 1)], rs_sem.at[piece])
        final[...] = lax.fori_loop(
            1, NC, lambda q, a: a + got[q].astype(F32), got[0].astype(F32)
        ).astype(BF16)
        for m in range(1, NC):
            b_to, x_to = chip_at(m)
            send(final, full.at[chip], sem_at, ag_sem.at[piece, m // 4], (b_to, x_to * 2 + core))
        send(final, out_h.at[core, chip], 8 + 5 * piece, fw_sem.at[piece], (blk, rep_other))
        copy = pltpu.make_async_copy(final, full.at[chip], own_sem.at[3 + piece])
        copy.start()
        return copy

    own_final_a = hand_out(own_a, got_a, final_a, full_a, grad_a_o, 0, 7)
    own_final_b = hand_out(own_b, got_b, final_b, full_b, grad_b_o, 1, 12)

    wait_for(small_rep.at[pl.ds(0, R - 1)], small_sem.at[0])
    acc = small_rep[0]
    for r in range(1, R):
        acc = acc + small_rep[r]
    small_sum[...] = acc
    for k in range(1, B):
        send(small_sum, small_blk.at[blk], 9, small_sem.at[1], (lax.rem(blk + k, B), rep))
    small_blk[blk] = acc

    for p in range(NP):
        names_v[p:p + 1, :] = (merged(got_index, p) >= half_table).astype(F32)
    upper = names_v[...].T
    for p in range(NP):
        values = got_values[2 * p:2 * p + 2].reshape(2 * CAP, W)
        above = values * jnp.broadcast_to(upper[:, p:p + 1], (2 * CAP, W)).astype(BF16)
        value_two[p * 128:(p + 1) * 128, 0:W] = values - above
        value_two[p * 128:(p + 1) * 128, W:2 * W] = above

    wait_for(res_got.at[pl.ds(0, ND - 1)], res_sem)
    total[...] = jnp.zeros_like(total)

    @pl.loop(0, NP // 8)
    def _(g):
        for h in range(8):
            p = g * 8 + h
            name = merged(got_index, p)
            low = jnp.where(name < 0, -1, lax.bitwise_and(name, half_table - 1))
            hit = lax.broadcasted_iota(jnp.int32, (half_table, 128), 0) == low
            block_hot[:, h * 128:(h + 1) * 128] = jnp.where(hit, merged(res_got, p), 0.0).astype(BF16)
        total[...] += mm(block_hot[...], value_two[pl.ds(pl.multiple_of(g * 1024, 1024), 1024), :])

    for h in range(2):
        span = slice(h * half_table, (h + 1) * half_table)
        grad = total[:, h * W:(h + 1) * W]
        n_old = n_v[span, :]
        n_new = n_old + grad * grad
        n_out_v[span, :] = n_new
        z_out_v[span, :] = z_v[span, :] + grad - (jnp.sqrt(n_new) - jnp.sqrt(n_old)) / 0.5 * weight_v[span, :]
    out_z = pltpu.make_async_copy(z_out_v, z_o, out_sem.at[0])
    out_z.start()
    out_n = pltpu.make_async_copy(n_out_v, n_o, out_sem.at[1])
    out_n.start()

    wait_for(small_blk.at[pl.ds(0, B - 1)], small_sem.at[1])
    acc = small_blk[0]
    for r in range(1, B):
        acc = acc + small_blk[r]
    small_all[...] = acc
    out_small = pltpu.make_async_copy(small_all, small_o, out_sem.at[5])
    out_small.start()

    def pass_all(own, got, full, out_h, piece):
        own.wait()

        def pass_on(m):
            b_from, x_from = chip_from(m)
            q = b_from * X + x_from
            send(full.at[q], out_h.at[core, q], 8 + 5 * piece, fw_sem.at[piece], (blk, rep_other))

        wait_for(got.at[pl.ds(0, 3)], ag_sem.at[piece, 0])
        for m in range(1, 4):
            pass_on(m)

        @pl.loop(1, NC // 4)
        def _(g):
            wait_for(got.at[pl.ds(0, 4)], ag_sem.at[piece, g])
            for i in range(4):
                pass_on(4 * g + i)

        copy = pltpu.make_async_copy(full, out_h.at[core], out_sem.at[2 + piece])
        copy.start()
        return copy

    out_a = pass_all(own_final_a, got_a, full_a, grad_a_o, 0)
    out_b = pass_all(own_final_b, got_b, full_b, grad_b_o, 1)
    wait_for(got_a, fw_sem.at[0])
    wait_for(got_b, fw_sem.at[1])

    wait_for(got_index.at[pl.ds(0, ND - 1)], send_sem.at[0])
    wait_for(got_values.at[pl.ds(0, ND - 1)], send_sem.at[1])
    wait_for(logit_got.at[pl.ds(0, ND - 1)], send_sem.at[2])
    wait_for(part_a, send_sem.at[3])
    wait_for(got_a.at[pl.ds(0, NC - 1)], send_sem.at[4])
    wait_for(res_got.at[pl.ds(0, ND - 1)], send_sem.at[5])
    wait_for(small_rep.at[pl.ds(0, R - 1)], send_sem.at[6])
    wait_for(got_a.at[pl.ds(0, NC - 1)], send_sem.at[7])
    wait_for(got_a, send_sem.at[8])
    wait_for(part_b, send_sem.at[10])
    wait_for(got_b.at[pl.ds(0, NC - 1)], send_sem.at[11])
    wait_for(got_b.at[pl.ds(0, NC - 1)], send_sem.at[12])
    wait_for(got_b, send_sem.at[13])
    wait_for(small_blk.at[pl.ds(0, B - 1)], send_sem.at[9])
    for copy in (out_z, out_n, out_a, out_b, out_prob, out_small):
        copy.wait()


def finish_kernel(
    c1, c2, grad_a_h, grad_b_h, small_h, prob_h, z_h, n_h, prob_o, z_o, n_o, g_one_o, b_one_o, g_two_o, b_two_o, head_o,
    grad_a_v, grad_b_v, z_v, n_v, one_v, two_v, small_v, prob_v, b_one_v, b_two_v, head_v, in_sem, out_sem,
):
    NC = grad_a_v.shape[1]
    DIN, H1 = one_v.shape
    H2 = two_v.shape[1]
    j1, j2 = H1 // 128, H2 // 128
    ca = c1 // 2
    quarter = DIN // 4
    ins = []
    for h in range(2):
        ins.append(pltpu.make_async_copy(grad_a_h.at[h], grad_a_v.at[h], in_sem.at[2 * h]))
        ins.append(pltpu.make_async_copy(grad_b_h.at[h], grad_b_v.at[h], in_sem.at[2 * h + 1]))
    in_z = pltpu.make_async_copy(z_h, z_v, in_sem.at[4])
    in_n = pltpu.make_async_copy(n_h, n_v, in_sem.at[5])
    in_prob = pltpu.make_async_copy(prob_h, prob_v, in_sem.at[6])
    in_small = pltpu.make_async_copy(small_h, small_v, in_sem.at[7])
    for copy in (*ins, in_z, in_n, in_prob, in_small):
        copy.start()
    outs = []

    def out(src, dst):
        outs.append(pltpu.make_async_copy(src, dst, out_sem.at[len(outs)]))
        outs[-1].start()

    for h in range(2):
        for piece, ref in ((0, grad_a_v), (1, grad_b_v)):
            ins[2 * h + piece].wait()
            top = h * (DIN // 2) + piece * quarter
            for q in range(NC):
                r1 = top + q // j1 * ca
                one_v[r1:r1 + ca, q % j1 * 128:(q % j1 + 1) * 128] = ref[h, q, 0:ca, :].astype(F32)
                if piece == 1:
                    r2 = h * (H1 // 2) + q // j2 * c2
                    two_v[r2:r2 + c2, q % j2 * 128:(q % j2 + 1) * 128] = ref[h, q, ca:ca + c2, :].astype(F32)
            out(one_v.at[pl.ds(top, quarter)], g_one_o.at[pl.ds(top, quarter)])
            if piece == 1:
                out(two_v.at[pl.ds(h * (H1 // 2), H1 // 2)], g_two_o.at[pl.ds(h * (H1 // 2), H1 // 2)])
        if h == 0:
            in_z.wait()
            out(z_v, z_o)
            in_n.wait()
            out(n_v, n_o)
        if h == 0:
            in_prob.wait()
            out(prob_v, prob_o)
            in_small.wait()
            for q in range(j1):
                b_one_v[:, q * 128:(q + 1) * 128] = small_v[q:q + 1, :]
            for q in range(j2):
                b_two_v[:, q * 128:(q + 1) * 128] = small_v[j1 + q:j1 + q + 1, :]
                head_v[:, q * 128:(q + 1) * 128] = small_v[j1 + j2 + q:j1 + j2 + q + 1, :]
            out(b_one_v, b_one_o)
            out(b_two_v, b_two_o)
            out(head_v, head_o)
    for copy in outs:
        copy.wait()


def solution(mesh):
    B, R = mesh.shape["blk"], mesh.shape["rep"]
    ND = B * R
    NC = ND // 2

    def per_device(
        dense, labels, tile_values, tile_block, tile_example, tile_count, z_state, n_state,
        w_one, b_one, w_two, b_two, head,
    ):
        E, DIN = dense.shape
        _, CAP, W = tile_values.shape
        BD = z_state.shape[0]
        H1, H2 = w_two.shape
        NH = E // 128
        NP = ND // 2
        c1 = DIN * H1 // (128 * ND)
        c2 = H1 * H2 // (128 * ND)
        hbm = pl.BlockSpec(memory_space=pl.ANY)
        I32 = jnp.int32

        def V(shape, kind=F32):
            return pltpu.VMEM(shape, kind)

        def slabs(high):
            each = V((NC, high, 128), BF16)
            return each, each, each, each, V((high, 128), BF16), each

        dma = pltpu.SemaphoreType.DMA
        scratch = [
            V((E, DIN), BF16), V((NH, 128), I32), V((CAP, ND), I32), V((CAP, ND), I32), V((1, ND), I32),
            V((BD, W)), V((BD, W)), V((DIN, H1), BF16), V((1, H1)), V((H1, H2), BF16), V((1, H2)), V((H2 // 128, 128), BF16),
            V((ND, 128), I32), V((ND, 1, 128), I32), V((NP, 1, 128), I32),
            V((ND, CAP, W), BF16), V((ND, 1, 128), I32), V((BD, W)), V((BD, 2 * W), BF16),
            V((E, H2), BF16), V((DIN, E), BF16), V((H1, E), BF16), V((E, H1)), V((E, H2)),
            V((NH, 128)), V((128, ND * CAP), BF16), V((ND * CAP, 128), BF16),
            V((2, NP, 1, 128)), V((ND, 1, 128)), V((2 * NH, ND * CAP), BF16), V((2 * NH, ND * CAP)),
            V((2, NP, 1, 128)), V((ND, 1, 128)),
            V((NP, 128)), V((ND * CAP, 2 * W), BF16), V((BD // 2, 1024), BF16), V((BD // 2, 2 * W)), V((BD, W)), V((BD, W)),
            V((E, H1), BF16), V((E, H2), BF16), V((DIN // 4, H1)), V((H1 // 2, H2)),
            *slabs(c1 // 2), *slabs(c1 // 2 + c2),
            V((8, 128)), V((R, 8, 128)), V((8, 128)), V((B, 8, 128)), V((8, 128)), V((NH, 128)),
            dma((12,)), dma((5,)), pltpu.SemaphoreType.REGULAR, dma((NC // 2,)), dma((NC // 2,)), dma(()), dma(()),
            dma((2,)), dma((2,)), dma((2, NC // 4)), dma((2,)), dma((2,)),
            dma((14,)), dma((6,)),
        ]
        shape = jax.ShapeDtypeStruct
        prob, z_new, n_new, grad_a, grad_b, small = pl.pallas_call(
            functools.partial(step_kernel, B, R),
            out_shape=(
                shape((NH, 128), F32), shape((BD, W), F32), shape((BD, W), F32),
                shape((2, NC, c1 // 2, 128), BF16), shape((2, NC, c1 // 2 + c2, 128), BF16), shape((8, 128), F32),
            ),
            in_specs=[hbm] * 13,
            out_specs=(hbm,) * 6,
            scratch_shapes=scratch,
            compiler_params=pltpu.CompilerParams(
                collective_id=0, has_side_effects=True, vmem_limit_bytes=60 * 1024 * 1024
            ),
        )(
            dense, labels.reshape(NH, 128), tile_values, tile_block.T, tile_example.T, tile_count.reshape(1, ND),
            z_state, n_state, w_one, b_one.reshape(1, H1), w_two, b_two.reshape(1, H2), head.reshape(H2 // 128, 128),
        )
        prob, z_new, n_new, g_one, g_b_one, g_two, g_b_two, g_head = pl.pallas_call(
            functools.partial(finish_kernel, c1, c2),
            out_shape=(
                shape((NH, 128), F32), shape((BD, W), F32), shape((BD, W), F32), shape((DIN, H1), F32),
                shape((1, H1), F32), shape((H1, H2), F32), shape((1, H2), F32), shape((1, H2), F32),
            ),
            in_specs=[hbm] * 6,
            out_specs=(hbm,) * 8,
            scratch_shapes=[
                V((2, NC, c1 // 2, 128), BF16), V((2, NC, c1 // 2 + c2, 128), BF16), V((BD, W)), V((BD, W)),
                V((DIN, H1)), V((H1, H2)), V((8, 128)), V((NH, 128)), V((1, H1)), V((1, H2)), V((1, H2)),
                dma((8,)), dma((12,)),
            ],
            compiler_params=pltpu.CompilerParams(vmem_limit_bytes=63 * 1024 * 1024),
        )(grad_a, grad_b, small, prob, z_new, n_new)
        return (
            prob.reshape(E), z_new, n_new, g_one, g_b_one.reshape(H1), g_two, g_b_two.reshape(H2), g_head.reshape(H2),
        )

    every = ("blk", "rep")
    return jax.shard_map(
        per_device,
        mesh=mesh,
        in_specs=(
            P(every, None), P(every), P(every, None, None), P(every, None), P(every, None), P(every),
            P(every, None), P(every, None), P(), P(), P(), P(), P(),
        ),
        out_specs=(P(every), P(every, None), P(every, None), P(), P(), P(), P(), P()),
        check_vma=False,
    )
```

```python
import functools

import jax
import jax.numpy as jnp
from jax import lax
from jax.experimental import pallas as pl
from jax.experimental.pallas import tpu as pltpu
from jax.sharding import PartitionSpec as P

MESH = pl.DeviceIdType.MESH
F32 = jnp.float32
BF16 = jnp.bfloat16
NT = (((1,), (1,)), ((), ()))
STRIDE = 37


def mm(a, b):
    return jnp.dot(a, b, preferred_element_type=F32)


def mm_nt(a, b):
    return lax.dot_general(a, b, NT, preferred_element_type=F32)


def step_kernel(
    B, R,
    dense_h, labels_h, values_h, block_h, example_h, count_h, z_h, n_h,
    w_one_h, b_one_h, w_two_h, b_two_h, head_h,
    prob_o, z_o, n_o, grad_a_o, grad_b_o, small_o,
    dense_v, labels_v, block_v, example_t, count_v, z_v, n_v, w_one_v, b_one_v, w_two_v, b_two_v, head_v,
    table_v, index_send, example_v,
    got_values, got_index, weight_v, weight_pair,
    hid_two_v, dense_t, hid_one_t, scale_one, scale_two, deep_v, low_hot, slot_hot,
    logit_send, logit_got, spread, picked, res_send, res_got,
    names_v, value_two, block_hot, total, z_out_v, n_out_v,
    d_one_v, d_two_v, own_one, own_two,
    part_a, pair_a, sum_a, got_a, final_a, full_a, part_b, pair_b, sum_b, got_b, final_b, full_b,
    small_v, small_rep, small_sum, small_blk, small_all, prob_v,
    load_sem, own_sem, ready_sem, index_sem, value_sem, logit_sem, res_sem,
    pair_sem, rs_sem, ag_sem, fw_sem, small_sem,
    send_sem, out_sem,
):
    ND = B * R
    NC = ND // 2
    X = R // 2
    Z = 4 if B % 4 == 0 else B
    Y = B // Z
    E, DIN = dense_v.shape
    H1 = w_one_v.shape[1]
    H2 = w_two_v.shape[1]
    CAP, W = got_values.shape[1], got_values.shape[2]
    BD = z_v.shape[0]
    NH = E // 128
    NP = ND // 2
    c1 = DIN * H1 // (128 * ND)
    c2 = H1 * H2 // (128 * ND)
    j1 = H1 // 128
    j2 = H2 // 128
    blk = lax.axis_index("blk")
    rep = lax.axis_index("rep")
    y, zz = lax.div(blk, Z), lax.rem(blk, Z)
    x, core = lax.div(rep, 2), lax.rem(rep, 2)
    other = 1 - core
    me = blk * R + rep
    chip = blk * X + x
    y_at = [lax.rem(y + i, Y) * Z for i in range(Y)]
    z_at = [lax.rem(zz + i, Z) for i in range(Z)]
    x_at = [lax.rem(x + i, X) for i in range(X)]

    order = [(m * STRIDE) % NC for m in range(NC)]

    def spread_of(spot):
        return spot // (Z * X), spot // X % Z, spot % X

    def chip_at(m):
        dy, dz, dx = spread_of(order[m])
        return y_at[dy] + z_at[dz], x_at[dx]

    def chip_from(m):
        spot = lax.rem(m * STRIDE, NC)
        dy, dz, dx = lax.div(spot, Z * X), lax.rem(lax.div(spot, X), Z), lax.rem(spot, X)
        return lax.rem(y + Y - dy, Y) * Z + lax.rem(zz + Z - dz, Z), lax.rem(x + X - dx, X)

    loads = [
        (block_h, block_v), (count_h, count_v), (example_h, example_t), (z_h, z_v), (n_h, n_v), (dense_h, dense_v),
        (w_one_h, w_one_v), (b_one_h, b_one_v), (w_two_h, w_two_v), (b_two_h, b_two_v), (head_h, head_v),
        (labels_h, labels_v),
    ]
    copies = [pltpu.make_async_copy(s, d, load_sem.at[i]) for i, (s, d) in enumerate(loads)]
    for copy in copies:
        copy.start()

    def send(src, dst, sem_at, recv, where):
        pltpu.make_async_remote_copy(
            src_ref=src, dst_ref=dst, send_sem=send_sem.at[sem_at], recv_sem=recv,
            device_id=where, device_id_type=MESH,
        ).start()

    def wait_for(ref, sem):
        pltpu.make_async_copy(ref, ref, sem).wait()

    barrier = pltpu.get_barrier_semaphore()
    for k in range(1, B):
        pl.semaphore_signal(barrier, inc=1, device_id=(lax.rem(blk + k, B), rep), device_id_type=MESH)
    for k in range(1, R):
        pl.semaphore_signal(barrier, inc=1, device_id=(blk, lax.rem(rep + k, R)), device_id_type=MESH)
    own_value = pltpu.make_async_copy(values_h.at[me], got_values.at[me], own_sem.at[0])
    own_value.start()

    first_half = lax.broadcasted_iota(jnp.int32, (1, 128), 1) < CAP
    copies[0].wait()
    copies[1].wait()
    live = lax.broadcasted_iota(jnp.int32, (CAP, ND), 0) < count_v[...]
    named = jnp.where(live, block_v[...], -1).astype(F32)
    table_v[...] = jnp.concatenate([named, named], axis=0).T.astype(jnp.int32)
    for o in range(ND):
        index_send[o] = table_v[o:o + 1, :]

    pl.semaphore_wait(barrier, B + R - 2)
    for k in range(1, R):
        pl.semaphore_signal(ready_sem, inc=1, device_id=(blk, lax.rem(rep + k, R)), device_id_type=MESH)

    def give(m, c):
        blk_to, x_to = chip_at(m)
        rep_to = x_to * 2 + c
        to = blk_to * R + rep_to
        send(index_send.at[to], got_index.at[me], 0, index_sem.at[m // 2], (blk_to, rep_to))
        send(values_h.at[to], got_values.at[me], 1, value_sem.at[m // 2], (blk_to, rep_to))

    give(0, other)
    for m in range(1, NC):
        spot = order[m]
        if spot < X:
            give(m, 0)
            give(m, 1)
        elif spot % X == 0:
            give(m, core)
    copies[2].wait()
    named = example_t[...].astype(F32)
    table_v[...] = jnp.concatenate([named, named], axis=0).T.astype(jnp.int32)
    for p in range(NP):
        example_v[p] = jnp.where(first_half, table_v[2 * p:2 * p + 1, :], table_v[2 * p + 1:2 * p + 2, :])
    pl.semaphore_wait(ready_sem, R - 1)

    for m in range(1, NC):
        spot = order[m]
        if spot >= X and spot % X == 0:
            give(m, other)
        elif spot >= X:
            give(m, 0)
            give(m, 1)
    got_index[me] = index_send[me]

    copies[3].wait()
    copies[4].wait()
    z = z_v[...]
    shrunk = z - jnp.where(z > 0, 0.5, -0.5)
    weight = jnp.where(jnp.abs(z) > 0.5, -shrunk / ((1.0 + jnp.sqrt(n_v[...])) / 0.5 + 0.1), 0.0)
    weight_v[...] = weight
    high = weight.astype(BF16)
    weight_pair[:, :W] = high
    weight_pair[:, W:] = (weight - high.astype(F32)).astype(BF16)

    for copy in copies[5:]:
        copy.wait()
    rows = 256
    head_row = jnp.concatenate([head_v[q:q + 1, :] for q in range(j2)], axis=1)
    head_rows = jnp.broadcast_to(head_row, (8, H2))

    @pl.loop(0, E // rows)
    def _(i):
        at = pl.multiple_of(i * rows, rows)
        dense = dense_v[pl.ds(at, rows), :]
        pre_one = mm(dense, w_one_v[...]) + b_one_v[...]
        gate_one = jax.nn.sigmoid(pre_one)
        hid_one = (pre_one * gate_one).astype(BF16)
        pre_two = mm(hid_one, w_two_v[...]) + b_two_v[...]
        gate_two = jax.nn.sigmoid(pre_two)
        hid_two = (pre_two * gate_two).astype(BF16)
        hid_two_v[pl.ds(at, rows), :] = hid_two
        two = head_row.astype(F32) * (gate_two * (1.0 + pre_two * (1.0 - gate_two)))
        scale_two[pl.ds(at, rows), :] = two
        back = mm_nt(two.astype(BF16), w_two_v[...])
        scale_one[pl.ds(at, rows), :] = back * (gate_one * (1.0 + pre_one * (1.0 - gate_one)))
        deep = mm_nt(head_rows, hid_two)
        for q in range(rows // 128):
            deep_v[pl.ds(i * (rows // 128) + q, 1), :] = deep[0:1, q * 128:(q + 1) * 128]
        dense_t[:, pl.ds(at, rows)] = dense.T
        hid_one_t[:, pl.ds(at, rows)] = hid_one.T

    @pl.loop(0, NP)
    def _(p):
        at = pl.multiple_of(p * 128, 128)
        low = lax.bitwise_and(example_v[p], 127)
        hot = (lax.broadcasted_iota(jnp.int32, (128, 128), 0) == low).astype(F32)
        low_hot[:, pl.ds(at, 128)] = hot.astype(BF16)
        slot_hot[pl.ds(at, 128), :] = hot.T.astype(BF16)

    def merged(ref, p):
        return jnp.where(first_half, ref[2 * p], ref[2 * p + 1])

    def flipped(row):
        return pltpu.roll(jnp.broadcast_to(row, (8, 128)), CAP, axis=1)[0:1]

    def logits_of(places):
        spots = [b * X + xs for b, xs in places]
        four = jnp.concatenate([got_values[pl.ds(2 * q, 2)].reshape(2 * CAP, W) for q in spots], axis=0)
        score = mm_nt(weight_pair[...], jnp.concatenate([four, four], axis=1))
        for i, q in enumerate(spots):
            hit = lax.broadcasted_iota(jnp.int32, (BD, 128), 0) == merged(got_index, q)
            row = jnp.sum(jnp.where(hit, score[:, i * 128:(i + 1) * 128], 0.0), axis=0, keepdims=True)
            logit_send[0, q] = row
            logit_send[1, q] = flipped(row)

    own_value.wait()
    wait_for(got_index.at[pl.ds(0, 3)], index_sem.at[0])
    wait_for(got_values.at[pl.ds(0, 3)], value_sem.at[0])
    b_next, x_next = chip_from(1)
    logits_of([(blk, x), (b_next, x_next)])
    send(logit_send.at[1, chip], logit_got.at[me], 2, logit_sem, (blk, x * 2 + other))
    for c, turn in ((0, core), (1, other)):
        send(logit_send.at[turn, b_next * X + x_next], logit_got.at[me], 2, logit_sem, (b_next, x_next * 2 + c))
    logit_got[me] = logit_send[0, chip]

    @pl.loop(1, NC // 2)
    def _(u):
        wait_for(got_index.at[pl.ds(0, 4)], index_sem.at[u])
        wait_for(got_values.at[pl.ds(0, 4)], value_sem.at[u])
        places = [chip_from(2 * u), chip_from(2 * u + 1)]
        logits_of(places)
        for b_to, x_to in places:
            for c, turn in ((0, core), (1, other)):
                send(logit_send.at[turn, b_to * X + x_to], logit_got.at[me], 2, logit_sem, (b_to, x_to * 2 + c))

    half_table = BD // 2

    wait_for(logit_got.at[pl.ds(0, ND - 1)], logit_sem)
    eight = lax.broadcasted_iota(jnp.int32, (NH, 128), 0)
    for p in range(NP):
        mine = eight == lax.shift_right_logical(example_v[p], 7)
        term = jnp.where(mine, merged(logit_got, p), 0.0)
        top = term.astype(BF16).astype(F32)
        spread[:, p * 128:(p + 1) * 128] = jnp.concatenate([top, term - top], axis=0).astype(BF16)
    wide = mm(spread[...], slot_hot[...])
    prob = jax.nn.sigmoid(wide[:NH] + wide[NH:] + deep_v[...])
    prob_v[...] = prob
    out_prob = pltpu.make_async_copy(prob_v, prob_o, out_sem.at[4])
    out_prob.start()
    residual = prob - labels_v[...].astype(F32)
    dlogit = residual.astype(BF16).astype(F32)

    upright = jnp.concatenate([dlogit, jnp.zeros((128 - NH, 128), F32)], axis=0).T
    for q in range(NH):
        span = slice(q * 128, (q + 1) * 128)
        column = upright[:, q:q + 1]
        d_two_v[span, :] = (scale_two[span, :] * column).astype(BF16)
        d_one_v[span, :] = (scale_one[span, :] * column).astype(BF16)

    half_one, half_two = DIN // 2, H1 // 2
    quarter = DIN // 4
    rep_other = x * 2 + other
    ca = c1 // 2

    def cut(q, height, across):
        return slice(q // across * height, (q // across + 1) * height), slice(q % across * 128, (q % across + 1) * 128)

    def grad_one(which, piece):
        return mm(dense_t[pl.ds(pl.multiple_of(which * half_one + piece * quarter, quarter), quarter), :], d_one_v[...])

    def grad_two(which):
        return mm(hid_one_t[pl.ds(pl.multiple_of(which * half_two, half_two), half_two), :], d_two_v[...])

    one = grad_one(other, 0)
    for q in range(NC):
        part_a[q] = one[cut(q, ca, j1)].astype(BF16)
    send(part_a, pair_a, 3, pair_sem.at[0], (blk, rep_other))
    one = grad_one(other, 1)
    two = grad_two(other)
    for q in range(NC):
        part_b[q, 0:ca, :] = one[cut(q, ca, j1)].astype(BF16)
        part_b[q, ca:ca + c2, :] = two[cut(q, c2, j2)].astype(BF16)
    send(part_b, pair_b, 10, pair_sem.at[1], (blk, rep_other))

    own_one[...] = grad_one(core, 0)
    wait_for(pair_a, pair_sem.at[0])
    for q in range(NC):
        sum_a[q] = (own_one[cut(q, ca, j1)] + pair_a[q].astype(F32)).astype(BF16)
    for m in range(1, NC):
        b_to, x_to = chip_at(m)
        send(sum_a.at[b_to * X + x_to], got_a.at[chip], 4, rs_sem.at[0], (b_to, x_to * 2 + core))
    own_a = pltpu.make_async_copy(sum_a.at[chip], got_a.at[chip], own_sem.at[1])
    own_a.start()

    own_one[...] = grad_one(core, 1)
    own_two[...] = grad_two(core)
    wait_for(pair_b, pair_sem.at[1])
    for q in range(NC):
        sum_b[q, 0:ca, :] = (own_one[cut(q, ca, j1)] + pair_b[q, 0:ca, :].astype(F32)).astype(BF16)
        sum_b[q, ca:ca + c2, :] = (own_two[cut(q, c2, j2)] + pair_b[q, ca:ca + c2, :].astype(F32)).astype(BF16)
    for m in range(1, NC):
        b_to, x_to = chip_at(m)
        send(sum_b.at[b_to * X + x_to], got_b.at[chip], 11, rs_sem.at[1], (b_to, x_to * 2 + core))
    own_b = pltpu.make_async_copy(sum_b.at[chip], got_b.at[chip], own_sem.at[2])
    own_b.start()

    table = jnp.concatenate([dlogit, jnp.zeros_like(dlogit)], axis=0).astype(BF16)
    picked[...] = mm(table, low_hot[...])
    for p in range(NP):
        mine = eight == lax.shift_right_logical(example_v[p], 7)
        row = jnp.sum(jnp.where(mine, picked[0:NH, p * 128:(p + 1) * 128], 0.0), axis=0, keepdims=True)
        res_send[0, p] = row
        res_send[1, p] = flipped(row)
    for m in range(NC):
        b_to, x_to = chip_at(m)
        q = b_to * X + x_to
        if m == 0:
            send(res_send.at[1, q], res_got.at[me], 5, res_sem, (b_to, x_to * 2 + other))
        else:
            for c, turn in ((0, core), (1, other)):
                send(res_send.at[turn, q], res_got.at[me], 5, res_sem, (b_to, x_to * 2 + c))
    res_got[me] = res_send[0, chip]

    grad_head = jnp.zeros((8, H2), F32)
    for q in range(NH):
        grad_head += mm(jnp.broadcast_to(dlogit[q:q + 1, :], (8, 128)).astype(BF16), hid_two_v[q * 128:(q + 1) * 128, :])
    ones = jnp.ones((8, E), BF16)
    bias_one = mm(ones, d_one_v[...])
    bias_two = mm(ones, d_two_v[...])
    small_v[...] = jnp.zeros_like(small_v)
    for q in range(j1):
        small_v[q:q + 1, :] = bias_one[0:1, q * 128:(q + 1) * 128]
    for q in range(j2):
        small_v[j1 + q:j1 + q + 1, :] = bias_two[0:1, q * 128:(q + 1) * 128]
        small_v[j1 + j2 + q:j1 + j2 + q + 1, :] = grad_head[0:1, q * 128:(q + 1) * 128]
    for k in range(1, R):
        send(small_v, small_rep.at[rep], 6, small_sem.at[0], (blk, lax.rem(rep + k, R)))
    small_rep[rep] = small_v[...]

    def hand_out(own, got, final, full, out_h, piece, sem_at):
        own.wait()
        wait_for(got.at[pl.ds(0, NC - 1)], rs_sem.at[piece])
        final[...] = lax.fori_loop(
            1, NC, lambda q, a: a + got[q].astype(F32), got[0].astype(F32)
        ).astype(BF16)
        for m in range(1, NC):
            b_to, x_to = chip_at(m)
            send(final, full.at[chip], sem_at, ag_sem.at[piece, m // 4], (b_to, x_to * 2 + core))
        send(final, out_h.at[core, chip], 8 + 5 * piece, fw_sem.at[piece], (blk, rep_other))
        copy = pltpu.make_async_copy(final, full.at[chip], own_sem.at[3 + piece])
        copy.start()
        return copy

    own_final_a = hand_out(own_a, got_a, final_a, full_a, grad_a_o, 0, 7)
    own_final_b = hand_out(own_b, got_b, final_b, full_b, grad_b_o, 1, 12)

    wait_for(small_rep.at[pl.ds(0, R - 1)], small_sem.at[0])
    acc = small_rep[0]
    for r in range(1, R):
        acc = acc + small_rep[r]
    small_sum[...] = acc
    for k in range(1, B):
        send(small_sum, small_blk.at[blk], 9, small_sem.at[1], (lax.rem(blk + k, B), rep))
    small_blk[blk] = acc

    for p in range(NP):
        names_v[p:p + 1, :] = (merged(got_index, p) >= half_table).astype(F32)
    upper = names_v[...].T
    for p in range(NP):
        values = got_values[2 * p:2 * p + 2].reshape(2 * CAP, W)
        above = values * jnp.broadcast_to(upper[:, p:p + 1], (2 * CAP, W)).astype(BF16)
        value_two[p * 128:(p + 1) * 128, 0:W] = values - above
        value_two[p * 128:(p + 1) * 128, W:2 * W] = above

    wait_for(res_got.at[pl.ds(0, ND - 1)], res_sem)
    total[...] = jnp.zeros_like(total)

    @pl.loop(0, NP // 8)
    def _(g):
        for h in range(8):
            p = g * 8 + h
            name = merged(got_index, p)
            low = jnp.where(name < 0, -1, lax.bitwise_and(name, half_table - 1))
            hit = lax.broadcasted_iota(jnp.int32, (half_table, 128), 0) == low
            block_hot[:, h * 128:(h + 1) * 128] = jnp.where(hit, merged(res_got, p), 0.0).astype(BF16)
        total[...] += mm(block_hot[...], value_two[pl.ds(pl.multiple_of(g * 1024, 1024), 1024), :])

    for h in range(2):
        span = slice(h * half_table, (h + 1) * half_table)
        grad = total[:, h * W:(h + 1) * W]
        n_old = n_v[span, :]
        n_new = n_old + grad * grad
        n_out_v[span, :] = n_new
        z_out_v[span, :] = z_v[span, :] + grad - (jnp.sqrt(n_new) - jnp.sqrt(n_old)) / 0.5 * weight_v[span, :]
    out_z = pltpu.make_async_copy(z_out_v, z_o, out_sem.at[0])
    out_z.start()
    out_n = pltpu.make_async_copy(n_out_v, n_o, out_sem.at[1])
    out_n.start()

    wait_for(small_blk.at[pl.ds(0, B - 1)], small_sem.at[1])
    acc = small_blk[0]
    for r in range(1, B):
        acc = acc + small_blk[r]
    small_all[...] = acc
    out_small = pltpu.make_async_copy(small_all, small_o, out_sem.at[5])
    out_small.start()

    def pass_all(own, got, full, out_h, piece):
        own.wait()

        def pass_on(m):
            b_from, x_from = chip_from(m)
            q = b_from * X + x_from
            send(full.at[q], out_h.at[core, q], 8 + 5 * piece, fw_sem.at[piece], (blk, rep_other))

        wait_for(got.at[pl.ds(0, 3)], ag_sem.at[piece, 0])
        for m in range(1, 4):
            pass_on(m)

        @pl.loop(1, NC // 4)
        def _(g):
            wait_for(got.at[pl.ds(0, 4)], ag_sem.at[piece, g])
            for i in range(4):
                pass_on(4 * g + i)

        copy = pltpu.make_async_copy(full, out_h.at[core], out_sem.at[2 + piece])
        copy.start()
        return copy

    out_a = pass_all(own_final_a, got_a, full_a, grad_a_o, 0)
    out_b = pass_all(own_final_b, got_b, full_b, grad_b_o, 1)
    wait_for(got_a, fw_sem.at[0])
    wait_for(got_b, fw_sem.at[1])

    wait_for(got_index.at[pl.ds(0, ND - 1)], send_sem.at[0])
    wait_for(got_values.at[pl.ds(0, ND - 1)], send_sem.at[1])
    wait_for(logit_got.at[pl.ds(0, ND - 1)], send_sem.at[2])
    wait_for(part_a, send_sem.at[3])
    wait_for(got_a.at[pl.ds(0, NC - 1)], send_sem.at[4])
    wait_for(res_got.at[pl.ds(0, ND - 1)], send_sem.at[5])
    wait_for(small_rep.at[pl.ds(0, R - 1)], send_sem.at[6])
    wait_for(got_a.at[pl.ds(0, NC - 1)], send_sem.at[7])
    wait_for(got_a, send_sem.at[8])
    wait_for(part_b, send_sem.at[10])
    wait_for(got_b.at[pl.ds(0, NC - 1)], send_sem.at[11])
    wait_for(got_b.at[pl.ds(0, NC - 1)], send_sem.at[12])
    wait_for(got_b, send_sem.at[13])
    wait_for(small_blk.at[pl.ds(0, B - 1)], send_sem.at[9])
    for copy in (out_z, out_n, out_a, out_b, out_prob, out_small):
        copy.wait()


def finish_kernel(
    c1, c2, grad_a_h, grad_b_h, small_h, prob_h, z_h, n_h, prob_o, z_o, n_o, g_one_o, b_one_o, g_two_o, b_two_o, head_o,
    grad_a_v, grad_b_v, z_v, n_v, one_v, two_v, small_v, prob_v, b_one_v, b_two_v, head_v, in_sem, out_sem,
):
    NC = grad_a_v.shape[1]
    DIN, H1 = one_v.shape
    H2 = two_v.shape[1]
    j1, j2 = H1 // 128, H2 // 128
    ca = c1 // 2
    quarter = DIN // 4
    ins = []
    for h in range(2):
        ins.append(pltpu.make_async_copy(grad_a_h.at[h], grad_a_v.at[h], in_sem.at[2 * h]))
        ins.append(pltpu.make_async_copy(grad_b_h.at[h], grad_b_v.at[h], in_sem.at[2 * h + 1]))
    in_z = pltpu.make_async_copy(z_h, z_v, in_sem.at[4])
    in_n = pltpu.make_async_copy(n_h, n_v, in_sem.at[5])
    in_prob = pltpu.make_async_copy(prob_h, prob_v, in_sem.at[6])
    in_small = pltpu.make_async_copy(small_h, small_v, in_sem.at[7])
    for copy in (*ins, in_z, in_n, in_prob, in_small):
        copy.start()
    outs = []

    def out(src, dst):
        outs.append(pltpu.make_async_copy(src, dst, out_sem.at[len(outs)]))
        outs[-1].start()

    for h in range(2):
        for piece, ref in ((0, grad_a_v), (1, grad_b_v)):
            ins[2 * h + piece].wait()
            top = h * (DIN // 2) + piece * quarter
            for q in range(NC):
                r1 = top + q // j1 * ca
                one_v[r1:r1 + ca, q % j1 * 128:(q % j1 + 1) * 128] = ref[h, q, 0:ca, :].astype(F32)
                if piece == 1:
                    r2 = h * (H1 // 2) + q // j2 * c2
                    two_v[r2:r2 + c2, q % j2 * 128:(q % j2 + 1) * 128] = ref[h, q, ca:ca + c2, :].astype(F32)
            out(one_v.at[pl.ds(top, quarter)], g_one_o.at[pl.ds(top, quarter)])
            if piece == 1:
                out(two_v.at[pl.ds(h * (H1 // 2), H1 // 2)], g_two_o.at[pl.ds(h * (H1 // 2), H1 // 2)])
        if h == 0:
            in_z.wait()
            out(z_v, z_o)
            in_n.wait()
            out(n_v, n_o)
        if h == 0:
            in_prob.wait()
            out(prob_v, prob_o)
            in_small.wait()
            for q in range(j1):
                b_one_v[:, q * 128:(q + 1) * 128] = small_v[q:q + 1, :]
            for q in range(j2):
                b_two_v[:, q * 128:(q + 1) * 128] = small_v[j1 + q:j1 + q + 1, :]
                head_v[:, q * 128:(q + 1) * 128] = small_v[j1 + j2 + q:j1 + j2 + q + 1, :]
            out(b_one_v, b_one_o)
            out(b_two_v, b_two_o)
            out(head_v, head_o)
    for copy in outs:
        copy.wait()


def solution(mesh):
    B, R = mesh.shape["blk"], mesh.shape["rep"]
    ND = B * R
    NC = ND // 2

    def per_device(
        dense, labels, tile_values, tile_block, tile_example, tile_count, z_state, n_state,
        w_one, b_one, w_two, b_two, head,
    ):
        E, DIN = dense.shape
        _, CAP, W = tile_values.shape
        BD = z_state.shape[0]
        H1, H2 = w_two.shape
        NH = E // 128
        NP = ND // 2
        c1 = DIN * H1 // (128 * ND)
        c2 = H1 * H2 // (128 * ND)
        hbm = pl.BlockSpec(memory_space=pl.ANY)
        I32 = jnp.int32

        def V(shape, kind=F32):
            return pltpu.VMEM(shape, kind)

        def slabs(high):
            each = V((NC, high, 128), BF16)
            return each, each, each, each, V((high, 128), BF16), each

        dma = pltpu.SemaphoreType.DMA
        scratch = [
            V((E, DIN), BF16), V((NH, 128), I32), V((CAP, ND), I32), V((CAP, ND), I32), V((1, ND), I32),
            V((BD, W)), V((BD, W)), V((DIN, H1), BF16), V((1, H1)), V((H1, H2), BF16), V((1, H2)), V((H2 // 128, 128), BF16),
            V((ND, 128), I32), V((ND, 1, 128), I32), V((NP, 1, 128), I32),
            V((ND, CAP, W), BF16), V((ND, 1, 128), I32), V((BD, W)), V((BD, 2 * W), BF16),
            V((E, H2), BF16), V((DIN, E), BF16), V((H1, E), BF16), V((E, H1)), V((E, H2)),
            V((NH, 128)), V((128, ND * CAP), BF16), V((ND * CAP, 128), BF16),
            V((2, NP, 1, 128)), V((ND, 1, 128)), V((2 * NH, ND * CAP), BF16), V((2 * NH, ND * CAP)),
            V((2, NP, 1, 128)), V((ND, 1, 128)),
            V((NP, 128)), V((ND * CAP, 2 * W), BF16), V((BD // 2, 1024), BF16), V((BD // 2, 2 * W)), V((BD, W)), V((BD, W)),
            V((E, H1), BF16), V((E, H2), BF16), V((DIN // 4, H1)), V((H1 // 2, H2)),
            *slabs(c1 // 2), *slabs(c1 // 2 + c2),
            V((8, 128)), V((R, 8, 128)), V((8, 128)), V((B, 8, 128)), V((8, 128)), V((NH, 128)),
            dma((12,)), dma((5,)), pltpu.SemaphoreType.REGULAR, dma((NC // 2,)), dma((NC // 2,)), dma(()), dma(()),
            dma((2,)), dma((2,)), dma((2, NC // 4)), dma((2,)), dma((2,)),
            dma((14,)), dma((6,)),
        ]
        shape = jax.ShapeDtypeStruct
        prob, z_new, n_new, grad_a, grad_b, small = pl.pallas_call(
            functools.partial(step_kernel, B, R),
            out_shape=(
                shape((NH, 128), F32), shape((BD, W), F32), shape((BD, W), F32),
                shape((2, NC, c1 // 2, 128), BF16), shape((2, NC, c1 // 2 + c2, 128), BF16), shape((8, 128), F32),
            ),
            in_specs=[hbm] * 13,
            out_specs=(hbm,) * 6,
            scratch_shapes=scratch,
            compiler_params=pltpu.CompilerParams(
                collective_id=0, has_side_effects=True, vmem_limit_bytes=60 * 1024 * 1024
            ),
        )(
            dense, labels.reshape(NH, 128), tile_values, tile_block.T, tile_example.T, tile_count.reshape(1, ND),
            z_state, n_state, w_one, b_one.reshape(1, H1), w_two, b_two.reshape(1, H2), head.reshape(H2 // 128, 128),
        )
        prob, z_new, n_new, g_one, g_b_one, g_two, g_b_two, g_head = pl.pallas_call(
            functools.partial(finish_kernel, c1, c2),
            out_shape=(
                shape((NH, 128), F32), shape((BD, W), F32), shape((BD, W), F32), shape((DIN, H1), F32),
                shape((1, H1), F32), shape((H1, H2), F32), shape((1, H2), F32), shape((1, H2), F32),
            ),
            in_specs=[hbm] * 6,
            out_specs=(hbm,) * 8,
            scratch_shapes=[
                V((2, NC, c1 // 2, 128), BF16), V((2, NC, c1 // 2 + c2, 128), BF16), V((BD, W)), V((BD, W)),
                V((DIN, H1)), V((H1, H2)), V((8, 128)), V((NH, 128)), V((1, H1)), V((1, H2)), V((1, H2)),
                dma((8,)), dma((12,)),
            ],
            compiler_params=pltpu.CompilerParams(vmem_limit_bytes=63 * 1024 * 1024),
        )(grad_a, grad_b, small, prob, z_new, n_new)
        return (
            prob.reshape(E), z_new, n_new, g_one, g_b_one.reshape(H1), g_two, g_b_two.reshape(H2), g_head.reshape(H2),
        )

    every = ("blk", "rep")
    return jax.shard_map(
        per_device,
        mesh=mesh,
        in_specs=(
            P(every, None), P(every), P(every, None, None), P(every, None), P(every, None), P(every),
            P(every, None), P(every, None), P(), P(), P(), P(), P(),
        ),
        out_specs=(P(every), P(every, None), P(every, None), P(), P(), P(), P(), P()),
        check_vma=False,
    )
```
